32 devices in a mesh: lat: 4 (over y, core), lon: 8 (over z, x).
Axes of the slice: x: 2, y: 2, z: 4, core: 2. Of those that a mesh axis runs over, the one named last changes fastest.
Arguments:
- tokens: bfloat16 [32, 128, 1024], P('lat', 'lon'), may hold values from -36 to 36
- shifts: int32 [2], replicated, may hold values from 1 to 7, as said below
- w_qkv: bfloat16 [1024, 3072], replicated, may hold values from -0.1875 to 0.1875
- w_out: bfloat16 [1024, 1024], replicated, may hold values from -0.1875 to 0.1875
- router: bfloat16 [1024, 64], replicated, may hold values from -0.1875 to 0.1875
- expert_ids: int32 [4, 8, 128, 2], P('lat', 'lon'), may hold values from 0 to 63, all different within a row; in each aligned block of 128 rows (0 to 127, 128 to 255, ..., all dimensions but the last counted through in order) at most 6 rows name the same one
- w_gate: bfloat16 [1024, 65536], P(None, ('lat', 'lon')), may hold values from -0.1875 to 0.1875
- w_up: bfloat16 [1024, 65536], P(None, ('lat', 'lon')), may hold values from -0.1875 to 0.1875
- w_down: bfloat16 [65536, 1024], P(('lat', 'lon')), may hold values from -0.1875 to 0.1875
Outputs:
- layer_out: bfloat16 [32, 128, 1024], P('lat', 'lon')
The draws below stay inside these ranges and needn't reach their ends.
Inputs may be any that keep to these rules, and one draw needn't show every extreme that they name: `expert_ids`: each token names two different experts; no expert is named by more than 6 of one device's tokens, a bound that some block reaches. The two shifts differ, and one of them is 7.
All inputs are finite; a program needn't handle non-finite values.
Results may differ from the reference program's by a relative error of at most 0.0095.
Values may be sent and summed in bfloat16 or wider, within the bound.
A program may use at most 64 MiB of HBM per device.

```python
import math
import jax
import jax.numpy as jnp
import numpy as np
from jax import lax

D = 1024
HEAD = 64
HEADS = 16
FF = 1024
EXPERTS = 64
TOP = 2
WIN = 8
CLAT = 8
CLON = 16
LAT = 32
LON = 128
TOK_DEV = 128
TOKENS = 4096
MOST = 6
PIECE = 1024
REPL = 1
N_LAT = 4
N_LON = 8


def draw_tokens(key, part):
    key_base, key_rows, key_cols = jax.random.split(key, 3)
    base = jnp.clip(jax.random.normal(key_base, (LAT, LON, D), jnp.float32), -4.0, 4.0)
    rows = jnp.exp(jax.random.uniform(key_rows, (LAT, LON, 1), jnp.float32, math.log(0.3), math.log(3.0)))
    cols = jnp.exp(jax.random.uniform(key_cols, (D,), jnp.float32, math.log(0.3), math.log(3.0)))
    return (base * rows * cols).astype(jnp.bfloat16)


def draw_shifts(key, part):
    key_order, key_other = jax.random.split(jax.random.fold_in(key, 71), 2)
    order = jax.random.randint(key_order, (), 0, 2, dtype=jnp.int32)
    other = jax.random.randint(key_other, (), 1, WIN - 1, dtype=jnp.int32)
    top_shift = jnp.int32(WIN - 1)
    first = jnp.where(order == 0, top_shift, other)
    second = jnp.where(order == 0, other, top_shift)
    return jnp.stack([first, second]).astype(jnp.int32)


def block_levels(rng, shape, cuts, smallest, top_value):
    level = 1.0
    for axis_at, shards_of in cuts:
        draws = jax.random.uniform(jax.random.fold_in(jax.random.fold_in(rng, 6), axis_at), (shards_of,), jnp.float32, smallest / len(cuts), top_value / len(cuts))
        level = level * jnp.repeat(jnp.exp(draws), shape[axis_at] // shards_of).reshape((-1,) + (1,) * (len(shape) - 1 - axis_at))
    return level


def shared_out(own_key, own, number, rows, amount, top, most, skew):
    ranking = jax.random.permutation(own_key, amount)
    packed, usual = portions_of(amount, rows * top, most, skew, True), portions_of(amount, rows * top, most, skew, False)
    places = jnp.arange(amount)

    def named(tallies, rotation):
        used = int((tallies > 0).sum())
        fixed = max(1, used // 4)
        moved = fixed + (places - fixed + rotation * (used - fixed)) % max(1, amount - fixed)
        return jnp.zeros((amount,), jnp.int32).at[ranking[jnp.where(places < fixed, places, moved)]].set(jnp.asarray(tallies, jnp.int32))

    tallies = jnp.where(number % 4 == 0, named(packed, number // 4), named(usual, number - number // 4 - 1))
    mixed = jax.random.permutation(jax.random.fold_in(own, 3), amount)
    giver, sink = mixed[0:amount // 2 * 2:2], mixed[1:amount // 2 * 2:2]
    margin = jnp.minimum(tallies[giver] - 1, most - tallies[sink]) // 2
    margin = jnp.where((giver == ranking[0]) | (sink == ranking[0]) | (tallies[sink] == 0), 0, jnp.maximum(margin, 0))
    moved = jax.random.randint(jax.random.fold_in(own, 4), (amount // 2,), 0, 1 << 20) % (margin + 1)
    tallies = tallies.at[giver].add(-moved).at[sink].add(moved)
    members = jnp.searchsorted(jnp.cumsum(tallies), jnp.arange(rows * top), side="right").astype(jnp.int32)
    table = members.reshape(top, rows).T
    table = table[jax.random.permutation(jax.random.fold_in(own, 1), rows)]
    rotation = jax.random.randint(jax.random.fold_in(own, 2), (rows, 1), 0, top)
    return jnp.take_along_axis(table, (jnp.arange(top)[None, :] + rotation) % top, axis=1)


def portions_of(count, total, most, skew, full):
    weights = [(1 << 20) // math.isqrt(standing ** skew) + 1 for standing in range(1, count + 1)]
    largest = most if full else min(most, max(-(-total // count), total * weights[0] // sum(weights)))
    least = 1 if total - largest >= count - 1 else 0
    given, rest = [largest] + [least] * (count - 1), total - largest - least * (count - 1)
    while rest > 0:
        free = [i for i in range(1, count) if given[i] < largest] or [i for i in range(1, count) if given[i] < most]
        pool, left = sum([weights[i] for i in free]), rest
        for i in free:
            more = min(most - given[i], max(1, left * weights[i] // pool), rest)
            given[i] = given[i] + more
            rest = rest - more
    return np.array(given)


def centred(stream_key, dims, deviation, most, cuts=(), kind=jnp.bfloat16):
    values = jax.random.normal(stream_key, dims, jnp.float32) * deviation
    if len(cuts) > 0:
        values = block_levels(stream_key, dims, cuts, -0.22, 0.18) * values
    return jnp.clip(values, min=-most, max=most).astype(kind)


def setup_inputs(seed: int = 0) -> dict:
    seeds = jax.random.split(jax.random.key(seed), 10)
    tokens = draw_tokens(jax.random.fold_in(seeds[9], 71), 0)
    shifts = draw_shifts(jax.random.fold_in(seeds[9], 71), 0)
    w_qkv = centred(seeds[2], (D, 3 * D), D ** -0.5, 0.1875)
    w_out = centred(seeds[3], (D, D), D ** -0.5, 0.1875)
    router = centred(seeds[4], (D, EXPERTS), D ** -0.5, 0.1875)
    expert_ids_keys = jax.random.split(jax.random.fold_in(seeds[5], 1), N_LAT * N_LON * TOK_DEV // TOK_DEV)
    expert_ids_turns = jax.random.permutation(jax.random.fold_in(seeds[5], 3), N_LAT * N_LON * TOK_DEV // TOK_DEV)
    expert_ids = jax.vmap(lambda own, number: shared_out(jax.random.fold_in(seeds[5], 2), own, number, TOK_DEV, EXPERTS, TOP, MOST, 2))(expert_ids_keys, expert_ids_turns).reshape((N_LAT, N_LON, TOK_DEV, TOP))
    w_gate = centred(seeds[6], (D, EXPERTS * FF), D ** -0.5, 0.1875, ((1, 32),))
    w_up = centred(seeds[7], (D, EXPERTS * FF), D ** -0.5, 0.1875, ((1, 32),))
    w_down = centred(seeds[8], (EXPERTS * FF, D), FF ** -0.5, 0.1875, ((0, 32),))
    return dict(tokens=tokens, shifts=shifts, w_qkv=w_qkv, w_out=w_out, router=router, expert_ids=expert_ids, w_gate=w_gate, w_up=w_up, w_down=w_down)


block_rows = 256

def rms_rows(x):
    xf = x.astype(jnp.float32)
    return xf * lax.rsqrt(lax.optimization_barrier(jnp.mean(xf * xf, axis=-1, keepdims=True)) + 1e-05)

def window_attention(qkv, key_valid):
    query = qkv[:, :, 0]
    keys = qkv[:, :, 1]
    values = qkv[:, :, 2]
    qn = rms_rows(query).astype(jnp.bfloat16)
    kn = rms_rows(keys).astype(jnp.bfloat16)
    scores = jnp.einsum('wqhd,wkhd->whqk', qn.astype(jnp.float32), kn.astype(jnp.float32)) / jnp.sqrt(jnp.float32(HEAD))
    expd = jnp.exp(scores) * key_valid[:, None, None, :]
    total = lax.optimization_barrier(jnp.sum(expd, axis=-1, keepdims=True))
    total = jnp.where(total > 0, total, 1.0)
    weights = (expd / total).astype(jnp.bfloat16)
    return jnp.einsum('whqk,wkhd->wqhd', weights.astype(jnp.float32), values.astype(jnp.float32)).astype(jnp.bfloat16)

def reference(tokens, shifts, w_qkv, w_out, router, expert_ids, w_gate, w_up, w_down):
    s_lat = shifts[0].astype(jnp.int32)
    s_lon = shifts[1].astype(jnp.int32)
    zero = jnp.int32(0)
    normed = rms_rows(tokens).astype(jnp.bfloat16)
    rolled = jnp.roll(normed, s_lon, axis=1)
    padded = lax.dynamic_update_slice(jnp.zeros((LAT + WIN, LON, D), jnp.bfloat16), rolled, (s_lat, zero, zero))
    lat_rows = jnp.arange(LAT + WIN, dtype=jnp.int32)
    valid = ((lat_rows >= s_lat) & (lat_rows < s_lat + LAT)).astype(jnp.float32)
    nbands = (LAT + WIN) // WIN
    wcols = LON // WIN
    bands = padded.reshape(nbands, WIN, LON, D)
    band_valid = valid.reshape(nbands, WIN)

    def band_attention(args):
        band, rows_valid = args
        qkv = jnp.dot(band.reshape(-1, D), w_qkv, preferred_element_type=jnp.float32).astype(jnp.bfloat16)
        qkv = qkv.reshape(WIN, wcols, WIN, 3, HEADS, HEAD).transpose(1, 0, 2, 3, 4, 5).reshape(wcols, WIN * WIN, 3, HEADS, HEAD)
        key_valid = jnp.broadcast_to(rows_valid[None, :, None], (wcols, WIN, WIN)).reshape(wcols, WIN * WIN)
        attended = window_attention(qkv, key_valid)
        return attended.reshape(wcols, WIN, WIN, D).transpose(1, 0, 2, 3).reshape(WIN, LON, D)
    out_bands = lax.map(band_attention, (bands, band_valid)).reshape(LAT + WIN, LON, D)
    attended = lax.dynamic_slice(out_bands, (s_lat, zero, zero), (LAT, LON, D))
    attended = jnp.roll(attended, -s_lon, axis=1).reshape(TOKENS, D)
    projected = jnp.dot(attended, w_out, preferred_element_type=jnp.float32)
    mixed = (tokens.reshape(TOKENS, D).astype(jnp.float32) + projected).astype(jnp.bfloat16)
    normed2 = rms_rows(mixed).astype(jnp.bfloat16)
    logits = jnp.dot(normed2, router, preferred_element_type=jnp.float32)
    ids = expert_ids.reshape(N_LAT, N_LON, CLAT, CLON, TOP).transpose(0, 2, 1, 3, 4).reshape(TOKENS, TOP).astype(jnp.int32)
    chosen = jnp.take_along_axis(logits, ids, axis=1)
    sig = jax.nn.sigmoid(chosen)
    gates = sig / lax.optimization_barrier(jnp.sum(sig, axis=1, keepdims=True))
    total_rows = TOKENS * TOP
    flat = ids.reshape(-1)
    counts = lax.optimization_barrier(jnp.sum((flat[:, None] == jnp.arange(EXPERTS, dtype=jnp.int32)[None, :]).astype(jnp.int32), axis=0)).astype(jnp.int32)
    padded_counts = (counts + block_rows - 1) // block_rows * block_rows
    ends = jnp.cumsum(padded_counts).astype(jnp.int32)
    starts = ends - padded_counts
    order = jnp.argsort(flat, stable=True).astype(jnp.int32)
    sorted_ids = flat[order]
    first_sorted = jnp.cumsum(counts).astype(jnp.int32) - counts
    rank_sorted = jnp.arange(total_rows, dtype=jnp.int32) - first_sorted[sorted_ids]
    dest_sorted = starts[sorted_ids] + rank_sorted
    dest = jnp.zeros((total_rows,), jnp.int32).at[order].set(dest_sorted)
    nblocks = -(-total_rows // block_rows) + EXPERTS
    slot_token = jnp.zeros((nblocks * block_rows,), jnp.int32).at[dest].set(jnp.arange(total_rows, dtype=jnp.int32) // TOP)
    block_start = jnp.arange(nblocks, dtype=jnp.int32) * block_rows
    block_expert = jnp.minimum(lax.optimization_barrier(jnp.sum((ends[None, :] <= block_start[:, None]).astype(jnp.int32), axis=1)), EXPERTS - 1).astype(jnp.int32)

    def run_block(index):
        rows_tok = lax.dynamic_slice_in_dim(slot_token, index * block_rows, block_rows)
        rows = normed2[rows_tok]
        expert = block_expert[index]
        total = jnp.zeros((block_rows, D), jnp.float32)
        for piece in range(REPL):
            start = (expert * FF + piece * PIECE).astype(jnp.int32)
            gate_cols = lax.dynamic_slice_in_dim(w_gate, start, PIECE, 1)
            up_cols = lax.dynamic_slice_in_dim(w_up, start, PIECE, 1)
            down_rows = lax.dynamic_slice_in_dim(w_down, start, PIECE, 0)
            gate = jnp.dot(rows, gate_cols, preferred_element_type=jnp.float32)
            upper = jnp.dot(rows, up_cols, preferred_element_type=jnp.float32)
            hidden = (jax.nn.silu(gate) * upper).astype(jnp.bfloat16)
            part = jnp.dot(hidden, down_rows, preferred_element_type=jnp.float32).astype(jnp.bfloat16)
            total = total + part.astype(jnp.float32)
        return total
    outputs = lax.map(run_block, jnp.arange(nblocks, dtype=jnp.int32)).reshape(nblocks * block_rows, D)
    combined = outputs[dest].reshape(TOKENS, TOP, D)
    moe = lax.optimization_barrier(jnp.sum(gates[:, :, None] * combined, axis=1))
    layer_out = (mixed.astype(jnp.float32) + moe).astype(jnp.bfloat16)
    return layer_out.reshape(LAT, LON, D)
```

```python
import functools

import jax
import jax.numpy as jnp
import numpy as np
from jax import lax
from jax.experimental import pallas as pl
from jax.experimental.pallas import tpu as pltpu
from jax.sharding import PartitionSpec as P

HEAD = 64
FF = 1024
TOP = 2
WIN = 8
MOST = 6
UNIT = 16
MAIN = 12
WIDE = 768
TAIL = 256
F32 = jnp.float32
BF16 = jnp.bfloat16


def rms_rows(x):
    xf = x.astype(jnp.float32)
    return xf * lax.rsqrt(jnp.mean(xf * xf, axis=-1, keepdims=True) + 1e-05)


def mm(a, b):
    return jnp.dot(a, b, preferred_element_type=F32)


def hit(cond):
    return jnp.where(cond, 1.0, 0.0)


def head_norm(x, ones):
    xf = x.astype(F32)
    sq = xf * xf
    hi = sq.astype(BF16)
    lo = (sq - hi.astype(F32)).astype(BF16)
    mean = (mm(hi, ones) + mm(lo, ones)) * (1.0 / HEAD)
    return xf * lax.rsqrt(mean + 1e-05)


def places(ids, rank):
    slot = lax.rem(ids, 2) * MOST + rank
    base = lax.div(ids, 2) * UNIT
    return base + slot, base + MAIN + lax.div(slot, 3), lax.rem(slot, 3)


REACH = WIN - 1


def front_kernel(
    packed, n_lat, n_lon, shifts_ref, tok_ref, router_ref, idc_ref, idr_ref, wqkv_hbm, wo_hbm,
    mixed_ref, send_ref, info_ref,
    tall, tosend, side, wqkv, wo, qbuf, kbuf, vbuf, w_sem, vs, vr, hs, hr
):
    lat, lon = lax.axis_index("lat"), lax.axis_index("lon")
    loads = [
        pltpu.make_async_copy(wqkv_hbm, wqkv, w_sem.at[0]),
        pltpu.make_async_copy(wo_hbm, wo, w_sem.at[1]),
    ]
    for load in loads:
        load.start()
    n, width = tok_ref.shape
    cols = n // WIN
    left = (lat, lax.rem(lon + n_lon - 1, n_lon))
    right = (lat, lax.rem(lon + 1, n_lon))
    up, down = (lat - 1, lon), (lat + 1, lon)
    has_up, has_down = lat > 0, lat < n_lat - 1
    mesh_id = pl.DeviceIdType.MESH
    barrier = pltpu.get_barrier_semaphore()
    around = (
        left, right, (lax.rem(lat + n_lat - 1, n_lat), lon), (lax.rem(lat + 1, n_lat), lon)
    )
    for other in around:
        pl.semaphore_signal(barrier, inc=1, device_id=other, device_id_type=mesh_id)

    tall[n : 2 * n, :] = rms_rows(tok_ref[...]).astype(BF16)
    tall[0:cols, :] = jnp.zeros((cols, width), BF16)
    tall[3 * n - cols : 3 * n, :] = jnp.zeros((cols, width), BF16)
    edge = REACH * cols

    @pl.when(lat == 0)
    def _():
        tall[cols:n, :] = jnp.zeros((edge, width), BF16)

    @pl.when(lat == n_lat - 1)
    def _():
        tall[2 * n : 2 * n + edge, :] = jnp.zeros((edge, width), BF16)

    pl.semaphore_wait(barrier, len(around))

    def remote(src, dst, ssem, rsem, to):
        return pltpu.make_async_remote_copy(
            src_ref=src, dst_ref=dst, send_sem=ssem, recv_sem=rsem,
            device_id=to, device_id_type=mesh_id,
        )

    above, below = tall.at[pl.ds(cols, edge)], tall.at[pl.ds(2 * n, edge)]
    go_down = remote(tall.at[pl.ds(n + cols, edge)], above, vs.at[0], vr.at[0], down)
    go_up = remote(tall.at[pl.ds(n, edge)], below, vs.at[1], vr.at[1], up)

    @pl.when(has_down)
    def _():
        go_down.start()

    @pl.when(has_up)
    def _():
        go_up.start()

    s_lat, s_lon = shifts_ref[0], shifts_ref[1]
    sides = 2 * WIN * REACH
    out_row = lax.broadcasted_iota(jnp.int32, (2 * sides, 1), 0)
    local = jnp.where(out_row >= sides, out_row - sides, out_row)
    at = local // REACH * cols + local % REACH + jnp.where(out_row >= sides, cols - REACH, 0)
    start = (WIN - s_lat) * cols
    pick = hit(lax.broadcasted_iota(jnp.int32, (2 * sides, 3 * n), 1) == at + start).astype(BF16)

    @pl.when(has_up)
    def _():
        go_down.wait_recv()

    @pl.when(has_down)
    def _():
        go_up.wait_recv()

    everything = tall[...]
    tosend[...] = mm(pick, everything).astype(BF16)
    go_left = remote(
        tosend.at[pl.ds(0, sides)], side.at[pl.ds(sides, sides)], hs.at[0], hr.at[0], left
    )
    go_right = remote(
        tosend.at[pl.ds(sides, sides)], side.at[pl.ds(0, sides)], hs.at[1], hr.at[1], right
    )
    go_left.start()
    go_right.start()
    there = lax.broadcasted_iota(jnp.int32, (2 * n, 3 * n), 0) + start
    shift = hit(lax.broadcasted_iota(jnp.int32, (2 * n, 3 * n), 1) == there).astype(BF16)
    keys = mm(shift, everything).astype(BF16)

    steps = 4
    group = width // steps
    heads = group // HEAD
    ra = lax.broadcasted_iota(jnp.int32, (group, group), 0) // HEAD
    rb = lax.broadcasted_iota(jnp.int32, (group, group), 1) // HEAD
    ones = hit(ra == rb).astype(BF16)
    own = tall[n : 2 * n, :]
    loads[0].wait()

    def project(cells, first, count):
        for j in range(steps):
            lanes = slice(j * group, (j + 1) * group)
            k = mm(cells, wqkv[:, width + j * group : width + (j + 1) * group]).astype(BF16)
            kbuf[first : first + count, lanes] = head_norm(k, ones).astype(BF16)
            v = mm(cells, wqkv[:, 2 * width + j * group : 2 * width + (j + 1) * group])
            vbuf[first : first + count, lanes] = v.astype(BF16)

    for j in range(steps):
        lanes = slice(j * group, (j + 1) * group)
        q = mm(own, wqkv[:, lanes]).astype(BF16)
        qbuf[:, lanes] = (head_norm(q, ones) * (1.0 / 8.0)).astype(BF16)
    project(keys, 0, 2 * n)

    total_keys = 2 * n + 2 * sides
    i = lax.broadcasted_iota(jnp.int32, (1, total_keys), 1)
    m = jnp.where(i < 2 * n + sides, i - 2 * n, i - 2 * n - sides)
    inner = i < 2 * n
    r_of = jnp.where(inner, i // cols, m // REACH)
    c_of = jnp.where(
        inner, i % cols, m % REACH + jnp.where(i < 2 * n + sides, -REACH, cols)
    )
    at_row = lat * WIN - s_lat + r_of
    valid = (at_row >= 0) & (at_row < WIN * n_lat)
    keyid = jnp.where(valid, (r_of // WIN) * 4 + (c_of + s_lon + WIN) // WIN, -1)
    qi = lax.broadcasted_iota(jnp.int32, (n, 1), 0)
    qid = (qi // cols + s_lat) // WIN * 4 + (qi % cols + s_lon + WIN) // WIN
    same = qid == keyid
    lane = lax.broadcasted_iota(jnp.int32, (n, group), 1) // HEAD

    go_left.wait_recv()
    go_right.wait_recv()
    project(side[...], 2 * n, 2 * sides)
    loads[1].wait()
    acc = tok_ref[...].astype(F32)
    for j in range(steps):
        lanes = slice(j * group, (j + 1) * group)
        qn = qbuf[:, lanes]
        stacked = jnp.concatenate(
            [jnp.where(lane == h, qn, jnp.zeros_like(qn)) for h in range(heads)], axis=0
        )
        scores = lax.dot_general(
            stacked, kbuf[:, lanes], (((1,), (1,)), ((), ())), preferred_element_type=F32
        )
        weights = []
        for h in range(heads):
            e = jnp.where(same, jnp.exp(scores[h * n : (h + 1) * n]), 0.0)
            total = jnp.sum(e, axis=1, keepdims=True)
            weights.append((e * (1.0 / total)).astype(BF16))
        mixedv = mm(jnp.concatenate(weights, axis=0), vbuf[:, lanes])
        att = jnp.zeros((n, group), F32)
        for h in range(heads):
            att = jnp.where(lane == h, mixedv[h * n : (h + 1) * n], att)
        acc = acc + mm(att.astype(BF16), wo[lanes, :])

    mixed = acc.astype(BF16)
    mixed_ref[...] = mixed
    normed2 = rms_rows(mixed).astype(BF16)
    if packed:
        pack(normed2, router_ref, idc_ref, idr_ref, send_ref, info_ref)
    else:
        send_ref[...] = normed2
        info_ref[...] = jnp.zeros_like(info_ref)

    go_left.wait_send()
    go_right.wait_send()

    @pl.when(has_down)
    def _():
        go_down.wait_send()

    @pl.when(has_up)
    def _():
        go_up.wait_send()


def pack(normed2, router_ref, idc_ref, idr_ref, send_ref, info_ref):
    n = normed2.shape[0]
    logits = mm(normed2, router_ref[...])
    experts = logits.shape[1]
    eid = lax.broadcasted_iota(jnp.int32, (n, experts), 1)
    c0, c1 = idc_ref[:, 0:1], idc_ref[:, 1:2]
    r0, r1 = idr_ref[0:1, :], idr_ref[1:2, :]
    s0 = jax.nn.sigmoid(jnp.sum(jnp.where(eid == c0, logits, 0.0), axis=1, keepdims=True))
    s1 = jax.nn.sigmoid(jnp.sum(jnp.where(eid == c1, logits, 0.0), axis=1, keepdims=True))
    g0 = s0 / (s0 + s1)
    g1 = s1 / (s0 + s1)
    ia = lax.broadcasted_iota(jnp.int32, (n, n), 0)
    ib = lax.broadcasted_iota(jnp.int32, (n, n), 1)
    rank0c = jnp.sum(hit((c0 == r0) & (ib < ia)), axis=1, keepdims=True)
    rank1c = jnp.sum(hit(c1 == r0) + hit((c1 == r1) & (ib < ia)), axis=1, keepdims=True)
    rank0r = jnp.sum(hit((c0 == r0) & (ia < ib)), axis=0, keepdims=True)
    rank1r = jnp.sum(hit(c0 == r1) + hit((c1 == r1) & (ia < ib)), axis=0, keepdims=True)
    m0, t0, q0 = places(c0, rank0c.astype(jnp.int32))
    m1, t1, q1 = places(c1, rank1c.astype(jnp.int32))
    col = lax.broadcasted_iota(jnp.int32, info_ref.shape, 1)
    info = jnp.zeros(info_ref.shape, F32)
    for i, x in enumerate((m0, t0, q0, g0, m1, t1, q1, g1)):
        info = jnp.where(col == i, x.astype(F32), info)
    info_ref[...] = info
    m0, t0, q0 = places(r0, rank0r.astype(jnp.int32))
    m1, t1, q1 = places(r1, rank1r.astype(jnp.int32))
    row = lax.broadcasted_iota(jnp.int32, (send_ref.shape[0], n), 0)
    main = (hit(row == m0) + hit(row == m1)).astype(BF16)
    last = normed2[:, WIDE:]
    for t in range(3):
        tail = (hit((row == t0) & (q0 == t)) + hit((row == t1) & (q1 == t))).astype(BF16)
        lanes = slice(t * TAIL, (t + 1) * TAIL)
        send_ref[:, lanes] = (mm(main, normed2[:, lanes]) + mm(tail, last)).astype(BF16)


def front_block(packed, n_lat, n_lon, shifts, tok, w_qkv, w_out, router, ids):
    n, width = tok.shape
    devices = n_lat * n_lon
    send_shape = (devices * UNIT, WIDE) if packed else (n, width)
    sides = 2 * 2 * WIN * REACH
    vm = pl.BlockSpec(memory_space=pltpu.VMEM)
    hbm = pl.BlockSpec(memory_space=pl.ANY)
    dma = pltpu.SemaphoreType.DMA
    keys = 2 * n + sides
    return pl.pallas_call(
        functools.partial(front_kernel, packed, n_lat, n_lon),
        in_specs=[pl.BlockSpec(memory_space=pltpu.SMEM), vm, vm, vm, vm, hbm, hbm],
        out_specs=[vm, vm, vm],
        out_shape=[
            jax.ShapeDtypeStruct((n, width), BF16),
            jax.ShapeDtypeStruct(send_shape, BF16),
            jax.ShapeDtypeStruct((n, 128), F32),
        ],
        scratch_shapes=[
            pltpu.VMEM((3 * n, width), BF16),
            pltpu.VMEM((sides, width), BF16),
            pltpu.VMEM((sides, width), BF16),
            pltpu.VMEM(w_qkv.shape, BF16),
            pltpu.VMEM(w_out.shape, BF16),
            pltpu.VMEM((n, width), BF16),
            pltpu.VMEM((keys, width), BF16),
            pltpu.VMEM((keys, width), BF16),
            dma((2,)), dma((2,)), dma((2,)), dma((2,)), dma((2,)),
        ],
        compiler_params=pltpu.CompilerParams(
            collective_id=2, has_side_effects=True, vmem_limit_bytes=40 * 2**20
        ),
    )(shifts, tok, router, ids, ids.T, w_qkv, w_out)


def expert_kernel(
    n_lat, n_lon, send_ref, tgc_ref, tgr_ref, info_ref, mixed_ref, wg_hbm, wu_hbm, wd_hbm,
    out_ref, got, results, back, wg, wu, wd, w_sem, l_sem, s1, r1, s2, r2
):
    devices = n_lat * n_lon
    lat, lon = lax.axis_index("lat"), lax.axis_index("lon")
    me = lat * n_lon + lon
    loads = [
        pltpu.make_async_copy(src, dst, w_sem.at[i])
        for i, (src, dst) in enumerate(((wg_hbm, wg), (wu_hbm, wu), (wd_hbm, wd)))
    ]
    for load in loads:
        load.start()

    def peer(k):
        return lax.rem(lat + k // n_lon, n_lat), lax.rem(lon + k % n_lon, n_lon)

    def source(k):
        return lax.rem(lat + n_lat - k // n_lon, n_lat), lax.rem(lon + n_lon - k % n_lon, n_lon)

    barrier = pltpu.get_barrier_semaphore()

    def greet(k, c):
        pl.semaphore_signal(
            barrier, inc=1, device_id=peer(k), device_id_type=pl.DeviceIdType.MESH
        )
        return c

    lax.fori_loop(1, devices, greet, 0)
    pl.semaphore_wait(barrier, devices - 1)

    def rows(d):
        return pl.ds(pl.multiple_of(d * UNIT, UNIT), UNIT)

    def copy(src, dst, ssem, rsem, k):
        a, b = peer(k)
        return pltpu.make_async_remote_copy(
            src_ref=src.at[rows(a * n_lon + b)], dst_ref=dst.at[rows(me)],
            send_sem=ssem.at[k], recv_sem=rsem.at[k],
            device_id=(a, b), device_id_type=pl.DeviceIdType.MESH,
        )

    def arrival(src, dst, ssem, rsem, k):
        a, b = source(k)
        return pltpu.make_async_remote_copy(
            src_ref=src.at[rows(me)], dst_ref=dst.at[rows(a * n_lon + b)],
            send_sem=ssem.at[k], recv_sem=rsem.at[k],
            device_id=(a, b), device_id_type=pl.DeviceIdType.MESH,
        )

    def exchange(src, dst, ssem, rsem):
        def start(k, c):
            copy(src, dst, ssem, rsem, k).start()
            return c

        lax.fori_loop(1, devices, start, 0)
        mine = pltpu.make_async_copy(src.at[rows(me)], dst.at[rows(me)], l_sem)
        mine.start()
        mine.wait()

    def finish(src, dst, ssem, rsem):
        def land(k, c):
            arrival(src, dst, ssem, rsem, k).wait_recv()
            return c

        lax.fori_loop(1, devices, land, 0)

    def drain(src, dst, ssem, rsem):
        def sent(k, c):
            copy(src, dst, ssem, rsem, k).wait_send()
            return c

        lax.fori_loop(1, devices, sent, 0)

    exchange(send_ref, got, s1, r1)
    total = devices * UNIT
    count = devices * MAIN
    col = lax.broadcasted_iota(jnp.int32, (count, total), 1)
    pick = hit(col == tgc_ref[:, 0:1]).astype(BF16)
    tails = [hit(col == tgc_ref[:, t + 1 : t + 2]).astype(BF16) for t in range(3)]
    for load in loads:
        load.wait()
    finish(send_ref, got, s1, r1)
    wide = mm(pick, got[...]).astype(BF16)
    last = mm(tails[0], got[:, 0:TAIL])
    for t in range(1, 3):
        last = last + mm(tails[t], got[:, t * TAIL : (t + 1) * TAIL])
    x = jnp.concatenate([wide, last.astype(BF16)], axis=1)
    half = count // 2
    parts = []
    for e in range(2):
        xe = x[e * half : (e + 1) * half]
        gate = mm(xe, wg[:, e * FF : (e + 1) * FF])
        upper = mm(xe, wu[:, e * FF : (e + 1) * FF])
        hidden = (jax.nn.silu(gate) * upper).astype(BF16)
        parts.append(mm(hidden, wd[e * FF : (e + 1) * FF, :]).astype(BF16))
    part = jnp.concatenate(parts, axis=0)
    row = lax.broadcasted_iota(jnp.int32, (total, count), 0)
    put = hit(row == tgr_ref[0:1, :]).astype(BF16)
    for t in range(3):
        put_tail = hit(row == tgr_ref[t + 1 : t + 2, :]).astype(BF16)
        lanes = slice(t * TAIL, (t + 1) * TAIL)
        results[:, lanes] = (mm(put, part[:, lanes]) + mm(put_tail, part[:, WIDE:])).astype(BF16)
    exchange(results, back, s2, r2)
    n = mixed_ref.shape[0]
    at = lax.broadcasted_iota(jnp.int32, (n, total), 1).astype(F32)
    info = info_ref[...]
    m0, t0, q0, g0 = (info[:, i : i + 1] for i in range(4))
    m1, t1, q1, g1 = (info[:, i : i + 1] for i in range(4, 8))

    def split(a):
        hi = a.astype(BF16)
        return jnp.concatenate([hi, (a - hi.astype(F32)).astype(BF16)], axis=0)

    main = split(jnp.where(at == m0, g0, 0.0) + jnp.where(at == m1, g1, 0.0))
    ends = [
        split(
            jnp.where((at == t0) & (q0 == t), g0, 0.0) + jnp.where((at == t1) & (q1 == t), g1, 0.0)
        )
        for t in range(3)
    ]
    finish(results, back, s2, r2)
    final = mm(ends[0], back[:, 0:TAIL])
    for t in range(1, 3):
        final = final + mm(ends[t], back[:, t * TAIL : (t + 1) * TAIL])
    first = mm(main, back[...])
    moe = jnp.concatenate([first[:n] + first[n:], final[:n] + final[n:]], axis=1)
    out_ref[...] = (mixed_ref[...].astype(F32) + moe).astype(BF16)
    drain(send_ref, got, s1, r1)
    drain(results, back, s2, r2)


def targets(devices):
    e, s, k = np.meshgrid(np.arange(2), np.arange(devices), np.arange(MOST), indexing="ij")
    slot = (e * MOST + k).reshape(-1)
    base = s.reshape(-1) * UNIT
    cols = [base + slot]
    for t in range(3):
        cols.append(np.where(slot % 3 == t, base + MAIN + slot // 3, -1))
    return np.stack(cols, axis=1).astype(np.int32)


def expert_block(n_lat, n_lon, send, info, mixed, w_gate, w_up, w_down):
    devices = n_lat * n_lon
    n, width = mixed.shape
    tg = targets(devices)
    vm = pl.BlockSpec(memory_space=pltpu.VMEM)
    hbm = pl.BlockSpec(memory_space=pl.ANY)
    dma = pltpu.SemaphoreType.DMA
    return pl.pallas_call(
        functools.partial(expert_kernel, n_lat, n_lon),
        out_shape=jax.ShapeDtypeStruct((n, width), BF16),
        in_specs=[vm] * 5 + [hbm] * 3,
        out_specs=vm,
        scratch_shapes=[
            pltpu.VMEM((devices * UNIT, WIDE), BF16),
            pltpu.VMEM((devices * UNIT, WIDE), BF16),
            pltpu.VMEM((devices * UNIT, WIDE), BF16),
            pltpu.VMEM(w_gate.shape, BF16),
            pltpu.VMEM(w_up.shape, BF16),
            pltpu.VMEM(w_down.shape, BF16),
            dma((3,)), dma, dma((devices,)), dma((devices,)), dma((devices,)), dma((devices,)),
        ],
        compiler_params=pltpu.CompilerParams(
            collective_id=1, has_side_effects=True, vmem_limit_bytes=56 * 2**20
        ),
    )(send, jnp.asarray(tg), jnp.asarray(tg.T), info, mixed, w_gate, w_up, w_down)


def body(tokens, shifts, w_qkv, w_out, router, expert_ids, w_gate, w_up, w_down):
    n_lat = lax.axis_size("lat")
    n_lon = lax.axis_size("lon")
    devices = n_lat * n_lon
    rows, cols, width = tokens.shape
    packed = w_gate.shape[1] == 2 * FF
    ids = expert_ids.reshape(-1, TOP)
    mixed, send, info = front_block(
        packed, n_lat, n_lon, shifts, tokens.reshape(-1, width), w_qkv, w_out, router, ids
    )
    if packed:
        out = expert_block(n_lat, n_lon, send, info, mixed, w_gate, w_up, w_down)
        return out.reshape(rows, cols, width)
    return general(mixed, send, router, ids, w_gate, w_up, w_down, devices, rows, cols)


def general(mixed, normed2, router, ids, w_gate, w_up, w_down, devices, rows, cols):
    width = mixed.shape[1]
    logits = jnp.dot(normed2, router, preferred_element_type=jnp.float32)
    experts = router.shape[1]
    expert_iota = jnp.arange(experts, dtype=jnp.int32)
    picks = ids[:, :, None] == expert_iota[None, None, :]
    chosen = jnp.sum(jnp.where(picks, logits[:, None, :], 0.0), axis=-1)
    sig = jax.nn.sigmoid(chosen)
    gates = sig / jnp.sum(sig, axis=1, keepdims=True)
    flat = ids.reshape(-1)
    order = jnp.arange(flat.shape[0], dtype=jnp.int32)
    earlier = (flat[:, None] == flat[None, :]) & (order[None, :] < order[:, None])
    rank = jnp.sum(earlier.astype(jnp.int32), axis=1)
    share = w_gate.shape[1]
    piece = min(FF, share)
    repl = FF // piece
    group = share // piece
    most = MOST
    cap = group * most
    token_of = jnp.arange(flat.shape[0], dtype=jnp.int32) // TOP
    slot = flat % group * most + rank
    slot_index = jnp.stack(
        [(flat // group * repl + copy) * cap + slot for copy in range(repl)], axis=0
    )
    routed = normed2[token_of]
    send = (
        jnp.zeros((devices * cap, width), jnp.bfloat16)
        .at[slot_index.reshape(-1)]
        .set(jnp.tile(routed, (repl, 1)))
    )
    send = send.reshape(devices, group, most, width)
    received = lax.all_to_all(send, ("lat", "lon"), split_axis=0, concat_axis=0, tiled=True)
    results = []
    for local in range(group):
        block = received[:, local].reshape(-1, width)
        gate = jnp.dot(
            block,
            w_gate[:, local * piece : (local + 1) * piece],
            preferred_element_type=jnp.float32,
        )
        upper = jnp.dot(
            block, w_up[:, local * piece : (local + 1) * piece], preferred_element_type=jnp.float32
        )
        hidden = (jax.nn.silu(gate) * upper).astype(jnp.bfloat16)
        part = jnp.dot(
            hidden, w_down[local * piece : (local + 1) * piece], preferred_element_type=jnp.float32
        ).astype(jnp.bfloat16)
        results.append(part.reshape(received.shape[0], received.shape[2], width))
    back = lax.all_to_all(
        jnp.stack(results, axis=1), ("lat", "lon"), split_axis=0, concat_axis=0, tiled=True
    )
    back_flat = back.reshape(devices * cap, width)
    combined = jnp.zeros((flat.shape[0], width), jnp.float32)
    for copy in range(repl):
        combined = combined + back_flat[slot_index[copy]].astype(jnp.float32)
    combined = combined.reshape(-1, TOP, width)
    moe = jnp.sum(gates[:, :, None] * combined, axis=1)
    layer_out = (mixed.astype(jnp.float32) + moe).astype(jnp.bfloat16)
    return layer_out.reshape(rows, cols, width)


def solution(mesh):
    placed = (
        P("lat", "lon", None),
        P(),
        P(),
        P(),
        P(),
        P("lat", "lon", None, None),
        P(None, ("lat", "lon")),
        P(None, ("lat", "lon")),
        P(("lat", "lon"), None),
    )
    return jax.shard_map(
        body, mesh=mesh, in_specs=placed, out_specs=P("lat", "lon", None), check_vma=False
    )
```

```python
import functools

import jax
import jax.numpy as jnp
import numpy as np
from jax import lax
from jax.experimental import pallas as pl
from jax.experimental.pallas import tpu as pltpu
from jax.sharding import PartitionSpec as P

HEAD = 64
FF = 1024
TOP = 2
WIN = 8
MOST = 6
UNIT = 16
MAIN = 12
WIDE = 768
TAIL = 256
F32 = jnp.float32
BF16 = jnp.bfloat16


def rms_rows(x):
    xf = x.astype(jnp.float32)
    return xf * lax.rsqrt(jnp.mean(xf * xf, axis=-1, keepdims=True) + 1e-05)


def mm(a, b):
    return jnp.dot(a, b, preferred_element_type=F32)


def hit(cond):
    return jnp.where(cond, 1.0, 0.0)


def head_norm(x, ones):
    xf = x.astype(F32)
    sq = xf * xf
    hi = sq.astype(BF16)
    lo = (sq - hi.astype(F32)).astype(BF16)
    mean = (mm(hi, ones) + mm(lo, ones)) * (1.0 / HEAD)
    return xf * lax.rsqrt(mean + 1e-05)


REACH = WIN - 1


def front_kernel(
    n_lat, n_lon, shifts_ref, tok_ref, wqkv_hbm, wo_hbm, mixed_ref, send_ref,
    tall, tosend, side, wqkv, wo, qbuf, kbuf, vbuf, w_sem, vs, vr, hs, hr
):
    lat, lon = lax.axis_index("lat"), lax.axis_index("lon")
    loads = [
        pltpu.make_async_copy(wqkv_hbm, wqkv, w_sem.at[0]),
        pltpu.make_async_copy(wo_hbm, wo, w_sem.at[1]),
    ]
    for load in loads:
        load.start()
    n, width = tok_ref.shape
    cols = n // WIN
    left = (lat, lax.rem(lon + n_lon - 1, n_lon))
    right = (lat, lax.rem(lon + 1, n_lon))
    up, down = (lat - 1, lon), (lat + 1, lon)
    has_up, has_down = lat > 0, lat < n_lat - 1
    mesh_id = pl.DeviceIdType.MESH
    barrier = pltpu.get_barrier_semaphore()
    around = (
        left, right, (lax.rem(lat + n_lat - 1, n_lat), lon), (lax.rem(lat + 1, n_lat), lon)
    )
    for other in around:
        pl.semaphore_signal(barrier, inc=1, device_id=other, device_id_type=mesh_id)

    tall[n : 2 * n, :] = rms_rows(tok_ref[...]).astype(BF16)
    tall[0:cols, :] = jnp.zeros((cols, width), BF16)
    tall[3 * n - cols : 3 * n, :] = jnp.zeros((cols, width), BF16)
    edge = REACH * cols

    @pl.when(lat == 0)
    def _():
        tall[cols:n, :] = jnp.zeros((edge, width), BF16)

    @pl.when(lat == n_lat - 1)
    def _():
        tall[2 * n : 2 * n + edge, :] = jnp.zeros((edge, width), BF16)

    pl.semaphore_wait(barrier, len(around))

    def remote(src, dst, ssem, rsem, to):
        return pltpu.make_async_remote_copy(
            src_ref=src, dst_ref=dst, send_sem=ssem, recv_sem=rsem,
            device_id=to, device_id_type=mesh_id,
        )

    above, below = tall.at[pl.ds(cols, edge)], tall.at[pl.ds(2 * n, edge)]
    go_down = remote(tall.at[pl.ds(n + cols, edge)], above, vs.at[0], vr.at[0], down)
    go_up = remote(tall.at[pl.ds(n, edge)], below, vs.at[1], vr.at[1], up)

    @pl.when(has_down)
    def _():
        go_down.start()

    @pl.when(has_up)
    def _():
        go_up.start()

    s_lat, s_lon = shifts_ref[0], shifts_ref[1]
    sides = 2 * WIN * REACH
    out_row = lax.broadcasted_iota(jnp.int32, (2 * sides, 1), 0)
    local = jnp.where(out_row >= sides, out_row - sides, out_row)
    at = local // REACH * cols + local % REACH + jnp.where(out_row >= sides, cols - REACH, 0)
    start = (WIN - s_lat) * cols
    pick = hit(lax.broadcasted_iota(jnp.int32, (2 * sides, 3 * n), 1) == at + start).astype(BF16)

    @pl.when(has_up)
    def _():
        go_down.wait_recv()

    @pl.when(has_down)
    def _():
        go_up.wait_recv()

    everything = tall[...]
    tosend[...] = mm(pick, everything).astype(BF16)
    go_left = remote(
        tosend.at[pl.ds(0, sides)], side.at[pl.ds(sides, sides)], hs.at[0], hr.at[0], left
    )
    go_right = remote(
        tosend.at[pl.ds(sides, sides)], side.at[pl.ds(0, sides)], hs.at[1], hr.at[1], right
    )
    go_left.start()
    go_right.start()
    there = lax.broadcasted_iota(jnp.int32, (2 * n, 3 * n), 0) + start
    shift = hit(lax.broadcasted_iota(jnp.int32, (2 * n, 3 * n), 1) == there).astype(BF16)
    keys = mm(shift, everything).astype(BF16)

    steps = 4
    group = width // steps
    heads = group // HEAD
    ra = lax.broadcasted_iota(jnp.int32, (group, group), 0) // HEAD
    rb = lax.broadcasted_iota(jnp.int32, (group, group), 1) // HEAD
    ones = hit(ra == rb).astype(BF16)
    own = tall[n : 2 * n, :]
    loads[0].wait()

    def project(cells, first, count):
        for j in range(steps):
            lanes = slice(j * group, (j + 1) * group)
            k = mm(cells, wqkv[:, width + j * group : width + (j + 1) * group]).astype(BF16)
            kbuf[first : first + count, lanes] = head_norm(k, ones).astype(BF16)
            v = mm(cells, wqkv[:, 2 * width + j * group : 2 * width + (j + 1) * group])
            vbuf[first : first + count, lanes] = v.astype(BF16)

    for j in range(steps):
        lanes = slice(j * group, (j + 1) * group)
        q = mm(own, wqkv[:, lanes]).astype(BF16)
        qbuf[:, lanes] = (head_norm(q, ones) * (1.0 / 8.0)).astype(BF16)
    project(keys, 0, 2 * n)

    total_keys = 2 * n + 2 * sides
    i = lax.broadcasted_iota(jnp.int32, (1, total_keys), 1)
    m = jnp.where(i < 2 * n + sides, i - 2 * n, i - 2 * n - sides)
    inner = i < 2 * n
    r_of = jnp.where(inner, i // cols, m // REACH)
    c_of = jnp.where(
        inner, i % cols, m % REACH + jnp.where(i < 2 * n + sides, -REACH, cols)
    )
    at_row = lat * WIN - s_lat + r_of
    valid = (at_row >= 0) & (at_row < WIN * n_lat)
    keyid = jnp.where(valid, (r_of // WIN) * 4 + (c_of + s_lon + WIN) // WIN, -1)
    qi = lax.broadcasted_iota(jnp.int32, (n, 1), 0)
    qid = (qi // cols + s_lat) // WIN * 4 + (qi % cols + s_lon + WIN) // WIN
    same = qid == keyid
    lane = lax.broadcasted_iota(jnp.int32, (n, group), 1) // HEAD

    go_left.wait_recv()
    go_right.wait_recv()
    project(side[...], 2 * n, 2 * sides)
    loads[1].wait()
    acc = tok_ref[...].astype(F32)
    for j in range(steps):
        lanes = slice(j * group, (j + 1) * group)
        qn = qbuf[:, lanes]
        stacked = jnp.concatenate(
            [jnp.where(lane == h, qn, jnp.zeros_like(qn)) for h in range(heads)], axis=0
        )
        scores = lax.dot_general(
            stacked, kbuf[:, lanes], (((1,), (1,)), ((), ())), preferred_element_type=F32
        )
        weights = []
        for h in range(heads):
            e = jnp.where(same, jnp.exp(scores[h * n : (h + 1) * n]), 0.0)
            total = jnp.sum(e, axis=1, keepdims=True)
            weights.append((e * (1.0 / total)).astype(BF16))
        mixedv = mm(jnp.concatenate(weights, axis=0), vbuf[:, lanes])
        att = jnp.zeros((n, group), F32)
        for h in range(heads):
            att = jnp.where(lane == h, mixedv[h * n : (h + 1) * n], att)
        acc = acc + mm(att.astype(BF16), wo[lanes, :])

    mixed = acc.astype(BF16)
    mixed_ref[...] = mixed
    normed2 = rms_rows(mixed).astype(BF16)
    send_ref[...] = normed2

    go_left.wait_send()
    go_right.wait_send()

    @pl.when(has_down)
    def _():
        go_down.wait_send()

    @pl.when(has_up)
    def _():
        go_up.wait_send()


def front_block(n_lat, n_lon, shifts, tok, w_qkv, w_out):
    n, width = tok.shape
    sides = 2 * 2 * WIN * REACH
    vm = pl.BlockSpec(memory_space=pltpu.VMEM)
    hbm = pl.BlockSpec(memory_space=pl.ANY)
    dma = pltpu.SemaphoreType.DMA
    keys = 2 * n + sides
    return pl.pallas_call(
        functools.partial(front_kernel, n_lat, n_lon),
        in_specs=[pl.BlockSpec(memory_space=pltpu.SMEM), vm, hbm, hbm],
        out_specs=[vm, vm],
        out_shape=[jax.ShapeDtypeStruct((n, width), BF16)] * 2,
        scratch_shapes=[
            pltpu.VMEM((3 * n, width), BF16),
            pltpu.VMEM((sides, width), BF16),
            pltpu.VMEM((sides, width), BF16),
            pltpu.VMEM(w_qkv.shape, BF16),
            pltpu.VMEM(w_out.shape, BF16),
            pltpu.VMEM((n, width), BF16),
            pltpu.VMEM((keys, width), BF16),
            pltpu.VMEM((keys, width), BF16),
            dma((2,)), dma((2,)), dma((2,)), dma((2,)), dma((2,)),
        ],
        compiler_params=pltpu.CompilerParams(
            collective_id=2, has_side_effects=True, vmem_limit_bytes=40 * 2**20
        ),
    )(shifts, tok, w_qkv, w_out)


def iota(shape, axis):
    return lax.broadcasted_iota(jnp.int32, shape, axis)


def onehot(shape, target):
    return hit(iota(shape, 1) == target).astype(BF16)


def flip(z, g):
    return 2 * ((z // 2 + g // 2) % 2) + (z + g) % 2


def layer_kernel(
    n_lat, n_lon, shifts_hbm, tok_hbm, router_hbm, ids_hbm, wqkv_hbm, wo_hbm, wg_hbm, wu_hbm,
    wd_hbm, out_ref, shifts, tok, router, ids, wqkv, wo, wg, wu, wd, own, sideout, sidein, vertin,
    side, cornin, qbuf, kbuf, vbuf, place, comb, info, normed2, acc, send, got, results, back,
    w_sem, vs, vr, hs, hr, cs, cr, s1, r1, s2, r2
):
    lat, lon = lax.axis_index("lat"), lax.axis_index("lon")
    z, x = lon // 2, lon % 2
    plane = 2 * n_lat
    slab = plane * UNIT
    here = lat * 2 + x
    loads = [
        pltpu.make_async_copy(src, dst, w_sem.at[i])
        for i, (src, dst) in enumerate((
            (tok_hbm, tok), (shifts_hbm, shifts), (ids_hbm, ids), (wqkv_hbm, wqkv),
            (wo_hbm, wo), (router_hbm, router), (wg_hbm, wg), (wu_hbm, wu), (wd_hbm, wd),
        ))
    ]
    for load in loads[:6]:
        load.start()
    n, width = tok.shape
    cols = n // WIN
    mesh_id = pl.DeviceIdType.MESH
    left = (lat, lax.rem(lon + n_lon - 1, n_lon))
    right = (lat, lax.rem(lon + 1, n_lon))
    up, down = (lat - 1, lon), (lat + 1, lon)
    has_up, has_down = lat > 0, lat < n_lat - 1

    barrier = pltpu.get_barrier_semaphore()
    devices = n_lat * n_lon

    def greet(k, c):
        other = (lax.rem(lat + k // n_lon, n_lat), lax.rem(lon + k % n_lon, n_lon))
        pl.semaphore_signal(barrier, inc=1, device_id=other, device_id_type=mesh_id)
        return c

    lax.fori_loop(1, devices, greet, 0)

    edge = REACH * cols
    nook = WIN * WIN

    @pl.when(lat == 0)
    def _():
        vertin[0:edge, :] = jnp.zeros((edge, width), BF16)
        cornin[0:nook, :] = jnp.zeros((nook, width), BF16)

    @pl.when(lat == n_lat - 1)
    def _():
        vertin[edge : 2 * edge, :] = jnp.zeros((edge, width), BF16)
        cornin[nook : 2 * nook, :] = jnp.zeros((nook, width), BF16)

    half = WIN * REACH
    lanes2 = width // 2
    r = iota((4 * half, 1), 0)
    within = r % half
    cell = within // REACH * cols + within % REACH + jnp.where(r >= 2 * half, cols - REACH, 0)
    second = r // half % 2 == 1
    pick0 = onehot((4 * half, n), jnp.where(second, -1, cell))
    pick1 = onehot((4 * half, n), jnp.where(second, cell, -1))
    loads[0].wait()
    own[...] = rms_rows(tok[...]).astype(BF16)
    sideout[...] = (
        mm(pick0, own[:, 0:lanes2]) + mm(pick1, own[:, lanes2:width])
    ).astype(BF16)
    pl.semaphore_wait(barrier, devices - 1)

    def remote(src, dst, ssem, rsem, to):
        return pltpu.make_async_remote_copy(
            src_ref=src, dst_ref=dst, send_sem=ssem, recv_sem=rsem,
            device_id=to, device_id_type=mesh_id,
        )

    first, last = pl.ds(0, 2 * half), pl.ds(2 * half, 2 * half)
    go_left = remote(sideout.at[first], sidein.at[last], hs.at[0], hr.at[0], left)
    go_right = remote(sideout.at[last], sidein.at[first], hs.at[1], hr.at[1], right)
    go_left.start()
    go_right.start()
    go_down = remote(
        own.at[pl.ds(n - edge, edge)], vertin.at[pl.ds(0, edge)], vs.at[0], vr.at[0], down
    )
    go_up = remote(own.at[pl.ds(0, edge)], vertin.at[pl.ds(edge, edge)], vs.at[1], vr.at[1], up)

    @pl.when(has_down)
    def _():
        go_down.start()

    @pl.when(has_up)
    def _():
        go_up.start()

    steps = 4
    group = width // steps
    heads = group // HEAD
    ones = hit(iota((group, group), 0) // HEAD == iota((group, group), 1) // HEAD).astype(BF16)
    loads[3].wait()
    for load in loads[6:]:
        load.start()

    def project(cells, at):
        for j in range(steps):
            lanes = slice(j * group, (j + 1) * group)
            k = mm(cells, wqkv[:, width + j * group : width + (j + 1) * group]).astype(BF16)
            kbuf[at : at + cells.shape[0], lanes] = head_norm(k, ones).astype(BF16)
            v = mm(cells, wqkv[:, 2 * width + j * group : 2 * width + (j + 1) * group])
            vbuf[at : at + cells.shape[0], lanes] = v.astype(BF16)

    for j in range(steps):
        lanes = slice(j * group, (j + 1) * group)
        q = mm(own[...], wqkv[:, lanes]).astype(BF16)
        qbuf[:, lanes] = (head_norm(q, ones) * (1.0 / 8.0)).astype(BF16)
    project(own[...], 0)

    loads[1].wait()
    s_lat, s_lon = shifts[0], shifts[1]
    w = iota((n, 1), 0)
    v_at = w // cols
    vert_at = jnp.where(v_at < s_lat, REACH - s_lat + v_at, REACH + v_at - s_lat)
    vert_pick = onehot((n, 2 * edge), vert_at * cols + w % cols)

    @pl.when(has_up)
    def _():
        go_down.wait_recv()

    @pl.when(has_down)
    def _():
        go_up.wait_recv()

    project(mm(vert_pick, vertin[...]).astype(BF16), n)

    loads[2].wait()
    routes(n_lon, z, ids, info, place)

    w = iota((nook, 1), 0)
    major, minor = w // WIN, w % WIN
    side_at = major * REACH + jnp.where(
        minor < s_lon, REACH - s_lon + minor, 2 * half + minor - s_lon
    )
    side0 = onehot((nook, 4 * half), side_at)
    side1 = onehot((nook, 4 * half), side_at + half)
    corn_at = jnp.where(major < s_lat, WIN - s_lat + major, WIN + major - s_lat)
    corn_pick = onehot((nook, 2 * nook), corn_at * WIN + minor)
    go_left.wait_recv()
    go_right.wait_recv()
    side[:, 0:lanes2] = mm(side0, sidein[...]).astype(BF16)
    side[:, lanes2:width] = mm(side1, sidein[...]).astype(BF16)
    corn_down = remote(side, cornin.at[pl.ds(0, nook)], cs.at[0], cr.at[0], down)
    corn_up = remote(side, cornin.at[pl.ds(nook, nook)], cs.at[1], cr.at[1], up)

    @pl.when(has_down)
    def _():
        corn_down.start()

    @pl.when(has_up)
    def _():
        corn_up.start()

    project(side[...], 2 * n)

    total_keys = 2 * n + 2 * nook
    i = iota((1, total_keys), 1)
    in_own, in_vert, in_side = i < n, i < 2 * n, i < 2 * n + nook
    m = i - jnp.where(in_side, 2 * n, 2 * n + nook)
    row = jnp.where(in_vert, jnp.where(in_own, i, i - n) // cols, m // WIN)
    col = jnp.where(in_vert, i % cols, m % WIN)
    inside = in_own | (in_side & ~in_vert)
    key_row = jnp.where(inside, (row + s_lat) // WIN, jnp.where(row < s_lat, 0, 1))
    key_col = jnp.where(in_vert, (col + s_lon) // WIN, jnp.where(col < s_lon, 0, 2))
    gone = ~inside & (((row < s_lat) & (lat == 0)) | ((row >= s_lat) & (lat == n_lat - 1)))
    keyid = jnp.where(gone, -1, key_row * 4 + key_col)
    w = iota((n, 1), 0)
    same = (w // cols + s_lat) // WIN * 4 + (w % cols + s_lon) // WIN == keyid
    lane = iota((n, group), 1) // HEAD

    @pl.when(has_up)
    def _():
        corn_down.wait_recv()

    @pl.when(has_down)
    def _():
        corn_up.wait_recv()

    project(mm(corn_pick, cornin[...]).astype(BF16), 2 * n + nook)

    loads[4].wait()
    total = tok[...].astype(F32)
    for j in range(steps):
        lanes = slice(j * group, (j + 1) * group)
        qn = qbuf[:, lanes]
        stacked = jnp.concatenate(
            [jnp.where(lane == h, qn, jnp.zeros_like(qn)) for h in range(heads)], axis=0
        )
        scores = lax.dot_general(
            stacked, kbuf[:, lanes], (((1,), (1,)), ((), ())), preferred_element_type=F32
        )
        weights = []
        for h in range(heads):
            e = jnp.where(same, jnp.exp(scores[h * n : (h + 1) * n]), 0.0)
            weights.append((e * (1.0 / jnp.sum(e, axis=1, keepdims=True))).astype(BF16))
        mixedv = mm(jnp.concatenate(weights, axis=0), vbuf[:, lanes])
        att = jnp.zeros((n, group), F32)
        for h in range(heads):
            att = jnp.where(lane == h, mixedv[h * n : (h + 1) * n], att)
        total = total + mm(att.astype(BF16), wo[lanes, :])

    mixed = total.astype(BF16)
    acc[...] = mixed.astype(F32)
    normed2[...] = rms_rows(mixed).astype(BF16)
    tail_rows = normed2[:, WIDE:width]
    for t in range(3):
        lanes = slice(t * TAIL, (t + 1) * TAIL)
        both = jnp.concatenate([normed2[:, lanes], tail_rows], axis=0)
        send[:, lanes] = mm(place[t * 4 * slab : (t + 1) * 4 * slab, :], both).astype(BF16)

    def rows(g, j):
        return pl.ds(pl.multiple_of(g * slab + j * UNIT, UNIT), UNIT)

    def copy(src, dst, ssem, rsem, g, k):
        to_lat, to_x = (lat + k // 2) % n_lat, (x + k) % 2
        return remote(
            src.at[rows(g, to_lat * 2 + to_x)], dst.at[rows(g, here)],
            ssem.at[g * plane + k], rsem.at[g * plane + k], (to_lat, flip(z, g) * 2 + to_x),
        )

    def arrival(src, dst, ssem, rsem, g, k):
        of_lat, of_x = (lat + n_lat - k // 2) % n_lat, (x + k) % 2
        return remote(
            src.at[rows(g, here)], dst.at[rows(g, of_lat * 2 + of_x)],
            ssem.at[g * plane + k], rsem.at[g * plane + k], (of_lat, flip(z, g) * 2 + of_x),
        )

    def launch(src, dst, ssem, rsem, g, begin=0):
        def go(k, c):
            copy(src, dst, ssem, rsem, g, k).start()
            return c

        lax.fori_loop(begin, plane, go, 0)

    def land(src, dst, ssem, rsem, g, begin=0):
        def go(k, c):
            arrival(src, dst, ssem, rsem, g, k).wait_recv()
            return c

        lax.fori_loop(begin, plane, go, 0)

    def drain(src, dst, ssem, rsem):
        def go(k, c):
            copy(src, dst, ssem, rsem, k // plane, k % plane).wait_send()
            return c

        lax.fori_loop(1, 4 * plane, go, 0)

    out1, out2 = (send, got, s1, r1), (results, back, s2, r2)

    def pair(k, c):
        copy(*out1, 3, k).start()
        copy(*out1, 1, k).start()
        return c

    lax.fori_loop(0, plane, pair, 0)
    launch(*out1, 2)
    launch(*out1, 0, 1)
    got[rows(0, here), :] = send[rows(0, here), :]

    loads[5].wait()
    gates(normed2, router, ids, info, comb)

    half_rows = plane * MOST
    count = 2 * half_rows
    r = iota((count, 1), 0)
    slot = r // half_rows * MOST + r % MOST
    base = r % half_rows // MOST * UNIT
    pick = onehot((count, slab), base + slot)
    tails = [
        onehot((count, slab), jnp.where(slot % 3 == t, base + MAIN + slot // 3, -1))
        for t in range(3)
    ]
    r = iota((1, count), 1)
    slot = r // half_rows * MOST + r % MOST
    base = r % half_rows // MOST * UNIT
    target = iota((slab, count), 0)
    put = hit(target == base + slot).astype(BF16)
    put_tails = [
        hit(target == jnp.where(slot % 3 == t, base + MAIN + slot // 3, -1)).astype(BF16)
        for t in range(3)
    ]
    for load in loads[6:]:
        load.wait()

    def experts(i, turn):
        g = turn - 1
        begin = jnp.where(g == 0, 1, 0)
        land(*out1, g, begin)
        at = pl.ds(pl.multiple_of(g * slab, slab), slab)
        wide = mm(pick, got[at, :]).astype(BF16)
        end = mm(tails[0], got[at, 0:TAIL])
        for t in range(1, 3):
            end = end + mm(tails[t], got[at, t * TAIL : (t + 1) * TAIL])
        cells = jnp.concatenate([wide, end.astype(BF16)], axis=1)
        parts = []
        for e in range(2):
            xe = cells[e * half_rows : (e + 1) * half_rows]
            gate = mm(xe, wg[:, e * FF : (e + 1) * FF])
            upper = mm(xe, wu[:, e * FF : (e + 1) * FF])
            hidden = (jax.nn.silu(gate) * upper).astype(BF16)
            parts.append(mm(hidden, wd[e * FF : (e + 1) * FF, :]).astype(BF16))
        part = jnp.concatenate(parts, axis=0)
        for t in range(3):
            lanes = slice(t * TAIL, (t + 1) * TAIL)
            results[at, lanes] = (
                mm(put, part[:, lanes]) + mm(put_tails[t], part[:, WIDE:width])
            ).astype(BF16)
        launch(*out2, g, begin)
        return turn * 3 % 5

    lax.fori_loop(0, 4, experts, 4)
    back[rows(0, here), :] = results[rows(0, here), :]

    def gather(i, turn):
        g = turn - 1
        land(*out2, g, jnp.where(g == 0, 1, 0))
        at = pl.ds(pl.multiple_of(g * slab, slab), slab)
        for t in range(3):
            lanes = slice(t * TAIL, (t + 1) * TAIL)
            s = mm(comb[t * 4 * n : (t + 1) * 4 * n, at], back[at, lanes])
            acc[:, lanes] += s[0:n] + s[n : 2 * n]
            acc[:, WIDE:width] += s[2 * n : 3 * n] + s[3 * n : 4 * n]
        return turn * 3 % 5

    lax.fori_loop(0, 4, gather, 4)
    out_ref[...] = acc[...].astype(BF16)

    go_left.wait_send()
    go_right.wait_send()

    @pl.when(has_down)
    def _():
        go_down.wait_send()
        corn_down.wait_send()

    @pl.when(has_up)
    def _():
        go_up.wait_send()
        corn_up.wait_send()

    drain(*out1)
    drain(*out2)


def routes(n_lon, z, ids, info, place):
    n = ids.shape[1]
    r0, r1 = ids[0:1, :], ids[1:2, :]
    ia, ib = iota((n, n), 0), iota((n, n), 1)

    def column(row):
        return jnp.sum(jnp.where(ia == ib, row.astype(F32), 0.0), axis=1, keepdims=True)

    c0, c1 = column(r0).astype(jnp.int32), column(r1).astype(jnp.int32)
    rank0c = jnp.sum(hit((c0 == r0) & (ib < ia)), axis=1, keepdims=True)
    rank1c = jnp.sum(hit(c1 == r0) + hit((c1 == r1) & (ib < ia)), axis=1, keepdims=True)
    rank0r = jnp.sum(hit((c0 == r0) & (ia < ib)), axis=0, keepdims=True)
    rank1r = jnp.sum(hit(c0 == r1) + hit((c1 == r1) & (ia < ib)), axis=0, keepdims=True)

    def places(e, rank):
        slot = e % 2 * MOST + rank.astype(jnp.int32)
        device = e // 2
        at_lat, at_lon = device // n_lon, device % n_lon
        base = (flip(at_lon // 2, z) * (place.shape[0] // 12 // UNIT) + at_lat * 2 + at_lon % 2) * UNIT
        return base + slot, base + MAIN + slot // 3, slot % 3

    m0, t0, q0 = places(c0, rank0c)
    m1, t1, q1 = places(c1, rank1c)
    col = iota(info.shape, 1)
    table = jnp.zeros(info.shape, F32)
    for i, v in enumerate((m0, t0, q0, m1, t1, q1, c0, c1)):
        table = jnp.where(col == i, v.astype(F32), table)
    info[...] = table
    m0, t0, q0 = places(r0, rank0r)
    m1, t1, q1 = places(r1, rank1r)
    total = place.shape[0] // 3
    row = iota((total, n), 0)
    main = (hit(row == m0) + hit(row == m1)).astype(BF16)
    for t in range(3):
        rows = slice(t * total, (t + 1) * total)
        place[rows, 0:n] = main
        place[rows, n : 2 * n] = (
            hit((row == t0) & (q0 == t)) + hit((row == t1) & (q1 == t))
        ).astype(BF16)


def gates(normed2, router, ids, info, comb):
    logits = lax.dot_general(
        normed2[...], router[...], (((1,), (1,)), ((), ())), preferred_element_type=F32
    )
    n = logits.shape[0]
    eid = iota(logits.shape, 1).astype(F32)
    m0, t0, q0, m1, t1, q1, c0, c1 = (info[:, i : i + 1] for i in range(8))
    s0 = jax.nn.sigmoid(jnp.sum(jnp.where(eid == c0, logits, 0.0), axis=1, keepdims=True))
    s1 = jax.nn.sigmoid(jnp.sum(jnp.where(eid == c1, logits, 0.0), axis=1, keepdims=True))
    g0 = s0 / (s0 + s1)
    g1 = s1 / (s0 + s1)
    at = iota((n, comb.shape[1]), 1).astype(F32)

    def keep(first, a):
        hi = a.astype(BF16)
        comb[first : first + n, :] = hi
        comb[first + n : first + 2 * n, :] = (a - hi.astype(F32)).astype(BF16)

    main = jnp.where(at == m0, g0, 0.0) + jnp.where(at == m1, g1, 0.0)
    for t in range(3):
        keep(t * 4 * n, main)
        keep(
            t * 4 * n + 2 * n,
            jnp.where((at == t0) & (q0 == t), g0, 0.0) + jnp.where((at == t1) & (q1 == t), g1, 0.0),
        )


def layer_block(n_lat, n_lon, shifts, tok, router, ids, w_qkv, w_out, w_gate, w_up, w_down):
    n, width = tok.shape
    total = n_lat * n_lon * UNIT
    keys = 2 * n + 2 * WIN * WIN
    hbm = pl.BlockSpec(memory_space=pl.ANY)
    dma = pltpu.SemaphoreType.DMA

    def vmem(*shape, dtype=BF16):
        return pltpu.VMEM(shape, dtype)

    return pl.pallas_call(
        functools.partial(layer_kernel, n_lat, n_lon),
        out_shape=jax.ShapeDtypeStruct((n, width), BF16),
        in_specs=[hbm] * 9,
        out_specs=pl.BlockSpec(memory_space=pltpu.VMEM),
        scratch_shapes=[
            pltpu.SMEM((2,), jnp.int32),
            vmem(n, width),
            vmem(router.shape[1], width),
            vmem(TOP, n, dtype=jnp.int32),
            vmem(*w_qkv.shape),
            vmem(*w_out.shape),
            vmem(*w_gate.shape),
            vmem(*w_up.shape),
            vmem(*w_down.shape),
            vmem(n, width),
            vmem(4 * WIN * REACH, width // 2),
            vmem(4 * WIN * REACH, width // 2),
            vmem(2 * REACH * (n // WIN), width),
            vmem(WIN * WIN, width),
            vmem(2 * WIN * WIN, width),
            vmem(n, width),
            vmem(keys, width),
            vmem(keys, width),
            vmem(3 * total, 2 * n),
            vmem(12 * n, total),
            vmem(n, 128, dtype=F32),
            vmem(n, width),
            vmem(n, width, dtype=F32),
            vmem(total, WIDE),
            vmem(total, WIDE),
            vmem(total, WIDE),
            vmem(total, WIDE),
            dma((9,)),
            dma((2,)), dma((2,)), dma((2,)), dma((2,)), dma((2,)), dma((2,)),
            dma((n_lat * n_lon,)), dma((n_lat * n_lon,)),
            dma((n_lat * n_lon,)), dma((n_lat * n_lon,)),
        ],
        compiler_params=pltpu.CompilerParams(
            collective_id=1, has_side_effects=True, vmem_limit_bytes=56 * 2**20
        ),
    )(shifts, tok, router.T, ids.T, w_qkv, w_out, w_gate, w_up, w_down)


def body(tokens, shifts, w_qkv, w_out, router, expert_ids, w_gate, w_up, w_down):
    n_lat = lax.axis_size("lat")
    n_lon = lax.axis_size("lon")
    devices = n_lat * n_lon
    rows, cols, width = tokens.shape
    ids = expert_ids.reshape(-1, TOP)
    tok = tokens.reshape(-1, width)
    if (n_lat, n_lon) == (4, 8) and w_gate.shape[1] == 2 * FF:
        out = layer_block(
            n_lat, n_lon, shifts, tok, router, ids, w_qkv, w_out, w_gate, w_up, w_down
        )
        return out.reshape(rows, cols, width)
    mixed, normed2 = front_block(n_lat, n_lon, shifts, tok, w_qkv, w_out)
    return general(mixed, normed2, router, ids, w_gate, w_up, w_down, devices, rows, cols)


def general(mixed, normed2, router, ids, w_gate, w_up, w_down, devices, rows, cols):
    width = mixed.shape[1]
    logits = jnp.dot(normed2, router, preferred_element_type=jnp.float32)
    experts = router.shape[1]
    expert_iota = jnp.arange(experts, dtype=jnp.int32)
    picks = ids[:, :, None] == expert_iota[None, None, :]
    chosen = jnp.sum(jnp.where(picks, logits[:, None, :], 0.0), axis=-1)
    sig = jax.nn.sigmoid(chosen)
    gates = sig / jnp.sum(sig, axis=1, keepdims=True)
    flat = ids.reshape(-1)
    order = jnp.arange(flat.shape[0], dtype=jnp.int32)
    earlier = (flat[:, None] == flat[None, :]) & (order[None, :] < order[:, None])
    rank = jnp.sum(earlier.astype(jnp.int32), axis=1)
    share = w_gate.shape[1]
    piece = min(FF, share)
    repl = FF // piece
    group = share // piece
    most = MOST
    cap = group * most
    token_of = jnp.arange(flat.shape[0], dtype=jnp.int32) // TOP
    slot = flat % group * most + rank
    slot_index = jnp.stack(
        [(flat // group * repl + copy) * cap + slot for copy in range(repl)], axis=0
    )
    routed = normed2[token_of]
    send = (
        jnp.zeros((devices * cap, width), jnp.bfloat16)
        .at[slot_index.reshape(-1)]
        .set(jnp.tile(routed, (repl, 1)))
    )
    send = send.reshape(devices, group, most, width)
    received = lax.all_to_all(send, ("lat", "lon"), split_axis=0, concat_axis=0, tiled=True)
    results = []
    for local in range(group):
        block = received[:, local].reshape(-1, width)
        gate = jnp.dot(
            block,
            w_gate[:, local * piece : (local + 1) * piece],
            preferred_element_type=jnp.float32,
        )
        upper = jnp.dot(
            block, w_up[:, local * piece : (local + 1) * piece], preferred_element_type=jnp.float32
        )
        hidden = (jax.nn.silu(gate) * upper).astype(jnp.bfloat16)
        part = jnp.dot(
            hidden, w_down[local * piece : (local + 1) * piece], preferred_element_type=jnp.float32
        ).astype(jnp.bfloat16)
        results.append(part.reshape(received.shape[0], received.shape[2], width))
    back = lax.all_to_all(
        jnp.stack(results, axis=1), ("lat", "lon"), split_axis=0, concat_axis=0, tiled=True
    )
    back_flat = back.reshape(devices * cap, width)
    combined = jnp.zeros((flat.shape[0], width), jnp.float32)
    for copy in range(repl):
        combined = combined + back_flat[slot_index[copy]].astype(jnp.float32)
    combined = combined.reshape(-1, TOP, width)
    moe = jnp.sum(gates[:, :, None] * combined, axis=1)
    layer_out = (mixed.astype(jnp.float32) + moe).astype(jnp.bfloat16)
    return layer_out.reshape(rows, cols, width)


def solution(mesh):
    placed = (
        P("lat", "lon", None),
        P(),
        P(),
        P(),
        P(),
        P("lat", "lon", None, None),
        P(None, ("lat", "lon")),
        P(None, ("lat", "lon")),
        P(("lat", "lon"), None),
    )
    return jax.shard_map(
        body, mesh=mesh, in_specs=placed, out_specs=P("lat", "lon", None), check_vma=False
    )
```

```python
import functools

import jax
import jax.numpy as jnp
import numpy as np
from jax import lax
from jax.experimental import pallas as pl
from jax.experimental.pallas import tpu as pltpu
from jax.sharding import PartitionSpec as P

HEAD = 64
FF = 1024
TOP = 2
WIN = 8
MOST = 6
UNIT = 16
MAIN = 12
WIDE = 768
TAIL = 256
F32 = jnp.float32
BF16 = jnp.bfloat16


def rms_rows(x):
    xf = x.astype(jnp.float32)
    return xf * lax.rsqrt(jnp.mean(xf * xf, axis=-1, keepdims=True) + 1e-05)


def mm(a, b):
    return jnp.dot(a, b, preferred_element_type=F32)


def hit(cond):
    return jnp.where(cond, 1.0, 0.0)


def head_norm(x, ones):
    xf = x.astype(F32)
    sq = xf * xf
    hi = sq.astype(BF16)
    lo = (sq - hi.astype(F32)).astype(BF16)
    mean = (mm(hi, ones) + mm(lo, ones)) * (1.0 / HEAD)
    return xf * lax.rsqrt(mean + 1e-05)


REACH = WIN - 1


def front_kernel(
    n_lat, n_lon, shifts_ref, tok_ref, wqkv_hbm, wo_hbm, mixed_ref, send_ref,
    tall, tosend, side, wqkv, wo, qbuf, kbuf, vbuf, w_sem, vs, vr, hs, hr
):
    lat, lon = lax.axis_index("lat"), lax.axis_index("lon")
    loads = [
        pltpu.make_async_copy(wqkv_hbm, wqkv, w_sem.at[0]),
        pltpu.make_async_copy(wo_hbm, wo, w_sem.at[1]),
    ]
    for load in loads:
        load.start()
    n, width = tok_ref.shape
    cols = n // WIN
    left = (lat, lax.rem(lon + n_lon - 1, n_lon))
    right = (lat, lax.rem(lon + 1, n_lon))
    up, down = (lat - 1, lon), (lat + 1, lon)
    has_up, has_down = lat > 0, lat < n_lat - 1
    mesh_id = pl.DeviceIdType.MESH
    barrier = pltpu.get_barrier_semaphore()
    around = (
        left, right, (lax.rem(lat + n_lat - 1, n_lat), lon), (lax.rem(lat + 1, n_lat), lon)
    )
    for other in around:
        pl.semaphore_signal(barrier, inc=1, device_id=other, device_id_type=mesh_id)

    tall[n : 2 * n, :] = rms_rows(tok_ref[...]).astype(BF16)
    tall[0:cols, :] = jnp.zeros((cols, width), BF16)
    tall[3 * n - cols : 3 * n, :] = jnp.zeros((cols, width), BF16)
    edge = REACH * cols

    @pl.when(lat == 0)
    def _():
        tall[cols:n, :] = jnp.zeros((edge, width), BF16)

    @pl.when(lat == n_lat - 1)
    def _():
        tall[2 * n : 2 * n + edge, :] = jnp.zeros((edge, width), BF16)

    pl.semaphore_wait(barrier, len(around))

    def remote(src, dst, ssem, rsem, to):
        return pltpu.make_async_remote_copy(
            src_ref=src, dst_ref=dst, send_sem=ssem, recv_sem=rsem,
            device_id=to, device_id_type=mesh_id,
        )

    above, below = tall.at[pl.ds(cols, edge)], tall.at[pl.ds(2 * n, edge)]
    go_down = remote(tall.at[pl.ds(n + cols, edge)], above, vs.at[0], vr.at[0], down)
    go_up = remote(tall.at[pl.ds(n, edge)], below, vs.at[1], vr.at[1], up)

    @pl.when(has_down)
    def _():
        go_down.start()

    @pl.when(has_up)
    def _():
        go_up.start()

    s_lat, s_lon = shifts_ref[0], shifts_ref[1]
    sides = 2 * WIN * REACH
    out_row = lax.broadcasted_iota(jnp.int32, (2 * sides, 1), 0)
    local = jnp.where(out_row >= sides, out_row - sides, out_row)
    at = local // REACH * cols + local % REACH + jnp.where(out_row >= sides, cols - REACH, 0)
    start = (WIN - s_lat) * cols
    pick = hit(lax.broadcasted_iota(jnp.int32, (2 * sides, 3 * n), 1) == at + start).astype(BF16)

    @pl.when(has_up)
    def _():
        go_down.wait_recv()

    @pl.when(has_down)
    def _():
        go_up.wait_recv()

    everything = tall[...]
    tosend[...] = mm(pick, everything).astype(BF16)
    go_left = remote(
        tosend.at[pl.ds(0, sides)], side.at[pl.ds(sides, sides)], hs.at[0], hr.at[0], left
    )
    go_right = remote(
        tosend.at[pl.ds(sides, sides)], side.at[pl.ds(0, sides)], hs.at[1], hr.at[1], right
    )
    go_left.start()
    go_right.start()
    there = lax.broadcasted_iota(jnp.int32, (2 * n, 3 * n), 0) + start
    shift = hit(lax.broadcasted_iota(jnp.int32, (2 * n, 3 * n), 1) == there).astype(BF16)
    keys = mm(shift, everything).astype(BF16)

    steps = 4
    group = width // steps
    heads = group // HEAD
    ra = lax.broadcasted_iota(jnp.int32, (group, group), 0) // HEAD
    rb = lax.broadcasted_iota(jnp.int32, (group, group), 1) // HEAD
    ones = hit(ra == rb).astype(BF16)
    own = tall[n : 2 * n, :]
    loads[0].wait()

    def project(cells, first, count):
        for j in range(steps):
            lanes = slice(j * group, (j + 1) * group)
            k = mm(cells, wqkv[:, width + j * group : width + (j + 1) * group]).astype(BF16)
            kbuf[first : first + count, lanes] = head_norm(k, ones).astype(BF16)
            v = mm(cells, wqkv[:, 2 * width + j * group : 2 * width + (j + 1) * group])
            vbuf[first : first + count, lanes] = v.astype(BF16)

    for j in range(steps):
        lanes = slice(j * group, (j + 1) * group)
        q = mm(own, wqkv[:, lanes]).astype(BF16)
        qbuf[:, lanes] = (head_norm(q, ones) * (1.0 / 8.0)).astype(BF16)
    project(keys, 0, 2 * n)

    total_keys = 2 * n + 2 * sides
    i = lax.broadcasted_iota(jnp.int32, (1, total_keys), 1)
    m = jnp.where(i < 2 * n + sides, i - 2 * n, i - 2 * n - sides)
    inner = i < 2 * n
    r_of = jnp.where(inner, i // cols, m // REACH)
    c_of = jnp.where(
        inner, i % cols, m % REACH + jnp.where(i < 2 * n + sides, -REACH, cols)
    )
    at_row = lat * WIN - s_lat + r_of
    valid = (at_row >= 0) & (at_row < WIN * n_lat)
    keyid = jnp.where(valid, (r_of // WIN) * 4 + (c_of + s_lon + WIN) // WIN, -1)
    qi = lax.broadcasted_iota(jnp.int32, (n, 1), 0)
    qid = (qi // cols + s_lat) // WIN * 4 + (qi % cols + s_lon + WIN) // WIN
    same = qid == keyid
    lane = lax.broadcasted_iota(jnp.int32, (n, group), 1) // HEAD

    go_left.wait_recv()
    go_right.wait_recv()
    project(side[...], 2 * n, 2 * sides)
    loads[1].wait()
    acc = tok_ref[...].astype(F32)
    for j in range(steps):
        lanes = slice(j * group, (j + 1) * group)
        qn = qbuf[:, lanes]
        stacked = jnp.concatenate(
            [jnp.where(lane == h, qn, jnp.zeros_like(qn)) for h in range(heads)], axis=0
        )
        scores = lax.dot_general(
            stacked, kbuf[:, lanes], (((1,), (1,)), ((), ())), preferred_element_type=F32
        )
        weights = []
        for h in range(heads):
            e = jnp.where(same, jnp.exp(scores[h * n : (h + 1) * n]), 0.0)
            total = jnp.sum(e, axis=1, keepdims=True)
            weights.append((e * (1.0 / total)).astype(BF16))
        mixedv = mm(jnp.concatenate(weights, axis=0), vbuf[:, lanes])
        att = jnp.zeros((n, group), F32)
        for h in range(heads):
            att = jnp.where(lane == h, mixedv[h * n : (h + 1) * n], att)
        acc = acc + mm(att.astype(BF16), wo[lanes, :])

    mixed = acc.astype(BF16)
    mixed_ref[...] = mixed
    normed2 = rms_rows(mixed).astype(BF16)
    send_ref[...] = normed2

    go_left.wait_send()
    go_right.wait_send()

    @pl.when(has_down)
    def _():
        go_down.wait_send()

    @pl.when(has_up)
    def _():
        go_up.wait_send()


def front_block(n_lat, n_lon, shifts, tok, w_qkv, w_out):
    n, width = tok.shape
    sides = 2 * 2 * WIN * REACH
    vm = pl.BlockSpec(memory_space=pltpu.VMEM)
    hbm = pl.BlockSpec(memory_space=pl.ANY)
    dma = pltpu.SemaphoreType.DMA
    keys = 2 * n + sides
    return pl.pallas_call(
        functools.partial(front_kernel, n_lat, n_lon),
        in_specs=[pl.BlockSpec(memory_space=pltpu.SMEM), vm, hbm, hbm],
        out_specs=[vm, vm],
        out_shape=[jax.ShapeDtypeStruct((n, width), BF16)] * 2,
        scratch_shapes=[
            pltpu.VMEM((3 * n, width), BF16),
            pltpu.VMEM((sides, width), BF16),
            pltpu.VMEM((sides, width), BF16),
            pltpu.VMEM(w_qkv.shape, BF16),
            pltpu.VMEM(w_out.shape, BF16),
            pltpu.VMEM((n, width), BF16),
            pltpu.VMEM((keys, width), BF16),
            pltpu.VMEM((keys, width), BF16),
            dma((2,)), dma((2,)), dma((2,)), dma((2,)), dma((2,)),
        ],
        compiler_params=pltpu.CompilerParams(
            collective_id=2, has_side_effects=True, vmem_limit_bytes=40 * 2**20
        ),
    )(shifts, tok, w_qkv, w_out)


def iota(shape, axis):
    return lax.broadcasted_iota(jnp.int32, shape, axis)


def onehot(shape, target):
    return hit(iota(shape, 1) == target).astype(BF16)


def flip(z, g):
    return 2 * ((z // 2 + g // 2) % 2) + (z + g) % 2


def layer_kernel(
    n_lat, n_lon, shifts_hbm, tok_hbm, router_hbm, ids_hbm, wqkv_hbm, wo_hbm, wg_hbm, wu_hbm,
    wd_hbm, out_ref, shifts, tok, router, ids, wqkv, wo, wg, wu, wd, own, sideout, sidein, vertin,
    side, cornin, qbuf, kbuf, vbuf, place, comb, info, normed2, acc, send, got, results, back,
    far_ids, far_info, far, far_acc, share, shared, w_sem, vs, vr, hs, hr, cs, cr, ms, mr, s1, r1, s2, r2
):
    lat, lon = lax.axis_index("lat"), lax.axis_index("lon")
    z, x = lon // 2, lon % 2
    plane = 2 * n_lat
    slab = plane * UNIT
    here = lat * 2 + x
    inner = (z + 1) // 2 % 2 == 1
    mirror = (lat, (3 - z) * 2 + x)
    loads = [
        pltpu.make_async_copy(src, dst, w_sem.at[i])
        for i, (src, dst) in enumerate((
            (tok_hbm, tok), (shifts_hbm, shifts), (ids_hbm, ids), (wqkv_hbm, wqkv),
            (wo_hbm, wo), (router_hbm, router), (wg_hbm, wg), (wu_hbm, wu), (wd_hbm, wd),
        ))
    ]
    for load in loads[:6]:
        load.start()
    n, width = tok.shape
    cols = n // WIN
    mesh_id = pl.DeviceIdType.MESH
    left = (lat, lax.rem(lon + n_lon - 1, n_lon))
    right = (lat, lax.rem(lon + 1, n_lon))
    up, down = (lat - 1, lon), (lat + 1, lon)
    has_up, has_down = lat > 0, lat < n_lat - 1

    barrier = pltpu.get_barrier_semaphore()
    devices = n_lat * n_lon

    def greet(k, c):
        other = (lax.rem(lat + k // n_lon, n_lat), lax.rem(lon + k % n_lon, n_lon))
        pl.semaphore_signal(barrier, inc=1, device_id=other, device_id_type=mesh_id)
        return c

    lax.fori_loop(1, devices, greet, 0)

    edge = REACH * cols
    nook = WIN * WIN

    @pl.when(lat == 0)
    def _():
        vertin[0:edge, :] = jnp.zeros((edge, width), BF16)
        cornin[0:nook, :] = jnp.zeros((nook, width), BF16)

    @pl.when(lat == n_lat - 1)
    def _():
        vertin[edge : 2 * edge, :] = jnp.zeros((edge, width), BF16)
        cornin[nook : 2 * nook, :] = jnp.zeros((nook, width), BF16)

    half = WIN * REACH
    lanes2 = width // 2
    r = iota((4 * half, 1), 0)
    within = r % half
    cell = within // REACH * cols + within % REACH + jnp.where(r >= 2 * half, cols - REACH, 0)
    second = r // half % 2 == 1
    pick0 = onehot((4 * half, n), jnp.where(second, -1, cell))
    pick1 = onehot((4 * half, n), jnp.where(second, cell, -1))
    loads[0].wait()
    own[...] = rms_rows(tok[...]).astype(BF16)
    sideout[...] = (
        mm(pick0, own[:, 0:lanes2]) + mm(pick1, own[:, lanes2:width])
    ).astype(BF16)
    pl.semaphore_wait(barrier, devices - 1)

    def remote(src, dst, ssem, rsem, to):
        return pltpu.make_async_remote_copy(
            src_ref=src, dst_ref=dst, send_sem=ssem, recv_sem=rsem,
            device_id=to, device_id_type=mesh_id,
        )

    first, last = pl.ds(0, 2 * half), pl.ds(2 * half, 2 * half)
    go_left = remote(sideout.at[first], sidein.at[last], hs.at[0], hr.at[0], left)
    go_right = remote(sideout.at[last], sidein.at[first], hs.at[1], hr.at[1], right)
    go_left.start()
    go_right.start()
    go_down = remote(
        own.at[pl.ds(n - edge, edge)], vertin.at[pl.ds(0, edge)], vs.at[0], vr.at[0], down
    )
    go_up = remote(own.at[pl.ds(0, edge)], vertin.at[pl.ds(edge, edge)], vs.at[1], vr.at[1], up)

    @pl.when(has_down)
    def _():
        go_down.start()

    @pl.when(has_up)
    def _():
        go_up.start()

    tell = remote(ids, far_ids, ms.at[0], mr.at[0], mirror)
    lend = remote(normed2, far, ms.at[1], mr.at[1], mirror)
    give = remote(share, shared, ms.at[2], mr.at[2], mirror)
    loads[2].wait()

    @pl.when(inner)
    def _():
        tell.start()

    @pl.when(~inner)
    def _():
        far_ids[...] = ids[...]

    steps = 4
    group = width // steps
    heads = group // HEAD
    ones = hit(iota((group, group), 0) // HEAD == iota((group, group), 1) // HEAD).astype(BF16)
    loads[3].wait()
    for load in loads[6:]:
        load.start()

    def project(cells, at):
        for j in range(steps):
            lanes = slice(j * group, (j + 1) * group)
            k = mm(cells, wqkv[:, width + j * group : width + (j + 1) * group]).astype(BF16)
            kbuf[at : at + cells.shape[0], lanes] = head_norm(k, ones).astype(BF16)
            v = mm(cells, wqkv[:, 2 * width + j * group : 2 * width + (j + 1) * group])
            vbuf[at : at + cells.shape[0], lanes] = v.astype(BF16)

    for j in range(steps):
        lanes = slice(j * group, (j + 1) * group)
        q = mm(own[...], wqkv[:, lanes]).astype(BF16)
        qbuf[:, lanes] = (head_norm(q, ones) * (1.0 / 8.0)).astype(BF16)
    project(own[...], 0)

    loads[1].wait()
    s_lat, s_lon = shifts[0], shifts[1]
    w = iota((n, 1), 0)
    v_at = w // cols
    vert_at = jnp.where(v_at < s_lat, REACH - s_lat + v_at, REACH + v_at - s_lat)
    vert_pick = onehot((n, 2 * edge), vert_at * cols + w % cols)

    @pl.when(has_up)
    def _():
        go_down.wait_recv()

    @pl.when(has_down)
    def _():
        go_up.wait_recv()

    project(mm(vert_pick, vertin[...]).astype(BF16), n)

    routes(n_lon, z, ids, info, place, 0)

    @pl.when(inner)
    def _():
        tell.wait_recv()

    far_z = jnp.where(inner, 3 - z, z)
    routes(n_lon, far_z, far_ids, far_info, place, 2 * slab)

    w = iota((nook, 1), 0)
    major, minor = w // WIN, w % WIN
    side_at = major * REACH + jnp.where(
        minor < s_lon, REACH - s_lon + minor, 2 * half + minor - s_lon
    )
    side0 = onehot((nook, 4 * half), side_at)
    side1 = onehot((nook, 4 * half), side_at + half)
    corn_at = jnp.where(major < s_lat, WIN - s_lat + major, WIN + major - s_lat)
    corn_pick = onehot((nook, 2 * nook), corn_at * WIN + minor)
    go_left.wait_recv()
    go_right.wait_recv()
    side[:, 0:lanes2] = mm(side0, sidein[...]).astype(BF16)
    side[:, lanes2:width] = mm(side1, sidein[...]).astype(BF16)
    corn_down = remote(side, cornin.at[pl.ds(0, nook)], cs.at[0], cr.at[0], down)
    corn_up = remote(side, cornin.at[pl.ds(nook, nook)], cs.at[1], cr.at[1], up)

    @pl.when(has_down)
    def _():
        corn_down.start()

    @pl.when(has_up)
    def _():
        corn_up.start()

    project(side[...], 2 * n)

    total_keys = 2 * n + 2 * nook
    i = iota((1, total_keys), 1)
    in_own, in_vert, in_side = i < n, i < 2 * n, i < 2 * n + nook
    m = i - jnp.where(in_side, 2 * n, 2 * n + nook)
    row = jnp.where(in_vert, jnp.where(in_own, i, i - n) // cols, m // WIN)
    col = jnp.where(in_vert, i % cols, m % WIN)
    inside = in_own | (in_side & ~in_vert)
    key_row = jnp.where(inside, (row + s_lat) // WIN, jnp.where(row < s_lat, 0, 1))
    key_col = jnp.where(in_vert, (col + s_lon) // WIN, jnp.where(col < s_lon, 0, 2))
    gone = ~inside & (((row < s_lat) & (lat == 0)) | ((row >= s_lat) & (lat == n_lat - 1)))
    keyid = jnp.where(gone, -1, key_row * 4 + key_col)
    w = iota((n, 1), 0)
    same = (w // cols + s_lat) // WIN * 4 + (w % cols + s_lon) // WIN == keyid
    lane = iota((n, group), 1) // HEAD

    @pl.when(has_up)
    def _():
        corn_down.wait_recv()

    @pl.when(has_down)
    def _():
        corn_up.wait_recv()

    project(mm(corn_pick, cornin[...]).astype(BF16), 2 * n + nook)

    loads[4].wait()
    total = tok[...].astype(F32)
    for j in range(steps):
        lanes = slice(j * group, (j + 1) * group)
        qn = qbuf[:, lanes]
        stacked = jnp.concatenate(
            [jnp.where(lane == h, qn, jnp.zeros_like(qn)) for h in range(heads)], axis=0
        )
        scores = lax.dot_general(
            stacked, kbuf[:, lanes], (((1,), (1,)), ((), ())), preferred_element_type=F32
        )
        weights = []
        for h in range(heads):
            e = jnp.where(same, jnp.exp(scores[h * n : (h + 1) * n]), 0.0)
            weights.append((e * (1.0 / jnp.sum(e, axis=1, keepdims=True))).astype(BF16))
        mixedv = mm(jnp.concatenate(weights, axis=0), vbuf[:, lanes])
        att = jnp.zeros((n, group), F32)
        for h in range(heads):
            att = jnp.where(lane == h, mixedv[h * n : (h + 1) * n], att)
        total = total + mm(att.astype(BF16), wo[lanes, :])

    mixed = total.astype(BF16)
    acc[...] = mixed.astype(F32)
    normed2[...] = rms_rows(mixed).astype(BF16)

    @pl.when(inner)
    def _():
        lend.start()

    @pl.when(~inner)
    def _():
        far[...] = normed2[...]

    def pack(cells, first):
        end = cells[:, WIDE:width]
        for t in range(3):
            lanes = slice(t * TAIL, (t + 1) * TAIL)
            both = jnp.concatenate([cells[:, lanes], end], axis=0)
            at = t * 4 * slab + first
            send[first : first + 2 * slab, lanes] = mm(place[at : at + 2 * slab, :], both).astype(BF16)

    def rows(g, j):
        return pl.ds(pl.multiple_of(g * slab + j * UNIT, UNIT), UNIT)

    def forth(g):
        return flip(z, jnp.where(inner & (g >= 2), 3 - g, g))

    def home(g):
        return flip(z, jnp.where(inner, jnp.where(g == 3, 0, g), jnp.where(g == 2, 1, g)))

    def begin(g):
        return jnp.where((g == 0) | (inner & (g == 3)), 1, 0)

    out1, out2 = (send, got, s1, r1, forth), (results, back, s2, r2, home)

    def copy(src, dst, ssem, rsem, to_plane, g, k):
        to_lat, to_x = (lat + k // 2) % n_lat, (x + k) % 2
        return remote(
            src.at[rows(g, to_lat * 2 + to_x)], dst.at[rows(g, here)],
            ssem.at[g * plane + k], rsem.at[g * plane + k], (to_lat, to_plane(g) * 2 + to_x),
        )

    def arrival(src, dst, ssem, rsem, to_plane, g, k):
        of_lat, of_x = (lat + n_lat - k // 2) % n_lat, (x + k) % 2
        return remote(
            src.at[rows(g, here)], dst.at[rows(g, of_lat * 2 + of_x)],
            ssem.at[g * plane + k], rsem.at[g * plane + k], (of_lat, to_plane(g) * 2 + of_x),
        )

    def launch(out, g):
        def go(k, c):
            copy(*out, g, k).start()
            return c

        lax.fori_loop(begin(g), plane, go, 0)

    def land(out, g):
        def go(k, c):
            arrival(*out, g, k).wait_recv()
            return c

        lax.fori_loop(begin(g), plane, go, 0)

    def drain(out, g):
        def go(k, c):
            copy(*out, g, k).wait_send()
            return c

        lax.fori_loop(begin(g), plane, go, 0)

    pack(normed2, 0)
    launch(out1, 1)
    launch(out1, 0)
    got[rows(0, here), :] = send[rows(0, here), :]
    loads[5].wait()
    gates(normed2, router, info, comb, 0)

    @pl.when(inner)
    def _():
        lend.wait_recv()

    pack(far, 2 * slab)
    launch(out1, 3)
    launch(out1, 2)

    @pl.when(inner)
    def _():
        got[rows(3, here), :] = send[rows(3, here), :]

    gates(far, router, far_info, comb, 2 * slab)

    half_rows = plane * MOST
    count = 2 * half_rows
    r = iota((count, 1), 0)
    slot = r // half_rows * MOST + r % MOST
    base = r % half_rows // MOST * UNIT
    pick = onehot((count, slab), base + slot)
    tails = [
        onehot((count, slab), jnp.where(slot % 3 == t, base + MAIN + slot // 3, -1))
        for t in range(3)
    ]
    r = iota((1, count), 1)
    slot = r // half_rows * MOST + r % MOST
    base = r % half_rows // MOST * UNIT
    target = iota((slab, count), 0)
    put = hit(target == base + slot).astype(BF16)
    put_tails = [
        hit(target == jnp.where(slot % 3 == t, base + MAIN + slot // 3, -1)).astype(BF16)
        for t in range(3)
    ]
    for load in loads[6:]:
        load.wait()

    def experts(i, c):
        g = i + 1 - 2 * (i % 2)
        land(out1, g)
        at = pl.ds(pl.multiple_of(g * slab, slab), slab)
        wide = mm(pick, got[at, :]).astype(BF16)
        end = mm(tails[0], got[at, 0:TAIL])
        for t in range(1, 3):
            end = end + mm(tails[t], got[at, t * TAIL : (t + 1) * TAIL])
        cells = jnp.concatenate([wide, end.astype(BF16)], axis=1)
        parts = []
        for e in range(2):
            xe = cells[e * half_rows : (e + 1) * half_rows]
            gate = mm(xe, wg[:, e * FF : (e + 1) * FF])
            upper = mm(xe, wu[:, e * FF : (e + 1) * FF])
            hidden = (jax.nn.silu(gate) * upper).astype(BF16)
            parts.append(mm(hidden, wd[e * FF : (e + 1) * FF, :]).astype(BF16))
        part = jnp.concatenate(parts, axis=0)
        for t in range(3):
            lanes = slice(t * TAIL, (t + 1) * TAIL)
            results[at, lanes] = (
                mm(put, part[:, lanes]) + mm(put_tails[t], part[:, WIDE:width])
            ).astype(BF16)
        launch(out2, g)
        return c

    lax.fori_loop(0, 4, experts, 0)
    back[rows(0, here), :] = results[rows(0, here), :]


    def gather(g, into):
        land(out2, g)
        at = slice(g * slab, (g + 1) * slab)
        for t in range(3):
            lanes = slice(t * TAIL, (t + 1) * TAIL)
            s = mm(comb[t * 4 * n : (t + 1) * 4 * n, at], back[at, lanes])
            into[:, lanes] += s[0:n] + s[n : 2 * n]
            into[:, WIDE:width] += s[2 * n : 3 * n] + s[3 * n : 4 * n]

    @pl.when(inner)
    def _():
        back[rows(3, here), :] = results[rows(3, here), :]
        far_acc[...] = jnp.zeros_like(far_acc)
        gather(3, far_acc)
        gather(2, far_acc)
        share[...] = far_acc[...].astype(BF16)
        give.start()

    gather(1, acc)
    gather(0, acc)

    @pl.when(~inner)
    def _():
        gather(3, acc)
        gather(2, acc)
        out_ref[...] = acc[...].astype(BF16)

    @pl.when(inner)
    def _():
        give.wait_recv()
        out_ref[...] = (acc[...] + shared[...].astype(F32)).astype(BF16)
        tell.wait_send()
        lend.wait_send()
        give.wait_send()

    go_left.wait_send()
    go_right.wait_send()

    @pl.when(has_down)
    def _():
        go_down.wait_send()
        corn_down.wait_send()

    @pl.when(has_up)
    def _():
        go_up.wait_send()
        corn_up.wait_send()

    for g in range(4):
        drain(out1, g)
        drain(out2, g)


def routes(n_lon, z, ids, info, place, first):
    n = ids.shape[1]
    r0, r1 = ids[0:1, :], ids[1:2, :]
    ia, ib = iota((n, n), 0), iota((n, n), 1)

    def column(row):
        return jnp.sum(jnp.where(ia == ib, row.astype(F32), 0.0), axis=1, keepdims=True)

    c0, c1 = column(r0).astype(jnp.int32), column(r1).astype(jnp.int32)
    rank0c = jnp.sum(hit((c0 == r0) & (ib < ia)), axis=1, keepdims=True)
    rank1c = jnp.sum(hit(c1 == r0) + hit((c1 == r1) & (ib < ia)), axis=1, keepdims=True)
    rank0r = jnp.sum(hit((c0 == r0) & (ia < ib)), axis=0, keepdims=True)
    rank1r = jnp.sum(hit(c0 == r1) + hit((c1 == r1) & (ia < ib)), axis=0, keepdims=True)

    def places(e, rank):
        slot = e % 2 * MOST + rank.astype(jnp.int32)
        device = e // 2
        at_lat, at_lon = device // n_lon, device % n_lon
        base = (flip(at_lon // 2, z) * (place.shape[0] // 12 // UNIT) + at_lat * 2 + at_lon % 2) * UNIT
        return base + slot, base + MAIN + slot // 3, slot % 3

    m0, t0, q0 = places(c0, rank0c)
    m1, t1, q1 = places(c1, rank1c)
    col = iota(info.shape, 1)
    table = jnp.zeros(info.shape, F32)
    for i, v in enumerate((m0, t0, q0, m1, t1, q1, c0, c1)):
        table = jnp.where(col == i, v.astype(F32), table)
    info[...] = table
    m0, t0, q0 = places(r0, rank0r)
    m1, t1, q1 = places(r1, rank1r)
    total = place.shape[0] // 3
    count = total // 2
    row = iota((count, n), 0) + first
    main = (hit(row == m0) + hit(row == m1)).astype(BF16)
    for t in range(3):
        rows = slice(t * total + first, t * total + first + count)
        place[rows, 0:n] = main
        place[rows, n : 2 * n] = (
            hit((row == t0) & (q0 == t)) + hit((row == t1) & (q1 == t))
        ).astype(BF16)


def gates(cells, router, info, comb, begin):
    logits = lax.dot_general(
        cells[...], router[...], (((1,), (1,)), ((), ())), preferred_element_type=F32
    )
    n = logits.shape[0]
    eid = iota(logits.shape, 1).astype(F32)
    m0, t0, q0, m1, t1, q1, c0, c1 = (info[:, i : i + 1] for i in range(8))
    s0 = jax.nn.sigmoid(jnp.sum(jnp.where(eid == c0, logits, 0.0), axis=1, keepdims=True))
    s1 = jax.nn.sigmoid(jnp.sum(jnp.where(eid == c1, logits, 0.0), axis=1, keepdims=True))
    g0 = s0 / (s0 + s1)
    g1 = s1 / (s0 + s1)
    count = comb.shape[1] // 2
    at = (iota((n, count), 1) + begin).astype(F32)

    def keep(first, a):
        hi = a.astype(BF16)
        comb[first : first + n, begin : begin + count] = hi
        comb[first + n : first + 2 * n, begin : begin + count] = (a - hi.astype(F32)).astype(BF16)

    main = jnp.where(at == m0, g0, 0.0) + jnp.where(at == m1, g1, 0.0)
    for t in range(3):
        keep(t * 4 * n, main)
        keep(
            t * 4 * n + 2 * n,
            jnp.where((at == t0) & (q0 == t), g0, 0.0) + jnp.where((at == t1) & (q1 == t), g1, 0.0),
        )


def layer_block(n_lat, n_lon, shifts, tok, router, ids, w_qkv, w_out, w_gate, w_up, w_down):
    n, width = tok.shape
    total = n_lat * n_lon * UNIT
    keys = 2 * n + 2 * WIN * WIN
    hbm = pl.BlockSpec(memory_space=pl.ANY)
    dma = pltpu.SemaphoreType.DMA

    def vmem(*shape, dtype=BF16):
        return pltpu.VMEM(shape, dtype)

    return pl.pallas_call(
        functools.partial(layer_kernel, n_lat, n_lon),
        out_shape=jax.ShapeDtypeStruct((n, width), BF16),
        in_specs=[hbm] * 9,
        out_specs=pl.BlockSpec(memory_space=pltpu.VMEM),
        scratch_shapes=[
            pltpu.SMEM((2,), jnp.int32),
            vmem(n, width),
            vmem(router.shape[1], width),
            vmem(TOP, n, dtype=jnp.int32),
            vmem(*w_qkv.shape),
            vmem(*w_out.shape),
            vmem(*w_gate.shape),
            vmem(*w_up.shape),
            vmem(*w_down.shape),
            vmem(n, width),
            vmem(4 * WIN * REACH, width // 2),
            vmem(4 * WIN * REACH, width // 2),
            vmem(2 * REACH * (n // WIN), width),
            vmem(WIN * WIN, width),
            vmem(2 * WIN * WIN, width),
            vmem(n, width),
            vmem(keys, width),
            vmem(keys, width),
            vmem(3 * total, 2 * n),
            vmem(12 * n, total),
            vmem(n, 128, dtype=F32),
            vmem(n, width),
            vmem(n, width, dtype=F32),
            vmem(total, WIDE),
            vmem(total, WIDE),
            vmem(total, WIDE),
            vmem(total, WIDE),
            vmem(TOP, n, dtype=jnp.int32),
            vmem(n, 128, dtype=F32),
            vmem(n, width),
            vmem(n, width, dtype=F32),
            vmem(n, width),
            vmem(n, width),
            dma((9,)),
            dma((2,)), dma((2,)), dma((2,)), dma((2,)), dma((2,)), dma((2,)),
            dma((3,)), dma((3,)),
            dma((n_lat * n_lon,)), dma((n_lat * n_lon,)),
            dma((n_lat * n_lon,)), dma((n_lat * n_lon,)),
        ],
        compiler_params=pltpu.CompilerParams(
            collective_id=1, has_side_effects=True, vmem_limit_bytes=56 * 2**20
        ),
    )(shifts, tok, router.T, ids.T, w_qkv, w_out, w_gate, w_up, w_down)


def body(tokens, shifts, w_qkv, w_out, router, expert_ids, w_gate, w_up, w_down):
    n_lat = lax.axis_size("lat")
    n_lon = lax.axis_size("lon")
    devices = n_lat * n_lon
    rows, cols, width = tokens.shape
    ids = expert_ids.reshape(-1, TOP)
    tok = tokens.reshape(-1, width)
    if (n_lat, n_lon) == (4, 8) and w_gate.shape[1] == 2 * FF:
        out = layer_block(
            n_lat, n_lon, shifts, tok, router, ids, w_qkv, w_out, w_gate, w_up, w_down
        )
        return out.reshape(rows, cols, width)
    mixed, normed2 = front_block(n_lat, n_lon, shifts, tok, w_qkv, w_out)
    return general(mixed, normed2, router, ids, w_gate, w_up, w_down, devices, rows, cols)


def general(mixed, normed2, router, ids, w_gate, w_up, w_down, devices, rows, cols):
    width = mixed.shape[1]
    logits = jnp.dot(normed2, router, preferred_element_type=jnp.float32)
    experts = router.shape[1]
    expert_iota = jnp.arange(experts, dtype=jnp.int32)
    picks = ids[:, :, None] == expert_iota[None, None, :]
    chosen = jnp.sum(jnp.where(picks, logits[:, None, :], 0.0), axis=-1)
    sig = jax.nn.sigmoid(chosen)
    gates = sig / jnp.sum(sig, axis=1, keepdims=True)
    flat = ids.reshape(-1)
    order = jnp.arange(flat.shape[0], dtype=jnp.int32)
    earlier = (flat[:, None] == flat[None, :]) & (order[None, :] < order[:, None])
    rank = jnp.sum(earlier.astype(jnp.int32), axis=1)
    share = w_gate.shape[1]
    piece = min(FF, share)
    repl = FF // piece
    group = share // piece
    most = MOST
    cap = group * most
    token_of = jnp.arange(flat.shape[0], dtype=jnp.int32) // TOP
    slot = flat % group * most + rank
    slot_index = jnp.stack(
        [(flat // group * repl + copy) * cap + slot for copy in range(repl)], axis=0
    )
    routed = normed2[token_of]
    send = (
        jnp.zeros((devices * cap, width), jnp.bfloat16)
        .at[slot_index.reshape(-1)]
        .set(jnp.tile(routed, (repl, 1)))
    )
    send = send.reshape(devices, group, most, width)
    received = lax.all_to_all(send, ("lat", "lon"), split_axis=0, concat_axis=0, tiled=True)
    results = []
    for local in range(group):
        block = received[:, local].reshape(-1, width)
        gate = jnp.dot(
            block,
            w_gate[:, local * piece : (local + 1) * piece],
            preferred_element_type=jnp.float32,
        )
        upper = jnp.dot(
            block, w_up[:, local * piece : (local + 1) * piece], preferred_element_type=jnp.float32
        )
        hidden = (jax.nn.silu(gate) * upper).astype(jnp.bfloat16)
        part = jnp.dot(
            hidden, w_down[local * piece : (local + 1) * piece], preferred_element_type=jnp.float32
        ).astype(jnp.bfloat16)
        results.append(part.reshape(received.shape[0], received.shape[2], width))
    back = lax.all_to_all(
        jnp.stack(results, axis=1), ("lat", "lon"), split_axis=0, concat_axis=0, tiled=True
    )
    back_flat = back.reshape(devices * cap, width)
    combined = jnp.zeros((flat.shape[0], width), jnp.float32)
    for copy in range(repl):
        combined = combined + back_flat[slot_index[copy]].astype(jnp.float32)
    combined = combined.reshape(-1, TOP, width)
    moe = jnp.sum(gates[:, :, None] * combined, axis=1)
    layer_out = (mixed.astype(jnp.float32) + moe).astype(jnp.bfloat16)
    return layer_out.reshape(rows, cols, width)


def solution(mesh):
    placed = (
        P("lat", "lon", None),
        P(),
        P(),
        P(),
        P(),
        P("lat", "lon", None, None),
        P(None, ("lat", "lon")),
        P(None, ("lat", "lon")),
        P(("lat", "lon"), None),
    )
    return jax.shard_map(
        body, mesh=mesh, in_specs=placed, out_specs=P("lat", "lon", None), check_vma=False
    )
```

```python
import functools

import jax
import jax.numpy as jnp
import numpy as np
from jax import lax
from jax.experimental import pallas as pl
from jax.experimental.pallas import tpu as pltpu
from jax.sharding import PartitionSpec as P

HEAD = 64
FF = 1024
TOP = 2
WIN = 8
MOST = 6
UNIT = 16
MAIN = 12
WIDE = 768
TAIL = 256
F32 = jnp.float32
BF16 = jnp.bfloat16


def rms_rows(x):
    xf = x.astype(jnp.float32)
    return xf * lax.rsqrt(jnp.mean(xf * xf, axis=-1, keepdims=True) + 1e-05)


def mm(a, b):
    return jnp.dot(a, b, preferred_element_type=F32)


def hit(cond):
    return jnp.where(cond, 1.0, 0.0)


def head_norm(x, ones):
    xf = x.astype(F32)
    sq = xf * xf
    hi = sq.astype(BF16)
    lo = (sq - hi.astype(F32)).astype(BF16)
    mean = (mm(hi, ones) + mm(lo, ones)) * (1.0 / HEAD)
    return xf * lax.rsqrt(mean + 1e-05)


REACH = WIN - 1


def front_kernel(
    n_lat, n_lon, shifts_ref, tok_ref, wqkv_hbm, wo_hbm, mixed_ref, send_ref,
    tall, tosend, side, wqkv, wo, qbuf, kbuf, vbuf, w_sem, vs, vr, hs, hr
):
    lat, lon = lax.axis_index("lat"), lax.axis_index("lon")
    loads = [
        pltpu.make_async_copy(wqkv_hbm, wqkv, w_sem.at[0]),
        pltpu.make_async_copy(wo_hbm, wo, w_sem.at[1]),
    ]
    for load in loads:
        load.start()
    n, width = tok_ref.shape
    cols = n // WIN
    left = (lat, lax.rem(lon + n_lon - 1, n_lon))
    right = (lat, lax.rem(lon + 1, n_lon))
    up, down = (lat - 1, lon), (lat + 1, lon)
    has_up, has_down = lat > 0, lat < n_lat - 1
    mesh_id = pl.DeviceIdType.MESH
    barrier = pltpu.get_barrier_semaphore()
    around = (
        left, right, (lax.rem(lat + n_lat - 1, n_lat), lon), (lax.rem(lat + 1, n_lat), lon)
    )
    for other in around:
        pl.semaphore_signal(barrier, inc=1, device_id=other, device_id_type=mesh_id)

    tall[n : 2 * n, :] = rms_rows(tok_ref[...]).astype(BF16)
    tall[0:cols, :] = jnp.zeros((cols, width), BF16)
    tall[3 * n - cols : 3 * n, :] = jnp.zeros((cols, width), BF16)
    edge = REACH * cols

    @pl.when(lat == 0)
    def _():
        tall[cols:n, :] = jnp.zeros((edge, width), BF16)

    @pl.when(lat == n_lat - 1)
    def _():
        tall[2 * n : 2 * n + edge, :] = jnp.zeros((edge, width), BF16)

    pl.semaphore_wait(barrier, len(around))

    def remote(src, dst, ssem, rsem, to):
        return pltpu.make_async_remote_copy(
            src_ref=src, dst_ref=dst, send_sem=ssem, recv_sem=rsem,
            device_id=to, device_id_type=mesh_id,
        )

    above, below = tall.at[pl.ds(cols, edge)], tall.at[pl.ds(2 * n, edge)]
    go_down = remote(tall.at[pl.ds(n + cols, edge)], above, vs.at[0], vr.at[0], down)
    go_up = remote(tall.at[pl.ds(n, edge)], below, vs.at[1], vr.at[1], up)

    @pl.when(has_down)
    def _():
        go_down.start()

    @pl.when(has_up)
    def _():
        go_up.start()

    s_lat, s_lon = shifts_ref[0], shifts_ref[1]
    sides = 2 * WIN * REACH
    out_row = lax.broadcasted_iota(jnp.int32, (2 * sides, 1), 0)
    local = jnp.where(out_row >= sides, out_row - sides, out_row)
    at = local // REACH * cols + local % REACH + jnp.where(out_row >= sides, cols - REACH, 0)
    start = (WIN - s_lat) * cols
    pick = hit(lax.broadcasted_iota(jnp.int32, (2 * sides, 3 * n), 1) == at + start).astype(BF16)

    @pl.when(has_up)
    def _():
        go_down.wait_recv()

    @pl.when(has_down)
    def _():
        go_up.wait_recv()

    everything = tall[...]
    tosend[...] = mm(pick, everything).astype(BF16)
    go_left = remote(
        tosend.at[pl.ds(0, sides)], side.at[pl.ds(sides, sides)], hs.at[0], hr.at[0], left
    )
    go_right = remote(
        tosend.at[pl.ds(sides, sides)], side.at[pl.ds(0, sides)], hs.at[1], hr.at[1], right
    )
    go_left.start()
    go_right.start()
    there = lax.broadcasted_iota(jnp.int32, (2 * n, 3 * n), 0) + start
    shift = hit(lax.broadcasted_iota(jnp.int32, (2 * n, 3 * n), 1) == there).astype(BF16)
    keys = mm(shift, everything).astype(BF16)

    steps = 4
    group = width // steps
    heads = group // HEAD
    ra = lax.broadcasted_iota(jnp.int32, (group, group), 0) // HEAD
    rb = lax.broadcasted_iota(jnp.int32, (group, group), 1) // HEAD
    ones = hit(ra == rb).astype(BF16)
    own = tall[n : 2 * n, :]
    loads[0].wait()

    def project(cells, first, count):
        for j in range(steps):
            lanes = slice(j * group, (j + 1) * group)
            k = mm(cells, wqkv[:, width + j * group : width + (j + 1) * group]).astype(BF16)
            kbuf[first : first + count, lanes] = head_norm(k, ones).astype(BF16)
            v = mm(cells, wqkv[:, 2 * width + j * group : 2 * width + (j + 1) * group])
            vbuf[first : first + count, lanes] = v.astype(BF16)

    for j in range(steps):
        lanes = slice(j * group, (j + 1) * group)
        q = mm(own, wqkv[:, lanes]).astype(BF16)
        qbuf[:, lanes] = (head_norm(q, ones) * (1.0 / 8.0)).astype(BF16)
    project(keys, 0, 2 * n)

    total_keys = 2 * n + 2 * sides
    i = lax.broadcasted_iota(jnp.int32, (1, total_keys), 1)
    m = jnp.where(i < 2 * n + sides, i - 2 * n, i - 2 * n - sides)
    inner = i < 2 * n
    r_of = jnp.where(inner, i // cols, m // REACH)
    c_of = jnp.where(
        inner, i % cols, m % REACH + jnp.where(i < 2 * n + sides, -REACH, cols)
    )
    at_row = lat * WIN - s_lat + r_of
    valid = (at_row >= 0) & (at_row < WIN * n_lat)
    keyid = jnp.where(valid, (r_of // WIN) * 4 + (c_of + s_lon + WIN) // WIN, -1)
    qi = lax.broadcasted_iota(jnp.int32, (n, 1), 0)
    qid = (qi // cols + s_lat) // WIN * 4 + (qi % cols + s_lon + WIN) // WIN
    same = qid == keyid
    lane = lax.broadcasted_iota(jnp.int32, (n, group), 1) // HEAD

    go_left.wait_recv()
    go_right.wait_recv()
    project(side[...], 2 * n, 2 * sides)
    loads[1].wait()
    acc = tok_ref[...].astype(F32)
    for j in range(steps):
        lanes = slice(j * group, (j + 1) * group)
        qn = qbuf[:, lanes]
        stacked = jnp.concatenate(
            [jnp.where(lane == h, qn, jnp.zeros_like(qn)) for h in range(heads)], axis=0
        )
        scores = lax.dot_general(
            stacked, kbuf[:, lanes], (((1,), (1,)), ((), ())), preferred_element_type=F32
        )
        weights = []
        for h in range(heads):
            e = jnp.where(same, jnp.exp(scores[h * n : (h + 1) * n]), 0.0)
            total = jnp.sum(e, axis=1, keepdims=True)
            weights.append((e * (1.0 / total)).astype(BF16))
        mixedv = mm(jnp.concatenate(weights, axis=0), vbuf[:, lanes])
        att = jnp.zeros((n, group), F32)
        for h in range(heads):
            att = jnp.where(lane == h, mixedv[h * n : (h + 1) * n], att)
        acc = acc + mm(att.astype(BF16), wo[lanes, :])

    mixed = acc.astype(BF16)
    mixed_ref[...] = mixed
    normed2 = rms_rows(mixed).astype(BF16)
    send_ref[...] = normed2

    go_left.wait_send()
    go_right.wait_send()

    @pl.when(has_down)
    def _():
        go_down.wait_send()

    @pl.when(has_up)
    def _():
        go_up.wait_send()


def front_block(n_lat, n_lon, shifts, tok, w_qkv, w_out):
    n, width = tok.shape
    sides = 2 * 2 * WIN * REACH
    vm = pl.BlockSpec(memory_space=pltpu.VMEM)
    hbm = pl.BlockSpec(memory_space=pl.ANY)
    dma = pltpu.SemaphoreType.DMA
    keys = 2 * n + sides
    return pl.pallas_call(
        functools.partial(front_kernel, n_lat, n_lon),
        in_specs=[pl.BlockSpec(memory_space=pltpu.SMEM), vm, hbm, hbm],
        out_specs=[vm, vm],
        out_shape=[jax.ShapeDtypeStruct((n, width), BF16)] * 2,
        scratch_shapes=[
            pltpu.VMEM((3 * n, width), BF16),
            pltpu.VMEM((sides, width), BF16),
            pltpu.VMEM((sides, width), BF16),
            pltpu.VMEM(w_qkv.shape, BF16),
            pltpu.VMEM(w_out.shape, BF16),
            pltpu.VMEM((n, width), BF16),
            pltpu.VMEM((keys, width), BF16),
            pltpu.VMEM((keys, width), BF16),
            dma((2,)), dma((2,)), dma((2,)), dma((2,)), dma((2,)),
        ],
        compiler_params=pltpu.CompilerParams(
            collective_id=2, has_side_effects=True, vmem_limit_bytes=40 * 2**20
        ),
    )(shifts, tok, w_qkv, w_out)


def iota(shape, axis):
    return lax.broadcasted_iota(jnp.int32, shape, axis)


def onehot(shape, target):
    return hit(iota(shape, 1) == target).astype(BF16)


def flip(z, g):
    return 2 * ((z // 2 + g // 2) % 2) + (z + g) % 2


def layer_kernel(
    n_lat, n_lon, shifts_hbm, tok_hbm, router_hbm, ids_hbm, wqkv_hbm, wo_hbm, wg_hbm, wu_hbm,
    wd_hbm, out_ref, shifts, tok, router, ids, wqkv, wo, wg, wu, wd, own, sideout, sidein, vertin,
    side, cornin, qbuf, kbuf, vbuf, place, comb, info, normed2, acc, send, got, results, back,
    far_ids, far_info, far, far_acc, share, shared, w_sem, vs, vr, hs, hr, cs, cr, ms, mr, s1, r1, s2, r2
):
    lat, lon = lax.axis_index("lat"), lax.axis_index("lon")
    z, x = lon // 2, lon % 2
    plane = 2 * n_lat
    slab = plane * UNIT
    here = lat * 2 + x
    inner = (z + 1) // 2 % 2 == 1
    mirror = (lat, (3 - z) * 2 + x)
    loads = [
        pltpu.make_async_copy(src, dst, w_sem.at[i])
        for i, (src, dst) in enumerate((
            (tok_hbm, tok), (shifts_hbm, shifts), (ids_hbm, ids), (wqkv_hbm, wqkv),
            (wo_hbm, wo), (router_hbm, router), (wg_hbm, wg), (wu_hbm, wu), (wd_hbm, wd),
        ))
    ]
    for load in loads[:6]:
        load.start()
    n, width = tok.shape
    cols = n // WIN
    mesh_id = pl.DeviceIdType.MESH
    left = (lat, lax.rem(lon + n_lon - 1, n_lon))
    right = (lat, lax.rem(lon + 1, n_lon))
    up, down = (lat - 1, lon), (lat + 1, lon)
    has_up, has_down = lat > 0, lat < n_lat - 1

    barrier = pltpu.get_barrier_semaphore()
    devices = n_lat * n_lon

    at_lat = [(lat + k) % n_lat for k in range(n_lat)]
    at_lon = [(lon + k) % n_lon for k in range(n_lon)]
    around = [(0, 1), (0, n_lon - 1), (1, 0), (n_lat - 1, 0)]
    others = [(a, b) for a in range(n_lat) for b in range(n_lon)]
    for a, b in around + [o for o in others if o not in around and o != (0, 0)]:
        pl.semaphore_signal(
            barrier, inc=1, device_id=(at_lat[a], at_lon[b]), device_id_type=mesh_id
        )

    edge = REACH * cols
    nook = WIN * WIN

    @pl.when(lat == 0)
    def _():
        vertin[0:edge, :] = jnp.zeros((edge, width), BF16)
        cornin[0:nook, :] = jnp.zeros((nook, width), BF16)

    @pl.when(lat == n_lat - 1)
    def _():
        vertin[edge : 2 * edge, :] = jnp.zeros((edge, width), BF16)
        cornin[nook : 2 * nook, :] = jnp.zeros((nook, width), BF16)

    half = WIN * REACH
    lanes2 = width // 2
    r = iota((4 * half, 1), 0)
    within = r % half
    cell = within // REACH * cols + within % REACH + jnp.where(r >= 2 * half, cols - REACH, 0)
    second = r // half % 2 == 1
    pick0 = onehot((4 * half, n), jnp.where(second, -1, cell))
    pick1 = onehot((4 * half, n), jnp.where(second, cell, -1))
    loads[0].wait()
    own[...] = rms_rows(tok[...]).astype(BF16)
    sideout[...] = (
        mm(pick0, own[:, 0:lanes2]) + mm(pick1, own[:, lanes2:width])
    ).astype(BF16)
    pl.semaphore_wait(barrier, devices - 1)

    def remote(src, dst, ssem, rsem, to):
        return pltpu.make_async_remote_copy(
            src_ref=src, dst_ref=dst, send_sem=ssem, recv_sem=rsem,
            device_id=to, device_id_type=mesh_id,
        )

    first, last = pl.ds(0, 2 * half), pl.ds(2 * half, 2 * half)
    go_left = remote(sideout.at[first], sidein.at[last], hs.at[0], hr.at[0], left)
    go_right = remote(sideout.at[last], sidein.at[first], hs.at[1], hr.at[1], right)
    go_left.start()
    go_right.start()
    go_down = remote(
        own.at[pl.ds(n - edge, edge)], vertin.at[pl.ds(0, edge)], vs.at[0], vr.at[0], down
    )
    go_up = remote(own.at[pl.ds(0, edge)], vertin.at[pl.ds(edge, edge)], vs.at[1], vr.at[1], up)

    @pl.when(has_down)
    def _():
        go_down.start()

    @pl.when(has_up)
    def _():
        go_up.start()

    tell = remote(ids, far_ids, ms.at[0], mr.at[0], mirror)
    lend = remote(normed2, far, ms.at[1], mr.at[1], mirror)
    give = remote(share, shared, ms.at[2], mr.at[2], mirror)
    loads[2].wait()

    @pl.when(inner)
    def _():
        tell.start()

    @pl.when(~inner)
    def _():
        far_ids[...] = ids[...]

    steps = 4
    group = width // steps
    heads = group // HEAD
    ones = hit(iota((group, group), 0) // HEAD == iota((group, group), 1) // HEAD).astype(BF16)
    loads[3].wait()
    for load in loads[6:]:
        load.start()

    def project(cells, at):
        for j in range(steps):
            lanes = slice(j * group, (j + 1) * group)
            k = mm(cells, wqkv[:, width + j * group : width + (j + 1) * group]).astype(BF16)
            kbuf[at : at + cells.shape[0], lanes] = head_norm(k, ones).astype(BF16)
            v = mm(cells, wqkv[:, 2 * width + j * group : 2 * width + (j + 1) * group])
            vbuf[at : at + cells.shape[0], lanes] = v.astype(BF16)

    for j in range(steps):
        lanes = slice(j * group, (j + 1) * group)
        q = mm(own[...], wqkv[:, lanes]).astype(BF16)
        qbuf[:, lanes] = (head_norm(q, ones) * (1.0 / 8.0)).astype(BF16)
    project(own[...], 0)

    loads[1].wait()
    s_lat, s_lon = shifts[0], shifts[1]
    w = iota((n, 1), 0)
    v_at = w // cols
    vert_at = jnp.where(v_at < s_lat, REACH - s_lat + v_at, REACH + v_at - s_lat)
    vert_pick = onehot((n, 2 * edge), vert_at * cols + w % cols)

    @pl.when(has_up)
    def _():
        go_down.wait_recv()

    @pl.when(has_down)
    def _():
        go_up.wait_recv()

    project(mm(vert_pick, vertin[...]).astype(BF16), n)

    routes(n_lon, z, ids, info, place, 0)

    @pl.when(inner)
    def _():
        tell.wait_recv()

    far_z = jnp.where(inner, 3 - z, z)
    routes(n_lon, far_z, far_ids, far_info, place, 2 * slab)

    w = iota((nook, 1), 0)
    major, minor = w // WIN, w % WIN
    side_at = major * REACH + jnp.where(
        minor < s_lon, REACH - s_lon + minor, 2 * half + minor - s_lon
    )
    side0 = onehot((nook, 4 * half), side_at)
    side1 = onehot((nook, 4 * half), side_at + half)
    corn_at = jnp.where(major < s_lat, WIN - s_lat + major, WIN + major - s_lat)
    corn_pick = onehot((nook, 2 * nook), corn_at * WIN + minor)
    go_left.wait_recv()
    go_right.wait_recv()
    side[:, 0:lanes2] = mm(side0, sidein[...]).astype(BF16)
    side[:, lanes2:width] = mm(side1, sidein[...]).astype(BF16)
    corn_down = remote(side, cornin.at[pl.ds(0, nook)], cs.at[0], cr.at[0], down)
    corn_up = remote(side, cornin.at[pl.ds(nook, nook)], cs.at[1], cr.at[1], up)

    @pl.when(has_down)
    def _():
        corn_down.start()

    @pl.when(has_up)
    def _():
        corn_up.start()

    project(side[...], 2 * n)

    total_keys = 2 * n + 2 * nook
    i = iota((1, total_keys), 1)
    in_own, in_vert, in_side = i < n, i < 2 * n, i < 2 * n + nook
    m = i - jnp.where(in_side, 2 * n, 2 * n + nook)
    row = jnp.where(in_vert, jnp.where(in_own, i, i - n) // cols, m // WIN)
    col = jnp.where(in_vert, i % cols, m % WIN)
    inside = in_own | (in_side & ~in_vert)
    key_row = jnp.where(inside, (row + s_lat) // WIN, jnp.where(row < s_lat, 0, 1))
    key_col = jnp.where(in_vert, (col + s_lon) // WIN, jnp.where(col < s_lon, 0, 2))
    gone = ~inside & (((row < s_lat) & (lat == 0)) | ((row >= s_lat) & (lat == n_lat - 1)))
    keyid = jnp.where(gone, -1, key_row * 4 + key_col)
    w = iota((n, 1), 0)
    same = (w // cols + s_lat) // WIN * 4 + (w % cols + s_lon) // WIN == keyid
    lane = iota((n, group), 1) // HEAD

    @pl.when(has_up)
    def _():
        corn_down.wait_recv()

    @pl.when(has_down)
    def _():
        corn_up.wait_recv()

    project(mm(corn_pick, cornin[...]).astype(BF16), 2 * n + nook)

    loads[4].wait()
    total = tok[...].astype(F32)
    for j in range(steps):
        lanes = slice(j * group, (j + 1) * group)
        qn = qbuf[:, lanes]
        stacked = jnp.concatenate(
            [jnp.where(lane == h, qn, jnp.zeros_like(qn)) for h in range(heads)], axis=0
        )
        scores = lax.dot_general(
            stacked, kbuf[:, lanes], (((1,), (1,)), ((), ())), preferred_element_type=F32
        )
        weights = []
        for h in range(heads):
            e = jnp.where(same, jnp.exp(scores[h * n : (h + 1) * n]), 0.0)
            weights.append((e * (1.0 / jnp.sum(e, axis=1, keepdims=True))).astype(BF16))
        mixedv = mm(jnp.concatenate(weights, axis=0), vbuf[:, lanes])
        att = jnp.zeros((n, group), F32)
        for h in range(heads):
            att = jnp.where(lane == h, mixedv[h * n : (h + 1) * n], att)
        total = total + mm(att.astype(BF16), wo[lanes, :])

    mixed = total.astype(BF16)
    acc[...] = mixed.astype(F32)
    normed2[...] = rms_rows(mixed).astype(BF16)

    @pl.when(inner)
    def _():
        lend.start()

    @pl.when(~inner)
    def _():
        far[...] = normed2[...]

    def pack(cells, first):
        end = cells[:, WIDE:width]
        for t in range(3):
            lanes = slice(t * TAIL, (t + 1) * TAIL)
            both = jnp.concatenate([cells[:, lanes], end], axis=0)
            at = t * 4 * slab + first
            send[first : first + 2 * slab, lanes] = mm(place[at : at + 2 * slab, :], both).astype(BF16)

    def rows(g, j):
        return pl.ds(pl.multiple_of(g * slab + j * UNIT, UNIT), UNIT)

    def forth(g):
        return flip(z, jnp.where(inner & (g >= 2), 3 - g, g))

    def home(g):
        return flip(z, jnp.where(inner, jnp.where(g == 3, 0, g), jnp.where(g == 2, 1, g)))

    def begin(g):
        return jnp.where((g == 0) | (inner & (g == 3)), 1, 0)

    out1, out2 = (send, got, s1, r1, forth), (results, back, s2, r2, home)

    to_x = [x, (x + 1) % 2]

    def launch(out, g):
        src, dst, ssem, rsem, to_plane = out
        base = to_plane(g) * 2
        mine = dst.at[rows(g, here)]

        @pl.when(begin(g) == 0)
        def _():
            remote(src.at[rows(g, here)], mine, ssem.at[g], rsem.at[g], (lat, base + x)).start()

        @pl.when(begin(g) == 1)
        def _():
            pltpu.make_async_copy(src.at[rows(g, here)], mine, rsem.at[g]).start()

        for k in range(1, plane):
            la, xx = at_lat[k // 2], to_x[k % 2]
            remote(
                src.at[rows(g, la * 2 + xx)], mine, ssem.at[g], rsem.at[g], (la, base + xx)
            ).start()

    def whole(g):
        return pl.ds(pl.multiple_of(g * slab, slab), slab)

    def land(out, g):
        src, dst, ssem, rsem, to_plane = out
        pltpu.make_async_copy(src.at[whole(g)], dst.at[whole(g)], rsem.at[g]).wait()

    def drain(out, g):
        src, dst, ssem, rsem, to_plane = out

        @pl.when(begin(g) == 0)
        def _():
            pltpu.make_async_copy(src.at[whole(g)], dst.at[whole(g)], ssem.at[g]).wait()

        @pl.when(begin(g) == 1)
        def _():
            few = pl.ds(pl.multiple_of(g * slab, slab), slab - UNIT)
            pltpu.make_async_copy(src.at[few], dst.at[few], ssem.at[g]).wait()

    pack(normed2, 0)
    launch(out1, 1)
    launch(out1, 0)
    loads[5].wait()
    gates(normed2, router, info, comb, 0)

    @pl.when(inner)
    def _():
        lend.wait_recv()

    pack(far, 2 * slab)
    launch(out1, 3)
    launch(out1, 2)

    gates(far, router, far_info, comb, 2 * slab)

    half_rows = plane * MOST
    count = 2 * half_rows
    r = iota((count, 1), 0)
    slot = r // half_rows * MOST + r % MOST
    base = r % half_rows // MOST * UNIT
    pick = onehot((count, slab), base + slot)
    tails = [
        onehot((count, slab), jnp.where(slot % 3 == t, base + MAIN + slot // 3, -1))
        for t in range(3)
    ]
    r = iota((1, count), 1)
    slot = r // half_rows * MOST + r % MOST
    base = r % half_rows // MOST * UNIT
    target = iota((slab, count), 0)
    put = hit(target == base + slot).astype(BF16)
    put_tails = [
        hit(target == jnp.where(slot % 3 == t, base + MAIN + slot // 3, -1)).astype(BF16)
        for t in range(3)
    ]
    for load in loads[6:]:
        load.wait()

    def experts(i, c):
        g = i + 1 - 2 * (i % 2)
        land(out1, g)
        at = pl.ds(pl.multiple_of(g * slab, slab), slab)
        wide = mm(pick, got[at, :]).astype(BF16)
        end = mm(tails[0], got[at, 0:TAIL])
        for t in range(1, 3):
            end = end + mm(tails[t], got[at, t * TAIL : (t + 1) * TAIL])
        cells = jnp.concatenate([wide, end.astype(BF16)], axis=1)
        parts = []
        for e in range(2):
            xe = cells[e * half_rows : (e + 1) * half_rows]
            gate = mm(xe, wg[:, e * FF : (e + 1) * FF])
            upper = mm(xe, wu[:, e * FF : (e + 1) * FF])
            hidden = (jax.nn.silu(gate) * upper).astype(BF16)
            parts.append(mm(hidden, wd[e * FF : (e + 1) * FF, :]).astype(BF16))
        part = jnp.concatenate(parts, axis=0)
        for t in range(3):
            lanes = slice(t * TAIL, (t + 1) * TAIL)
            results[at, lanes] = (
                mm(put, part[:, lanes]) + mm(put_tails[t], part[:, WIDE:width])
            ).astype(BF16)
        launch(out2, g)
        return c

    lax.fori_loop(0, 4, experts, 0)


    def gather(g, into):
        land(out2, g)
        at = slice(g * slab, (g + 1) * slab)
        for t in range(3):
            lanes = slice(t * TAIL, (t + 1) * TAIL)
            s = mm(comb[t * 4 * n : (t + 1) * 4 * n, at], back[at, lanes])
            into[:, lanes] += s[0:n] + s[n : 2 * n]
            into[:, WIDE:width] += s[2 * n : 3 * n] + s[3 * n : 4 * n]

    @pl.when(inner)
    def _():
        far_acc[...] = jnp.zeros_like(far_acc)
        gather(3, far_acc)
        gather(2, far_acc)
        share[...] = far_acc[...].astype(BF16)
        give.start()

    gather(1, acc)
    gather(0, acc)

    @pl.when(~inner)
    def _():
        gather(3, acc)
        gather(2, acc)
        out_ref[...] = acc[...].astype(BF16)

    @pl.when(inner)
    def _():
        give.wait_recv()
        out_ref[...] = (acc[...] + shared[...].astype(F32)).astype(BF16)
        tell.wait_send()
        lend.wait_send()
        give.wait_send()

    go_left.wait_send()
    go_right.wait_send()

    @pl.when(has_down)
    def _():
        go_down.wait_send()
        corn_down.wait_send()

    @pl.when(has_up)
    def _():
        go_up.wait_send()
        corn_up.wait_send()

    for g in range(4):
        drain(out1, g)
        drain(out2, g)


def routes(n_lon, z, ids, info, place, first):
    n = ids.shape[1]
    r0, r1 = ids[0:1, :], ids[1:2, :]
    ia, ib = iota((n, n), 0), iota((n, n), 1)

    def column(row):
        return jnp.sum(jnp.where(ia == ib, row.astype(F32), 0.0), axis=1, keepdims=True)

    c0, c1 = column(r0).astype(jnp.int32), column(r1).astype(jnp.int32)
    rank0c = jnp.sum(hit((c0 == r0) & (ib < ia)), axis=1, keepdims=True)
    rank1c = jnp.sum(hit(c1 == r0) + hit((c1 == r1) & (ib < ia)), axis=1, keepdims=True)
    rank0r = jnp.sum(hit((c0 == r0) & (ia < ib)), axis=0, keepdims=True)
    rank1r = jnp.sum(hit(c0 == r1) + hit((c1 == r1) & (ia < ib)), axis=0, keepdims=True)

    def places(e, rank):
        slot = e % 2 * MOST + rank.astype(jnp.int32)
        device = e // 2
        at_lat, at_lon = device // n_lon, device % n_lon
        base = (flip(at_lon // 2, z) * (place.shape[0] // 12 // UNIT) + at_lat * 2 + at_lon % 2) * UNIT
        return base + slot, base + MAIN + slot // 3, slot % 3

    m0, t0, q0 = places(c0, rank0c)
    m1, t1, q1 = places(c1, rank1c)
    col = iota(info.shape, 1)
    table = jnp.zeros(info.shape, F32)
    for i, v in enumerate((m0, t0, q0, m1, t1, q1, c0, c1)):
        table = jnp.where(col == i, v.astype(F32), table)
    info[...] = table
    m0, t0, q0 = places(r0, rank0r)
    m1, t1, q1 = places(r1, rank1r)
    total = place.shape[0] // 3
    count = total // 2
    row = iota((count, n), 0) + first
    main = (hit(row == m0) + hit(row == m1)).astype(BF16)
    for t in range(3):
        rows = slice(t * total + first, t * total + first + count)
        place[rows, 0:n] = main
        place[rows, n : 2 * n] = (
            hit((row == t0) & (q0 == t)) + hit((row == t1) & (q1 == t))
        ).astype(BF16)


def gates(cells, router, info, comb, begin):
    logits = lax.dot_general(
        cells[...], router[...], (((1,), (1,)), ((), ())), preferred_element_type=F32
    )
    n = logits.shape[0]
    eid = iota(logits.shape, 1).astype(F32)
    m0, t0, q0, m1, t1, q1, c0, c1 = (info[:, i : i + 1] for i in range(8))
    s0 = jax.nn.sigmoid(jnp.sum(jnp.where(eid == c0, logits, 0.0), axis=1, keepdims=True))
    s1 = jax.nn.sigmoid(jnp.sum(jnp.where(eid == c1, logits, 0.0), axis=1, keepdims=True))
    g0 = s0 / (s0 + s1)
    g1 = s1 / (s0 + s1)
    count = comb.shape[1] // 2
    at = (iota((n, count), 1) + begin).astype(F32)

    def keep(first, a):
        hi = a.astype(BF16)
        comb[first : first + n, begin : begin + count] = hi
        comb[first + n : first + 2 * n, begin : begin + count] = (a - hi.astype(F32)).astype(BF16)

    main = jnp.where(at == m0, g0, 0.0) + jnp.where(at == m1, g1, 0.0)
    for t in range(3):
        keep(t * 4 * n, main)
        keep(
            t * 4 * n + 2 * n,
            jnp.where((at == t0) & (q0 == t), g0, 0.0) + jnp.where((at == t1) & (q1 == t), g1, 0.0),
        )


def layer_block(n_lat, n_lon, shifts, tok, router, ids, w_qkv, w_out, w_gate, w_up, w_down):
    n, width = tok.shape
    total = n_lat * n_lon * UNIT
    keys = 2 * n + 2 * WIN * WIN
    hbm = pl.BlockSpec(memory_space=pl.ANY)
    dma = pltpu.SemaphoreType.DMA

    def vmem(*shape, dtype=BF16):
        return pltpu.VMEM(shape, dtype)

    return pl.pallas_call(
        functools.partial(layer_kernel, n_lat, n_lon),
        out_shape=jax.ShapeDtypeStruct((n, width), BF16),
        in_specs=[hbm] * 9,
        out_specs=pl.BlockSpec(memory_space=pltpu.VMEM),
        scratch_shapes=[
            pltpu.SMEM((2,), jnp.int32),
            vmem(n, width),
            vmem(router.shape[1], width),
            vmem(TOP, n, dtype=jnp.int32),
            vmem(*w_qkv.shape),
            vmem(*w_out.shape),
            vmem(*w_gate.shape),
            vmem(*w_up.shape),
            vmem(*w_down.shape),
            vmem(n, width),
            vmem(4 * WIN * REACH, width // 2),
            vmem(4 * WIN * REACH, width // 2),
            vmem(2 * REACH * (n // WIN), width),
            vmem(WIN * WIN, width),
            vmem(2 * WIN * WIN, width),
            vmem(n, width),
            vmem(keys, width),
            vmem(keys, width),
            vmem(3 * total, 2 * n),
            vmem(12 * n, total),
            vmem(n, 128, dtype=F32),
            vmem(n, width),
            vmem(n, width, dtype=F32),
            vmem(total, WIDE),
            vmem(total, WIDE),
            vmem(total, WIDE),
            vmem(total, WIDE),
            vmem(TOP, n, dtype=jnp.int32),
            vmem(n, 128, dtype=F32),
            vmem(n, width),
            vmem(n, width, dtype=F32),
            vmem(n, width),
            vmem(n, width),
            dma((9,)),
            dma((2,)), dma((2,)), dma((2,)), dma((2,)), dma((2,)), dma((2,)),
            dma((3,)), dma((3,)),
            dma((4,)), dma((4,)), dma((4,)), dma((4,)),
        ],
        compiler_params=pltpu.CompilerParams(
            collective_id=1, has_side_effects=True, vmem_limit_bytes=56 * 2**20
        ),
    )(shifts, tok, router.T, ids.T, w_qkv, w_out, w_gate, w_up, w_down)


def body(tokens, shifts, w_qkv, w_out, router, expert_ids, w_gate, w_up, w_down):
    n_lat = lax.axis_size("lat")
    n_lon = lax.axis_size("lon")
    devices = n_lat * n_lon
    rows, cols, width = tokens.shape
    ids = expert_ids.reshape(-1, TOP)
    tok = tokens.reshape(-1, width)
    if (n_lat, n_lon) == (4, 8) and w_gate.shape[1] == 2 * FF:
        out = layer_block(
            n_lat, n_lon, shifts, tok, router, ids, w_qkv, w_out, w_gate, w_up, w_down
        )
        return out.reshape(rows, cols, width)
    mixed, normed2 = front_block(n_lat, n_lon, shifts, tok, w_qkv, w_out)
    return general(mixed, normed2, router, ids, w_gate, w_up, w_down, devices, rows, cols)


def general(mixed, normed2, router, ids, w_gate, w_up, w_down, devices, rows, cols):
    width = mixed.shape[1]
    logits = jnp.dot(normed2, router, preferred_element_type=jnp.float32)
    experts = router.shape[1]
    expert_iota = jnp.arange(experts, dtype=jnp.int32)
    picks = ids[:, :, None] == expert_iota[None, None, :]
    chosen = jnp.sum(jnp.where(picks, logits[:, None, :], 0.0), axis=-1)
    sig = jax.nn.sigmoid(chosen)
    gates = sig / jnp.sum(sig, axis=1, keepdims=True)
    flat = ids.reshape(-1)
    order = jnp.arange(flat.shape[0], dtype=jnp.int32)
    earlier = (flat[:, None] == flat[None, :]) & (order[None, :] < order[:, None])
    rank = jnp.sum(earlier.astype(jnp.int32), axis=1)
    share = w_gate.shape[1]
    piece = min(FF, share)
    repl = FF // piece
    group = share // piece
    most = MOST
    cap = group * most
    token_of = jnp.arange(flat.shape[0], dtype=jnp.int32) // TOP
    slot = flat % group * most + rank
    slot_index = jnp.stack(
        [(flat // group * repl + copy) * cap + slot for copy in range(repl)], axis=0
    )
    routed = normed2[token_of]
    send = (
        jnp.zeros((devices * cap, width), jnp.bfloat16)
        .at[slot_index.reshape(-1)]
        .set(jnp.tile(routed, (repl, 1)))
    )
    send = send.reshape(devices, group, most, width)
    received = lax.all_to_all(send, ("lat", "lon"), split_axis=0, concat_axis=0, tiled=True)
    results = []
    for local in range(group):
        block = received[:, local].reshape(-1, width)
        gate = jnp.dot(
            block,
            w_gate[:, local * piece : (local + 1) * piece],
            preferred_element_type=jnp.float32,
        )
        upper = jnp.dot(
            block, w_up[:, local * piece : (local + 1) * piece], preferred_element_type=jnp.float32
        )
        hidden = (jax.nn.silu(gate) * upper).astype(jnp.bfloat16)
        part = jnp.dot(
            hidden, w_down[local * piece : (local + 1) * piece], preferred_element_type=jnp.float32
        ).astype(jnp.bfloat16)
        results.append(part.reshape(received.shape[0], received.shape[2], width))
    back = lax.all_to_all(
        jnp.stack(results, axis=1), ("lat", "lon"), split_axis=0, concat_axis=0, tiled=True
    )
    back_flat = back.reshape(devices * cap, width)
    combined = jnp.zeros((flat.shape[0], width), jnp.float32)
    for copy in range(repl):
        combined = combined + back_flat[slot_index[copy]].astype(jnp.float32)
    combined = combined.reshape(-1, TOP, width)
    moe = jnp.sum(gates[:, :, None] * combined, axis=1)
    layer_out = (mixed.astype(jnp.float32) + moe).astype(jnp.bfloat16)
    return layer_out.reshape(rows, cols, width)


def solution(mesh):
    placed = (
        P("lat", "lon", None),
        P(),
        P(),
        P(),
        P(),
        P("lat", "lon", None, None),
        P(None, ("lat", "lon")),
        P(None, ("lat", "lon")),
        P(("lat", "lon"), None),
    )
    return jax.shard_map(
        body, mesh=mesh, in_specs=placed, out_specs=P("lat", "lon", None), check_vma=False
    )
```

```python
import functools

import jax
import jax.numpy as jnp
import numpy as np
from jax import lax
from jax.experimental import pallas as pl
from jax.experimental.pallas import tpu as pltpu
from jax.sharding import PartitionSpec as P

HEAD = 64
FF = 1024
TOP = 2
WIN = 8
MOST = 6
UNIT = 16
MAIN = 12
WIDE = 768
TAIL = 256
F32 = jnp.float32
BF16 = jnp.bfloat16


def rms_rows(x):
    xf = x.astype(jnp.float32)
    return xf * lax.rsqrt(jnp.mean(xf * xf, axis=-1, keepdims=True) + 1e-05)


def mm(a, b):
    return jnp.dot(a, b, preferred_element_type=F32)


def hit(cond):
    return jnp.where(cond, 1.0, 0.0)


def head_norm(x, ones):
    xf = x.astype(F32)
    sq = xf * xf
    hi = sq.astype(BF16)
    lo = (sq - hi.astype(F32)).astype(BF16)
    mean = (mm(hi, ones) + mm(lo, ones)) * (1.0 / HEAD)
    return xf * lax.rsqrt(mean + 1e-05)


REACH = WIN - 1


def front_kernel(
    n_lat, n_lon, shifts_ref, tok_ref, wqkv_hbm, wo_hbm, mixed_ref, send_ref,
    tall, tosend, side, wqkv, wo, qbuf, kbuf, vbuf, w_sem, vs, vr, hs, hr
):
    lat, lon = lax.axis_index("lat"), lax.axis_index("lon")
    loads = [
        pltpu.make_async_copy(wqkv_hbm, wqkv, w_sem.at[0]),
        pltpu.make_async_copy(wo_hbm, wo, w_sem.at[1]),
    ]
    for load in loads:
        load.start()
    n, width = tok_ref.shape
    cols = n // WIN
    left = (lat, lax.rem(lon + n_lon - 1, n_lon))
    right = (lat, lax.rem(lon + 1, n_lon))
    up, down = (lat - 1, lon), (lat + 1, lon)
    has_up, has_down = lat > 0, lat < n_lat - 1
    mesh_id = pl.DeviceIdType.MESH
    barrier = pltpu.get_barrier_semaphore()
    around = (
        left, right, (lax.rem(lat + n_lat - 1, n_lat), lon), (lax.rem(lat + 1, n_lat), lon)
    )
    for other in around:
        pl.semaphore_signal(barrier, inc=1, device_id=other, device_id_type=mesh_id)

    tall[n : 2 * n, :] = rms_rows(tok_ref[...]).astype(BF16)
    tall[0:cols, :] = jnp.zeros((cols, width), BF16)
    tall[3 * n - cols : 3 * n, :] = jnp.zeros((cols, width), BF16)
    edge = REACH * cols

    @pl.when(lat == 0)
    def _():
        tall[cols:n, :] = jnp.zeros((edge, width), BF16)

    @pl.when(lat == n_lat - 1)
    def _():
        tall[2 * n : 2 * n + edge, :] = jnp.zeros((edge, width), BF16)

    pl.semaphore_wait(barrier, len(around))

    def remote(src, dst, ssem, rsem, to):
        return pltpu.make_async_remote_copy(
            src_ref=src, dst_ref=dst, send_sem=ssem, recv_sem=rsem,
            device_id=to, device_id_type=mesh_id,
        )

    above, below = tall.at[pl.ds(cols, edge)], tall.at[pl.ds(2 * n, edge)]
    go_down = remote(tall.at[pl.ds(n + cols, edge)], above, vs.at[0], vr.at[0], down)
    go_up = remote(tall.at[pl.ds(n, edge)], below, vs.at[1], vr.at[1], up)

    @pl.when(has_down)
    def _():
        go_down.start()

    @pl.when(has_up)
    def _():
        go_up.start()

    s_lat, s_lon = shifts_ref[0], shifts_ref[1]
    sides = 2 * WIN * REACH
    out_row = lax.broadcasted_iota(jnp.int32, (2 * sides, 1), 0)
    local = jnp.where(out_row >= sides, out_row - sides, out_row)
    at = local // REACH * cols + local % REACH + jnp.where(out_row >= sides, cols - REACH, 0)
    start = (WIN - s_lat) * cols
    pick = hit(lax.broadcasted_iota(jnp.int32, (2 * sides, 3 * n), 1) == at + start).astype(BF16)

    @pl.when(has_up)
    def _():
        go_down.wait_recv()

    @pl.when(has_down)
    def _():
        go_up.wait_recv()

    everything = tall[...]
    tosend[...] = mm(pick, everything).astype(BF16)
    go_left = remote(
        tosend.at[pl.ds(0, sides)], side.at[pl.ds(sides, sides)], hs.at[0], hr.at[0], left
    )
    go_right = remote(
        tosend.at[pl.ds(sides, sides)], side.at[pl.ds(0, sides)], hs.at[1], hr.at[1], right
    )
    go_left.start()
    go_right.start()
    there = lax.broadcasted_iota(jnp.int32, (2 * n, 3 * n), 0) + start
    shift = hit(lax.broadcasted_iota(jnp.int32, (2 * n, 3 * n), 1) == there).astype(BF16)
    keys = mm(shift, everything).astype(BF16)

    steps = 4
    group = width // steps
    heads = group // HEAD
    ra = lax.broadcasted_iota(jnp.int32, (group, group), 0) // HEAD
    rb = lax.broadcasted_iota(jnp.int32, (group, group), 1) // HEAD
    ones = hit(ra == rb).astype(BF16)
    own = tall[n : 2 * n, :]
    loads[0].wait()

    def project(cells, first, count):
        for j in range(steps):
            lanes = slice(j * group, (j + 1) * group)
            k = mm(cells, wqkv[:, width + j * group : width + (j + 1) * group]).astype(BF16)
            kbuf[first : first + count, lanes] = head_norm(k, ones).astype(BF16)
            v = mm(cells, wqkv[:, 2 * width + j * group : 2 * width + (j + 1) * group])
            vbuf[first : first + count, lanes] = v.astype(BF16)

    for j in range(steps):
        lanes = slice(j * group, (j + 1) * group)
        q = mm(own, wqkv[:, lanes]).astype(BF16)
        qbuf[:, lanes] = (head_norm(q, ones) * (1.0 / 8.0)).astype(BF16)
    project(keys, 0, 2 * n)

    total_keys = 2 * n + 2 * sides
    i = lax.broadcasted_iota(jnp.int32, (1, total_keys), 1)
    m = jnp.where(i < 2 * n + sides, i - 2 * n, i - 2 * n - sides)
    inner = i < 2 * n
    r_of = jnp.where(inner, i // cols, m // REACH)
    c_of = jnp.where(
        inner, i % cols, m % REACH + jnp.where(i < 2 * n + sides, -REACH, cols)
    )
    at_row = lat * WIN - s_lat + r_of
    valid = (at_row >= 0) & (at_row < WIN * n_lat)
    keyid = jnp.where(valid, (r_of // WIN) * 4 + (c_of + s_lon + WIN) // WIN, -1)
    qi = lax.broadcasted_iota(jnp.int32, (n, 1), 0)
    qid = (qi // cols + s_lat) // WIN * 4 + (qi % cols + s_lon + WIN) // WIN
    same = qid == keyid
    lane = lax.broadcasted_iota(jnp.int32, (n, group), 1) // HEAD

    go_left.wait_recv()
    go_right.wait_recv()
    project(side[...], 2 * n, 2 * sides)
    loads[1].wait()
    acc = tok_ref[...].astype(F32)
    for j in range(steps):
        lanes = slice(j * group, (j + 1) * group)
        qn = qbuf[:, lanes]
        stacked = jnp.concatenate(
            [jnp.where(lane == h, qn, jnp.zeros_like(qn)) for h in range(heads)], axis=0
        )
        scores = lax.dot_general(
            stacked, kbuf[:, lanes], (((1,), (1,)), ((), ())), preferred_element_type=F32
        )
        weights = []
        for h in range(heads):
            e = jnp.where(same, jnp.exp(scores[h * n : (h + 1) * n]), 0.0)
            total = jnp.sum(e, axis=1, keepdims=True)
            weights.append((e * (1.0 / total)).astype(BF16))
        mixedv = mm(jnp.concatenate(weights, axis=0), vbuf[:, lanes])
        att = jnp.zeros((n, group), F32)
        for h in range(heads):
            att = jnp.where(lane == h, mixedv[h * n : (h + 1) * n], att)
        acc = acc + mm(att.astype(BF16), wo[lanes, :])

    mixed = acc.astype(BF16)
    mixed_ref[...] = mixed
    normed2 = rms_rows(mixed).astype(BF16)
    send_ref[...] = normed2

    go_left.wait_send()
    go_right.wait_send()

    @pl.when(has_down)
    def _():
        go_down.wait_send()

    @pl.when(has_up)
    def _():
        go_up.wait_send()


def front_block(n_lat, n_lon, shifts, tok, w_qkv, w_out):
    n, width = tok.shape
    sides = 2 * 2 * WIN * REACH
    vm = pl.BlockSpec(memory_space=pltpu.VMEM)
    hbm = pl.BlockSpec(memory_space=pl.ANY)
    dma = pltpu.SemaphoreType.DMA
    keys = 2 * n + sides
    return pl.pallas_call(
        functools.partial(front_kernel, n_lat, n_lon),
        in_specs=[pl.BlockSpec(memory_space=pltpu.SMEM), vm, hbm, hbm],
        out_specs=[vm, vm],
        out_shape=[jax.ShapeDtypeStruct((n, width), BF16)] * 2,
        scratch_shapes=[
            pltpu.VMEM((3 * n, width), BF16),
            pltpu.VMEM((sides, width), BF16),
            pltpu.VMEM((sides, width), BF16),
            pltpu.VMEM(w_qkv.shape, BF16),
            pltpu.VMEM(w_out.shape, BF16),
            pltpu.VMEM((n, width), BF16),
            pltpu.VMEM((keys, width), BF16),
            pltpu.VMEM((keys, width), BF16),
            dma((2,)), dma((2,)), dma((2,)), dma((2,)), dma((2,)),
        ],
        compiler_params=pltpu.CompilerParams(
            collective_id=2, has_side_effects=True, vmem_limit_bytes=40 * 2**20
        ),
    )(shifts, tok, w_qkv, w_out)


def iota(shape, axis):
    return lax.broadcasted_iota(jnp.int32, shape, axis)


def onehot(shape, target):
    return hit(iota(shape, 1) == target).astype(BF16)


def flip(z, g):
    return 2 * ((z // 2 + g // 2) % 2) + (z + g) % 2


def layer_kernel(
    n_lat, n_lon, shifts_hbm, tok_hbm, router_hbm, ids_hbm, wqkv_hbm, wo_hbm, wg_hbm, wu_hbm,
    wd_hbm, out_ref, shifts, tok, router, ids, wqkv, wo, wg, wu, wd, own, sideout, sidein, vertin,
    side, cornin, qbuf, kbuf, vbuf, numer, denom, place, comb, info, normed2, acc, send, got, results, back,
    far_ids, far_info, far, far_acc, share, shared, w_sem, vs, vr, hs, hr, cs, cr, ms, mr, s1, r1, s2, r2
):
    lat, lon = lax.axis_index("lat"), lax.axis_index("lon")
    z, x = lon // 2, lon % 2
    plane = 2 * n_lat
    slab = plane * UNIT
    here = lat * 2 + x
    inner = (z + 1) // 2 % 2 == 1
    mirror = (lat, (3 - z) * 2 + x)
    loads = [
        pltpu.make_async_copy(src, dst, w_sem.at[i])
        for i, (src, dst) in enumerate((
            (tok_hbm, tok), (shifts_hbm, shifts), (ids_hbm, ids), (wqkv_hbm, wqkv),
            (wo_hbm, wo), (router_hbm, router), (wg_hbm, wg), (wu_hbm, wu), (wd_hbm, wd),
        ))
    ]
    for load in loads[:6]:
        load.start()
    n, width = tok.shape
    cols = n // WIN
    mesh_id = pl.DeviceIdType.MESH
    left = (lat, lax.rem(lon + n_lon - 1, n_lon))
    right = (lat, lax.rem(lon + 1, n_lon))
    up, down = (lat - 1, lon), (lat + 1, lon)
    has_up, has_down = lat > 0, lat < n_lat - 1

    barrier = pltpu.get_barrier_semaphore()
    devices = n_lat * n_lon

    at_lat = [(lat + k) % n_lat for k in range(n_lat)]
    at_lon = [(lon + k) % n_lon for k in range(n_lon)]
    around = [(0, 1), (0, n_lon - 1), (1, 0), (n_lat - 1, 0)]
    others = [(a, b) for a in range(n_lat) for b in range(n_lon)]
    for a, b in around + [o for o in others if o not in around and o != (0, 0)]:
        pl.semaphore_signal(
            barrier, inc=1, device_id=(at_lat[a], at_lon[b]), device_id_type=mesh_id
        )

    edge = REACH * cols
    nook = WIN * WIN

    @pl.when(lat == 0)
    def _():
        vertin[0:edge, :] = jnp.zeros((edge, width), BF16)
        cornin[0:nook, :] = jnp.zeros((nook, width), BF16)

    @pl.when(lat == n_lat - 1)
    def _():
        vertin[edge : 2 * edge, :] = jnp.zeros((edge, width), BF16)
        cornin[nook : 2 * nook, :] = jnp.zeros((nook, width), BF16)

    half = WIN * REACH
    lanes2 = width // 2
    r = iota((4 * half, 1), 0)
    within = r % half
    cell = within // REACH * cols + within % REACH + jnp.where(r >= 2 * half, cols - REACH, 0)
    second = r // half % 2 == 1
    pick0 = onehot((4 * half, n), jnp.where(second, -1, cell))
    pick1 = onehot((4 * half, n), jnp.where(second, cell, -1))
    loads[0].wait()
    own[...] = rms_rows(tok[...]).astype(BF16)
    sideout[...] = (
        mm(pick0, own[:, 0:lanes2]) + mm(pick1, own[:, lanes2:width])
    ).astype(BF16)
    pl.semaphore_wait(barrier, devices - 1)

    def remote(src, dst, ssem, rsem, to):
        return pltpu.make_async_remote_copy(
            src_ref=src, dst_ref=dst, send_sem=ssem, recv_sem=rsem,
            device_id=to, device_id_type=mesh_id,
        )

    first, last = pl.ds(0, 2 * half), pl.ds(2 * half, 2 * half)
    go_left = remote(sideout.at[first], sidein.at[last], hs.at[0], hr.at[0], left)
    go_right = remote(sideout.at[last], sidein.at[first], hs.at[1], hr.at[1], right)
    go_left.start()
    go_right.start()
    go_down = remote(
        own.at[pl.ds(n - edge, edge)], vertin.at[pl.ds(0, edge)], vs.at[0], vr.at[0], down
    )
    go_up = remote(own.at[pl.ds(0, edge)], vertin.at[pl.ds(edge, edge)], vs.at[1], vr.at[1], up)

    @pl.when(has_down)
    def _():
        go_down.start()

    @pl.when(has_up)
    def _():
        go_up.start()

    tell = remote(ids, far_ids, ms.at[0], mr.at[0], mirror)
    lend = remote(normed2, far, ms.at[1], mr.at[1], mirror)
    give = remote(share, shared, ms.at[2], mr.at[2], mirror)
    loads[2].wait()

    @pl.when(inner)
    def _():
        tell.start()

    @pl.when(~inner)
    def _():
        far_ids[...] = ids[...]

    steps = 4
    group = width // steps
    heads = group // HEAD
    ones = hit(iota((group, group), 0) // HEAD == iota((group, group), 1) // HEAD).astype(BF16)
    loads[3].wait()
    for load in loads[6:]:
        load.start()

    twice = jnp.concatenate([ones, ones], axis=0)

    def unit(a, into, at, scale):
        m = a.shape[0]
        a = a.astype(BF16).astype(F32)
        sq = a * a
        hi = sq.astype(BF16)
        lo = (sq - hi.astype(F32)).astype(BF16)
        parts = [slice(j * group, (j + 1) * group) for j in range(steps)]
        mean = mm(
            jnp.concatenate(
                [jnp.concatenate([hi[:, p], lo[:, p]], axis=1) for p in parts], axis=0
            ),
            twice,
        ) * (1.0 / HEAD)
        for j, p in enumerate(parts):
            r = lax.rsqrt(mean[j * m : (j + 1) * m] + 1e-05) * scale
            into[at : at + m, p] = (a[:, p] * r).astype(BF16)

    def project(cells, at):
        unit(mm(cells, wqkv[:, width : 2 * width]), kbuf, at, 1.0)
        v = mm(cells, wqkv[:, 2 * width : 3 * width])
        vbuf[at : at + cells.shape[0], :] = v.astype(BF16)

    unit(mm(own[...], wqkv[:, 0:width]), qbuf, 0, 1.0 / 8.0)
    project(own[...], 0)

    loads[1].wait()
    s_lat, s_lon = shifts[0], shifts[1]
    total_keys = 2 * n + 2 * nook
    i = iota((1, total_keys), 1)
    in_own, in_vert, in_side = i < n, i < 2 * n, i < 2 * n + nook
    m = i - jnp.where(in_side, 2 * n, 2 * n + nook)
    row = jnp.where(in_vert, jnp.where(in_own, i, i - n) // cols, m // WIN)
    col = jnp.where(in_vert, i % cols, m % WIN)
    inside = in_own | (in_side & ~in_vert)
    key_row = jnp.where(inside, (row + s_lat) // WIN, jnp.where(row < s_lat, 0, 1))
    key_col = jnp.where(in_vert, (col + s_lon) // WIN, jnp.where(col < s_lon, 0, 2))
    gone = ~inside & (((row < s_lat) & (lat == 0)) | ((row >= s_lat) & (lat == n_lat - 1)))
    keyid = jnp.where(gone, -1, key_row * 4 + key_col)
    w = iota((n, 1), 0)
    same = (w // cols + s_lat) // WIN * 4 + (w % cols + s_lon) // WIN == keyid
    lane = iota((n, group), 1) // HEAD

    def attend(first, count, fresh):
        seen = same[:, first : first + count]
        for j in range(steps):
            lanes = slice(j * group, (j + 1) * group)
            qn = qbuf[:, lanes]
            stacked = jnp.concatenate(
                [jnp.where(lane == h, qn, jnp.zeros_like(qn)) for h in range(heads)], axis=0
            )
            scores = lax.dot_general(
                stacked, kbuf[first : first + count, lanes], (((1,), (1,)), ((), ())),
                preferred_element_type=F32,
            )
            e = []
            for h in range(heads):
                e.append(jnp.where(seen, jnp.exp(scores[h * n : (h + 1) * n]), 0.0))
                at = (j * heads + h) * n
                part = jnp.sum(e[h], axis=1, keepdims=True)
                denom[at : at + n, 0:1] = part if fresh else denom[at : at + n, 0:1] + part
            e = jnp.concatenate([v.astype(BF16) for v in e], axis=0)
            part = mm(e, vbuf[first : first + count, lanes])
            at = slice(j * heads * n, (j + 1) * heads * n)
            numer[at, :] = part if fresh else numer[at, :] + part

    attend(0, n, True)
    w = iota((n, 1), 0)
    v_at = w // cols
    vert_at = jnp.where(v_at < s_lat, REACH - s_lat + v_at, REACH + v_at - s_lat)
    vert_pick = onehot((n, 2 * edge), vert_at * cols + w % cols)

    @pl.when(has_up)
    def _():
        go_down.wait_recv()

    @pl.when(has_down)
    def _():
        go_up.wait_recv()

    project(mm(vert_pick, vertin[...]).astype(BF16), n)

    routes(n_lon, z, ids, info, place, 0)

    @pl.when(inner)
    def _():
        tell.wait_recv()

    far_z = jnp.where(inner, 3 - z, z)
    routes(n_lon, far_z, far_ids, far_info, place, 2 * slab)

    w = iota((nook, 1), 0)
    major, minor = w // WIN, w % WIN
    side_at = major * REACH + jnp.where(
        minor < s_lon, REACH - s_lon + minor, 2 * half + minor - s_lon
    )
    side0 = onehot((nook, 4 * half), side_at)
    side1 = onehot((nook, 4 * half), side_at + half)
    corn_at = jnp.where(major < s_lat, WIN - s_lat + major, WIN + major - s_lat)
    corn_pick = onehot((nook, 2 * nook), corn_at * WIN + minor)
    go_left.wait_recv()
    go_right.wait_recv()
    side[:, 0:lanes2] = mm(side0, sidein[...]).astype(BF16)
    side[:, lanes2:width] = mm(side1, sidein[...]).astype(BF16)
    corn_down = remote(side, cornin.at[pl.ds(0, nook)], cs.at[0], cr.at[0], down)
    corn_up = remote(side, cornin.at[pl.ds(nook, nook)], cs.at[1], cr.at[1], up)

    @pl.when(has_down)
    def _():
        corn_down.start()

    @pl.when(has_up)
    def _():
        corn_up.start()

    project(side[...], 2 * n)

    attend(n, n, False)

    @pl.when(has_up)
    def _():
        corn_down.wait_recv()

    @pl.when(has_down)
    def _():
        corn_up.wait_recv()

    project(mm(corn_pick, cornin[...]).astype(BF16), 2 * n + nook)

    loads[4].wait()
    attend(2 * n, 2 * nook, False)
    total = tok[...].astype(F32)
    for j in range(steps):
        lanes = slice(j * group, (j + 1) * group)
        at = j * heads * n
        num, den = numer[at : at + n, :], denom[at : at + n, 0:1]
        for h in range(1, heads):
            rows_h = slice(at + h * n, at + (h + 1) * n)
            num = jnp.where(lane == h, numer[rows_h, :], num)
            den = jnp.where(lane == h, denom[rows_h, 0:1], den)
        total = total + mm((num / den).astype(BF16), wo[lanes, :])

    mixed = total.astype(BF16)
    acc[...] = mixed.astype(F32)
    normed2[...] = rms_rows(mixed).astype(BF16)

    @pl.when(inner)
    def _():
        lend.start()

    @pl.when(~inner)
    def _():
        far[...] = normed2[...]

    def pack(cells, first):
        end = cells[:, WIDE:width]
        for t in range(3):
            lanes = slice(t * TAIL, (t + 1) * TAIL)
            both = jnp.concatenate([cells[:, lanes], end], axis=0)
            at = t * 4 * slab + first
            send[first : first + 2 * slab, lanes] = mm(place[at : at + 2 * slab, :], both).astype(BF16)

    def rows(g, j):
        return pl.ds(pl.multiple_of(g * slab + j * UNIT, UNIT), UNIT)

    def forth(g):
        return flip(z, jnp.where(inner & (g >= 2), 3 - g, g))

    def home(g):
        return flip(z, jnp.where(inner, jnp.where(g == 3, 0, g), jnp.where(g == 2, 1, g)))

    def begin(g):
        return jnp.where((g == 0) | (inner & (g == 3)), 1, 0)

    out1, out2 = (send, got, s1, r1, forth), (results, back, s2, r2, home)

    to_x = [x, (x + 1) % 2]

    def launch(out, g):
        src, dst, ssem, rsem, to_plane = out
        base = to_plane(g) * 2
        mine = dst.at[rows(g, here)]

        @pl.when(begin(g) == 0)
        def _():
            remote(src.at[rows(g, here)], mine, ssem.at[g], rsem.at[g], (lat, base + x)).start()

        @pl.when(begin(g) == 1)
        def _():
            pltpu.make_async_copy(src.at[rows(g, here)], mine, rsem.at[g]).start()

        for k in range(1, plane):
            la, xx = at_lat[k // 2], to_x[k % 2]
            remote(
                src.at[rows(g, la * 2 + xx)], mine, ssem.at[g], rsem.at[g], (la, base + xx)
            ).start()

    def whole(g):
        return pl.ds(pl.multiple_of(g * slab, slab), slab)

    def land(out, g):
        src, dst, ssem, rsem, to_plane = out
        pltpu.make_async_copy(src.at[whole(g)], dst.at[whole(g)], rsem.at[g]).wait()

    def drain(out, g):
        src, dst, ssem, rsem, to_plane = out

        @pl.when(begin(g) == 0)
        def _():
            pltpu.make_async_copy(src.at[whole(g)], dst.at[whole(g)], ssem.at[g]).wait()

        @pl.when(begin(g) == 1)
        def _():
            few = pl.ds(pl.multiple_of(g * slab, slab), slab - UNIT)
            pltpu.make_async_copy(src.at[few], dst.at[few], ssem.at[g]).wait()

    pack(normed2, 0)
    launch(out1, 1)
    launch(out1, 0)
    loads[5].wait()
    gates(normed2, router, info, comb, 0)

    @pl.when(inner)
    def _():
        lend.wait_recv()

    pack(far, 2 * slab)
    launch(out1, 3)
    launch(out1, 2)

    gates(far, router, far_info, comb, 2 * slab)

    half_rows = plane * MOST
    count = 2 * half_rows
    r = iota((count, 1), 0)
    slot = r // half_rows * MOST + r % MOST
    base = r % half_rows // MOST * UNIT
    pick = onehot((count, slab), base + slot)
    tails = [
        onehot((count, slab), jnp.where(slot % 3 == t, base + MAIN + slot // 3, -1))
        for t in range(3)
    ]
    r = iota((1, count), 1)
    slot = r // half_rows * MOST + r % MOST
    base = r % half_rows // MOST * UNIT
    target = iota((slab, count), 0)
    put = hit(target == base + slot).astype(BF16)
    put_tails = [
        hit(target == jnp.where(slot % 3 == t, base + MAIN + slot // 3, -1)).astype(BF16)
        for t in range(3)
    ]
    for load in loads[6:]:
        load.wait()

    def experts(i, c):
        g = i + 1 - 2 * (i % 2)
        land(out1, g)
        at = pl.ds(pl.multiple_of(g * slab, slab), slab)
        wide = mm(pick, got[at, :]).astype(BF16)
        end = mm(tails[0], got[at, 0:TAIL])
        for t in range(1, 3):
            end = end + mm(tails[t], got[at, t * TAIL : (t + 1) * TAIL])
        cells = jnp.concatenate([wide, end.astype(BF16)], axis=1)
        parts = []
        for e in range(2):
            xe = cells[e * half_rows : (e + 1) * half_rows]
            gate = mm(xe, wg[:, e * FF : (e + 1) * FF])
            upper = mm(xe, wu[:, e * FF : (e + 1) * FF])
            hidden = (jax.nn.silu(gate) * upper).astype(BF16)
            parts.append(mm(hidden, wd[e * FF : (e + 1) * FF, :]).astype(BF16))
        part = jnp.concatenate(parts, axis=0)
        for t in range(3):
            lanes = slice(t * TAIL, (t + 1) * TAIL)
            results[at, lanes] = (
                mm(put, part[:, lanes]) + mm(put_tails[t], part[:, WIDE:width])
            ).astype(BF16)
        launch(out2, g)
        return c

    lax.fori_loop(0, 4, experts, 0)


    def gather(g, into):
        land(out2, g)
        at = slice(g * slab, (g + 1) * slab)
        for t in range(3):
            lanes = slice(t * TAIL, (t + 1) * TAIL)
            s = mm(comb[t * 4 * n : (t + 1) * 4 * n, at], back[at, lanes])
            into[:, lanes] += s[0:n] + s[n : 2 * n]
            into[:, WIDE:width] += s[2 * n : 3 * n] + s[3 * n : 4 * n]

    @pl.when(inner)
    def _():
        far_acc[...] = jnp.zeros_like(far_acc)
        gather(3, far_acc)
        gather(2, far_acc)
        share[...] = far_acc[...].astype(BF16)
        give.start()

    gather(1, acc)
    gather(0, acc)

    @pl.when(~inner)
    def _():
        gather(3, acc)
        gather(2, acc)
        out_ref[...] = acc[...].astype(BF16)

    @pl.when(inner)
    def _():
        give.wait_recv()
        out_ref[...] = (acc[...] + shared[...].astype(F32)).astype(BF16)
        tell.wait_send()
        lend.wait_send()
        give.wait_send()

    go_left.wait_send()
    go_right.wait_send()

    @pl.when(has_down)
    def _():
        go_down.wait_send()
        corn_down.wait_send()

    @pl.when(has_up)
    def _():
        go_up.wait_send()
        corn_up.wait_send()

    for g in range(4):
        drain(out1, g)
        drain(out2, g)


def routes(n_lon, z, ids, info, place, first):
    n = ids.shape[1]
    r0, r1 = ids[0:1, :], ids[1:2, :]
    ia, ib = iota((n, n), 0), iota((n, n), 1)

    def column(row):
        return jnp.sum(jnp.where(ia == ib, row.astype(F32), 0.0), axis=1, keepdims=True)

    c0, c1 = column(r0).astype(jnp.int32), column(r1).astype(jnp.int32)
    rank0c = jnp.sum(hit((c0 == r0) & (ib < ia)), axis=1, keepdims=True)
    rank1c = jnp.sum(hit(c1 == r0) + hit((c1 == r1) & (ib < ia)), axis=1, keepdims=True)
    rank0r = jnp.sum(hit((c0 == r0) & (ia < ib)), axis=0, keepdims=True)
    rank1r = jnp.sum(hit(c0 == r1) + hit((c1 == r1) & (ia < ib)), axis=0, keepdims=True)

    def places(e, rank):
        slot = e % 2 * MOST + rank.astype(jnp.int32)
        device = e // 2
        at_lat, at_lon = device // n_lon, device % n_lon
        base = (flip(at_lon // 2, z) * (place.shape[0] // 12 // UNIT) + at_lat * 2 + at_lon % 2) * UNIT
        return base + slot, base + MAIN + slot // 3, slot % 3

    m0, t0, q0 = places(c0, rank0c)
    m1, t1, q1 = places(c1, rank1c)
    col = iota(info.shape, 1)
    table = jnp.zeros(info.shape, F32)
    for i, v in enumerate((m0, t0, q0, m1, t1, q1, c0, c1)):
        table = jnp.where(col == i, v.astype(F32), table)
    info[...] = table
    m0, t0, q0 = places(r0, rank0r)
    m1, t1, q1 = places(r1, rank1r)
    total = place.shape[0] // 3
    count = total // 2
    row = iota((count, n), 0) + first
    main = (hit(row == m0) + hit(row == m1)).astype(BF16)
    for t in range(3):
        rows = slice(t * total + first, t * total + first + count)
        place[rows, 0:n] = main
        place[rows, n : 2 * n] = (
            hit((row == t0) & (q0 == t)) + hit((row == t1) & (q1 == t))
        ).astype(BF16)


def gates(cells, router, info, comb, begin):
    logits = lax.dot_general(
        cells[...], router[...], (((1,), (1,)), ((), ())), preferred_element_type=F32
    )
    n = logits.shape[0]
    eid = iota(logits.shape, 1).astype(F32)
    m0, t0, q0, m1, t1, q1, c0, c1 = (info[:, i : i + 1] for i in range(8))
    s0 = jax.nn.sigmoid(jnp.sum(jnp.where(eid == c0, logits, 0.0), axis=1, keepdims=True))
    s1 = jax.nn.sigmoid(jnp.sum(jnp.where(eid == c1, logits, 0.0), axis=1, keepdims=True))
    g0 = s0 / (s0 + s1)
    g1 = s1 / (s0 + s1)
    count = comb.shape[1] // 2
    at = (iota((n, count), 1) + begin).astype(F32)

    def keep(first, a):
        hi = a.astype(BF16)
        comb[first : first + n, begin : begin + count] = hi
        comb[first + n : first + 2 * n, begin : begin + count] = (a - hi.astype(F32)).astype(BF16)

    main = jnp.where(at == m0, g0, 0.0) + jnp.where(at == m1, g1, 0.0)
    for t in range(3):
        keep(t * 4 * n, main)
        keep(
            t * 4 * n + 2 * n,
            jnp.where((at == t0) & (q0 == t), g0, 0.0) + jnp.where((at == t1) & (q1 == t), g1, 0.0),
        )


def layer_block(n_lat, n_lon, shifts, tok, router, ids, w_qkv, w_out, w_gate, w_up, w_down):
    n, width = tok.shape
    total = n_lat * n_lon * UNIT
    keys = 2 * n + 2 * WIN * WIN
    hbm = pl.BlockSpec(memory_space=pl.ANY)
    dma = pltpu.SemaphoreType.DMA

    def vmem(*shape, dtype=BF16):
        return pltpu.VMEM(shape, dtype)

    return pl.pallas_call(
        functools.partial(layer_kernel, n_lat, n_lon),
        out_shape=pltpu.VMEM((n, width), BF16),
        in_specs=[hbm] * 9,
        out_specs=pl.BlockSpec(memory_space=pltpu.VMEM),
        scratch_shapes=[
            pltpu.SMEM((2,), jnp.int32),
            vmem(n, width),
            vmem(router.shape[1], width),
            vmem(TOP, n, dtype=jnp.int32),
            vmem(*w_qkv.shape),
            vmem(*w_out.shape),
            vmem(*w_gate.shape),
            vmem(*w_up.shape),
            vmem(*w_down.shape),
            vmem(n, width),
            vmem(4 * WIN * REACH, width // 2),
            vmem(4 * WIN * REACH, width // 2),
            vmem(2 * REACH * (n // WIN), width),
            vmem(WIN * WIN, width),
            vmem(2 * WIN * WIN, width),
            vmem(n, width),
            vmem(keys, width),
            vmem(keys, width),
            vmem(width // HEAD * n, width // 4, dtype=F32),
            vmem(width // HEAD * n, 128, dtype=F32),
            vmem(3 * total, 2 * n),
            vmem(12 * n, total),
            vmem(n, 128, dtype=F32),
            vmem(n, width),
            vmem(n, width, dtype=F32),
            vmem(total, WIDE),
            vmem(total, WIDE),
            vmem(total, WIDE),
            vmem(total, WIDE),
            vmem(TOP, n, dtype=jnp.int32),
            vmem(n, 128, dtype=F32),
            vmem(n, width),
            vmem(n, width, dtype=F32),
            vmem(n, width),
            vmem(n, width),
            dma((9,)),
            dma((2,)), dma((2,)), dma((2,)), dma((2,)), dma((2,)), dma((2,)),
            dma((3,)), dma((3,)),
            dma((4,)), dma((4,)), dma((4,)), dma((4,)),
        ],
        compiler_params=pltpu.CompilerParams(
            collective_id=1, has_side_effects=True, vmem_limit_bytes=56 * 2**20
        ),
    )(shifts, tok, router.T, ids.T, w_qkv, w_out, w_gate, w_up, w_down)


def body(tokens, shifts, w_qkv, w_out, router, expert_ids, w_gate, w_up, w_down):
    n_lat = lax.axis_size("lat")
    n_lon = lax.axis_size("lon")
    devices = n_lat * n_lon
    rows, cols, width = tokens.shape
    ids = expert_ids.reshape(-1, TOP)
    tok = tokens.reshape(-1, width)
    if (n_lat, n_lon) == (4, 8) and w_gate.shape[1] == 2 * FF:
        out = layer_block(
            n_lat, n_lon, shifts, tok, router, ids, w_qkv, w_out, w_gate, w_up, w_down
        )
        return out.reshape(rows, cols, width)
    mixed, normed2 = front_block(n_lat, n_lon, shifts, tok, w_qkv, w_out)
    return general(mixed, normed2, router, ids, w_gate, w_up, w_down, devices, rows, cols)


def general(mixed, normed2, router, ids, w_gate, w_up, w_down, devices, rows, cols):
    width = mixed.shape[1]
    logits = jnp.dot(normed2, router, preferred_element_type=jnp.float32)
    experts = router.shape[1]
    expert_iota = jnp.arange(experts, dtype=jnp.int32)
    picks = ids[:, :, None] == expert_iota[None, None, :]
    chosen = jnp.sum(jnp.where(picks, logits[:, None, :], 0.0), axis=-1)
    sig = jax.nn.sigmoid(chosen)
    gates = sig / jnp.sum(sig, axis=1, keepdims=True)
    flat = ids.reshape(-1)
    order = jnp.arange(flat.shape[0], dtype=jnp.int32)
    earlier = (flat[:, None] == flat[None, :]) & (order[None, :] < order[:, None])
    rank = jnp.sum(earlier.astype(jnp.int32), axis=1)
    share = w_gate.shape[1]
    piece = min(FF, share)
    repl = FF // piece
    group = share // piece
    most = MOST
    cap = group * most
    token_of = jnp.arange(flat.shape[0], dtype=jnp.int32) // TOP
    slot = flat % group * most + rank
    slot_index = jnp.stack(
        [(flat // group * repl + copy) * cap + slot for copy in range(repl)], axis=0
    )
    routed = normed2[token_of]
    send = (
        jnp.zeros((devices * cap, width), jnp.bfloat16)
        .at[slot_index.reshape(-1)]
        .set(jnp.tile(routed, (repl, 1)))
    )
    send = send.reshape(devices, group, most, width)
    received = lax.all_to_all(send, ("lat", "lon"), split_axis=0, concat_axis=0, tiled=True)
    results = []
    for local in range(group):
        block = received[:, local].reshape(-1, width)
        gate = jnp.dot(
            block,
            w_gate[:, local * piece : (local + 1) * piece],
            preferred_element_type=jnp.float32,
        )
        upper = jnp.dot(
            block, w_up[:, local * piece : (local + 1) * piece], preferred_element_type=jnp.float32
        )
        hidden = (jax.nn.silu(gate) * upper).astype(jnp.bfloat16)
        part = jnp.dot(
            hidden, w_down[local * piece : (local + 1) * piece], preferred_element_type=jnp.float32
        ).astype(jnp.bfloat16)
        results.append(part.reshape(received.shape[0], received.shape[2], width))
    back = lax.all_to_all(
        jnp.stack(results, axis=1), ("lat", "lon"), split_axis=0, concat_axis=0, tiled=True
    )
    back_flat = back.reshape(devices * cap, width)
    combined = jnp.zeros((flat.shape[0], width), jnp.float32)
    for copy in range(repl):
        combined = combined + back_flat[slot_index[copy]].astype(jnp.float32)
    combined = combined.reshape(-1, TOP, width)
    moe = jnp.sum(gates[:, :, None] * combined, axis=1)
    layer_out = (mixed.astype(jnp.float32) + moe).astype(jnp.bfloat16)
    return layer_out.reshape(rows, cols, width)


def solution(mesh):
    placed = (
        P("lat", "lon", None),
        P(),
        P(),
        P(),
        P(),
        P("lat", "lon", None, None),
        P(None, ("lat", "lon")),
        P(None, ("lat", "lon")),
        P(("lat", "lon"), None),
    )
    return jax.shard_map(
        body, mesh=mesh, in_specs=placed, out_specs=P("lat", "lon", None), check_vma=False
    )
```

```python
import functools

import jax
import jax.numpy as jnp
import numpy as np
from jax import lax
from jax.experimental import pallas as pl
from jax.experimental.pallas import tpu as pltpu
from jax.sharding import PartitionSpec as P

HEAD = 64
FF = 1024
TOP = 2
WIN = 8
MOST = 6
UNIT = 16
MAIN = 12
WIDE = 768
TAIL = 256
F32 = jnp.float32
BF16 = jnp.bfloat16


def rms_rows(x):
    xf = x.astype(jnp.float32)
    return xf * lax.rsqrt(jnp.mean(xf * xf, axis=-1, keepdims=True) + 1e-05)


def mm(a, b):
    return jnp.dot(a, b, preferred_element_type=F32)


def hit(cond):
    return jnp.where(cond, 1.0, 0.0)


def head_norm(x, ones):
    xf = x.astype(F32)
    sq = xf * xf
    hi = sq.astype(BF16)
    lo = (sq - hi.astype(F32)).astype(BF16)
    mean = (mm(hi, ones) + mm(lo, ones)) * (1.0 / HEAD)
    return xf * lax.rsqrt(mean + 1e-05)


REACH = WIN - 1


def front_kernel(
    n_lat, n_lon, shifts_ref, tok_ref, wqkv_hbm, wo_hbm, mixed_ref, send_ref,
    tall, tosend, side, wqkv, wo, qbuf, kbuf, vbuf, w_sem, vs, vr, hs, hr
):
    lat, lon = lax.axis_index("lat"), lax.axis_index("lon")
    loads = [
        pltpu.make_async_copy(wqkv_hbm, wqkv, w_sem.at[0]),
        pltpu.make_async_copy(wo_hbm, wo, w_sem.at[1]),
    ]
    for load in loads:
        load.start()
    n, width = tok_ref.shape
    cols = n // WIN
    left = (lat, lax.rem(lon + n_lon - 1, n_lon))
    right = (lat, lax.rem(lon + 1, n_lon))
    up, down = (lat - 1, lon), (lat + 1, lon)
    has_up, has_down = lat > 0, lat < n_lat - 1
    mesh_id = pl.DeviceIdType.MESH
    barrier = pltpu.get_barrier_semaphore()
    around = (
        left, right, (lax.rem(lat + n_lat - 1, n_lat), lon), (lax.rem(lat + 1, n_lat), lon)
    )
    for other in around:
        pl.semaphore_signal(barrier, inc=1, device_id=other, device_id_type=mesh_id)

    tall[n : 2 * n, :] = rms_rows(tok_ref[...]).astype(BF16)
    tall[0:cols, :] = jnp.zeros((cols, width), BF16)
    tall[3 * n - cols : 3 * n, :] = jnp.zeros((cols, width), BF16)
    edge = REACH * cols

    @pl.when(lat == 0)
    def _():
        tall[cols:n, :] = jnp.zeros((edge, width), BF16)

    @pl.when(lat == n_lat - 1)
    def _():
        tall[2 * n : 2 * n + edge, :] = jnp.zeros((edge, width), BF16)

    pl.semaphore_wait(barrier, len(around))

    def remote(src, dst, ssem, rsem, to):
        return pltpu.make_async_remote_copy(
            src_ref=src, dst_ref=dst, send_sem=ssem, recv_sem=rsem,
            device_id=to, device_id_type=mesh_id,
        )

    above, below = tall.at[pl.ds(cols, edge)], tall.at[pl.ds(2 * n, edge)]
    go_down = remote(tall.at[pl.ds(n + cols, edge)], above, vs.at[0], vr.at[0], down)
    go_up = remote(tall.at[pl.ds(n, edge)], below, vs.at[1], vr.at[1], up)

    @pl.when(has_down)
    def _():
        go_down.start()

    @pl.when(has_up)
    def _():
        go_up.start()

    s_lat, s_lon = shifts_ref[0], shifts_ref[1]
    sides = 2 * WIN * REACH
    out_row = lax.broadcasted_iota(jnp.int32, (2 * sides, 1), 0)
    local = jnp.where(out_row >= sides, out_row - sides, out_row)
    at = local // REACH * cols + local % REACH + jnp.where(out_row >= sides, cols - REACH, 0)
    start = (WIN - s_lat) * cols
    pick = hit(lax.broadcasted_iota(jnp.int32, (2 * sides, 3 * n), 1) == at + start).astype(BF16)

    @pl.when(has_up)
    def _():
        go_down.wait_recv()

    @pl.when(has_down)
    def _():
        go_up.wait_recv()

    everything = tall[...]
    tosend[...] = mm(pick, everything).astype(BF16)
    go_left = remote(
        tosend.at[pl.ds(0, sides)], side.at[pl.ds(sides, sides)], hs.at[0], hr.at[0], left
    )
    go_right = remote(
        tosend.at[pl.ds(sides, sides)], side.at[pl.ds(0, sides)], hs.at[1], hr.at[1], right
    )
    go_left.start()
    go_right.start()
    there = lax.broadcasted_iota(jnp.int32, (2 * n, 3 * n), 0) + start
    shift = hit(lax.broadcasted_iota(jnp.int32, (2 * n, 3 * n), 1) == there).astype(BF16)
    keys = mm(shift, everything).astype(BF16)

    steps = 4
    group = width // steps
    heads = group // HEAD
    ra = lax.broadcasted_iota(jnp.int32, (group, group), 0) // HEAD
    rb = lax.broadcasted_iota(jnp.int32, (group, group), 1) // HEAD
    ones = hit(ra == rb).astype(BF16)
    own = tall[n : 2 * n, :]
    loads[0].wait()

    def project(cells, first, count):
        for j in range(steps):
            lanes = slice(j * group, (j + 1) * group)
            k = mm(cells, wqkv[:, width + j * group : width + (j + 1) * group]).astype(BF16)
            kbuf[first : first + count, lanes] = head_norm(k, ones).astype(BF16)
            v = mm(cells, wqkv[:, 2 * width + j * group : 2 * width + (j + 1) * group])
            vbuf[first : first + count, lanes] = v.astype(BF16)

    for j in range(steps):
        lanes = slice(j * group, (j + 1) * group)
        q = mm(own, wqkv[:, lanes]).astype(BF16)
        qbuf[:, lanes] = (head_norm(q, ones) * (1.0 / 8.0)).astype(BF16)
    project(keys, 0, 2 * n)

    total_keys = 2 * n + 2 * sides
    i = lax.broadcasted_iota(jnp.int32, (1, total_keys), 1)
    m = jnp.where(i < 2 * n + sides, i - 2 * n, i - 2 * n - sides)
    inner = i < 2 * n
    r_of = jnp.where(inner, i // cols, m // REACH)
    c_of = jnp.where(
        inner, i % cols, m % REACH + jnp.where(i < 2 * n + sides, -REACH, cols)
    )
    at_row = lat * WIN - s_lat + r_of
    valid = (at_row >= 0) & (at_row < WIN * n_lat)
    keyid = jnp.where(valid, (r_of // WIN) * 4 + (c_of + s_lon + WIN) // WIN, -1)
    qi = lax.broadcasted_iota(jnp.int32, (n, 1), 0)
    qid = (qi // cols + s_lat) // WIN * 4 + (qi % cols + s_lon + WIN) // WIN
    same = qid == keyid
    lane = lax.broadcasted_iota(jnp.int32, (n, group), 1) // HEAD

    go_left.wait_recv()
    go_right.wait_recv()
    project(side[...], 2 * n, 2 * sides)
    loads[1].wait()
    acc = tok_ref[...].astype(F32)
    for j in range(steps):
        lanes = slice(j * group, (j + 1) * group)
        qn = qbuf[:, lanes]
        stacked = jnp.concatenate(
            [jnp.where(lane == h, qn, jnp.zeros_like(qn)) for h in range(heads)], axis=0
        )
        scores = lax.dot_general(
            stacked, kbuf[:, lanes], (((1,), (1,)), ((), ())), preferred_element_type=F32
        )
        weights = []
        for h in range(heads):
            e = jnp.where(same, jnp.exp(scores[h * n : (h + 1) * n]), 0.0)
            total = jnp.sum(e, axis=1, keepdims=True)
            weights.append((e * (1.0 / total)).astype(BF16))
        mixedv = mm(jnp.concatenate(weights, axis=0), vbuf[:, lanes])
        att = jnp.zeros((n, group), F32)
        for h in range(heads):
            att = jnp.where(lane == h, mixedv[h * n : (h + 1) * n], att)
        acc = acc + mm(att.astype(BF16), wo[lanes, :])

    mixed = acc.astype(BF16)
    mixed_ref[...] = mixed
    normed2 = rms_rows(mixed).astype(BF16)
    send_ref[...] = normed2

    go_left.wait_send()
    go_right.wait_send()

    @pl.when(has_down)
    def _():
        go_down.wait_send()

    @pl.when(has_up)
    def _():
        go_up.wait_send()


def front_block(n_lat, n_lon, shifts, tok, w_qkv, w_out):
    n, width = tok.shape
    sides = 2 * 2 * WIN * REACH
    vm = pl.BlockSpec(memory_space=pltpu.VMEM)
    hbm = pl.BlockSpec(memory_space=pl.ANY)
    dma = pltpu.SemaphoreType.DMA
    keys = 2 * n + sides
    return pl.pallas_call(
        functools.partial(front_kernel, n_lat, n_lon),
        in_specs=[pl.BlockSpec(memory_space=pltpu.SMEM), vm, hbm, hbm],
        out_specs=[vm, vm],
        out_shape=[jax.ShapeDtypeStruct((n, width), BF16)] * 2,
        scratch_shapes=[
            pltpu.VMEM((3 * n, width), BF16),
            pltpu.VMEM((sides, width), BF16),
            pltpu.VMEM((sides, width), BF16),
            pltpu.VMEM(w_qkv.shape, BF16),
            pltpu.VMEM(w_out.shape, BF16),
            pltpu.VMEM((n, width), BF16),
            pltpu.VMEM((keys, width), BF16),
            pltpu.VMEM((keys, width), BF16),
            dma((2,)), dma((2,)), dma((2,)), dma((2,)), dma((2,)),
        ],
        compiler_params=pltpu.CompilerParams(
            collective_id=2, has_side_effects=True, vmem_limit_bytes=40 * 2**20
        ),
    )(shifts, tok, w_qkv, w_out)


def iota(shape, axis):
    return lax.broadcasted_iota(jnp.int32, shape, axis)


def onehot(shape, target):
    return hit(iota(shape, 1) == target).astype(BF16)


def flip(z, g):
    return 2 * ((z // 2 + g // 2) % 2) + (z + g) % 2


def layer_kernel(
    n_lat, n_lon, shifts_hbm, tok_hbm, router_hbm, ids_hbm, wqkv_hbm, wo_hbm, wg_hbm, wu_hbm,
    wd_hbm, out_ref, shifts, tok, router, ids, wqkv, wo, wg, wu, wd, own, sideout, sidein, vertin,
    side, cornin, qbuf, kbuf, vbuf, numer, denom, place, comb, info, normed2, acc, send, got, results, back,
    far_ids, far_info, far, far_acc, share, shared, w_sem, vs, vr, hs, hr, cs, cr, ms, mr, s1, r1, s2, r2
):
    lat, lon = lax.axis_index("lat"), lax.axis_index("lon")
    z, x = lon // 2, lon % 2
    plane = 2 * n_lat
    slab = plane * UNIT
    here = lat * 2 + x
    inner = (z + 1) // 2 % 2 == 1
    mirror = (lat, (3 - z) * 2 + x)
    loads = [
        pltpu.make_async_copy(src, dst, w_sem.at[i])
        for i, (src, dst) in enumerate((
            (tok_hbm, tok), (shifts_hbm, shifts), (ids_hbm, ids), (wqkv_hbm, wqkv),
            (wo_hbm, wo), (router_hbm, router), (wg_hbm, wg), (wu_hbm, wu), (wd_hbm, wd),
        ))
    ]
    for load in loads[:6]:
        load.start()
    n, width = tok.shape
    cols = n // WIN
    mesh_id = pl.DeviceIdType.MESH
    left = (lat, lax.rem(lon + n_lon - 1, n_lon))
    right = (lat, lax.rem(lon + 1, n_lon))
    up, down = (lat - 1, lon), (lat + 1, lon)
    has_up, has_down = lat > 0, lat < n_lat - 1

    barrier = pltpu.get_barrier_semaphore()
    devices = n_lat * n_lon

    at_lat = [(lat + k) % n_lat for k in range(n_lat)]
    at_lon = [(lon + k) % n_lon for k in range(n_lon)]
    around = [(0, 1), (0, n_lon - 1), (1, 0), (n_lat - 1, 0)]
    others = [(a, b) for a in range(n_lat) for b in range(n_lon)]
    for a, b in around + [o for o in others if o not in around and o != (0, 0)]:
        pl.semaphore_signal(
            barrier, inc=1, device_id=(at_lat[a], at_lon[b]), device_id_type=mesh_id
        )

    edge = REACH * cols
    nook = WIN * WIN

    @pl.when(lat == 0)
    def _():
        vertin[0:edge, :] = jnp.zeros((edge, width), BF16)
        cornin[0:nook, :] = jnp.zeros((nook, width), BF16)

    @pl.when(lat == n_lat - 1)
    def _():
        vertin[edge : 2 * edge, :] = jnp.zeros((edge, width), BF16)
        cornin[nook : 2 * nook, :] = jnp.zeros((nook, width), BF16)

    half = WIN * REACH
    lanes2 = width // 2
    r = iota((4 * half, 1), 0)
    within = r % half
    cell = within // REACH * cols + within % REACH + jnp.where(r >= 2 * half, cols - REACH, 0)
    second = r // half % 2 == 1
    pick0 = onehot((4 * half, n), jnp.where(second, -1, cell))
    pick1 = onehot((4 * half, n), jnp.where(second, cell, -1))
    loads[0].wait()
    own[...] = rms_rows(tok[...]).astype(BF16)
    sideout[...] = (
        mm(pick0, own[:, 0:lanes2]) + mm(pick1, own[:, lanes2:width])
    ).astype(BF16)
    pl.semaphore_wait(barrier, devices - 1)

    def remote(src, dst, ssem, rsem, to):
        return pltpu.make_async_remote_copy(
            src_ref=src, dst_ref=dst, send_sem=ssem, recv_sem=rsem,
            device_id=to, device_id_type=mesh_id,
        )

    first, last = pl.ds(0, 2 * half), pl.ds(2 * half, 2 * half)
    go_left = remote(sideout.at[first], sidein.at[last], hs.at[0], hr.at[0], left)
    go_right = remote(sideout.at[last], sidein.at[first], hs.at[1], hr.at[1], right)
    go_left.start()
    go_right.start()
    go_down = remote(
        own.at[pl.ds(n - edge, edge)], vertin.at[pl.ds(0, edge)], vs.at[0], vr.at[0], down
    )
    go_up = remote(own.at[pl.ds(0, edge)], vertin.at[pl.ds(edge, edge)], vs.at[1], vr.at[1], up)

    @pl.when(has_down)
    def _():
        go_down.start()

    @pl.when(has_up)
    def _():
        go_up.start()

    tell = remote(ids, far_ids, ms.at[0], mr.at[0], mirror)
    lend = remote(normed2, far, ms.at[1], mr.at[1], mirror)
    give = remote(share, shared, ms.at[2], mr.at[2], mirror)
    loads[2].wait()

    @pl.when(inner)
    def _():
        tell.start()

    @pl.when(~inner)
    def _():
        far_ids[...] = ids[...]

    steps = 4
    group = width // steps
    heads = group // HEAD
    ones = hit(iota((group, group), 0) // HEAD == iota((group, group), 1) // HEAD).astype(BF16)
    loads[3].wait()
    for load in loads[6:]:
        load.start()

    twice = jnp.concatenate([ones, ones], axis=0)

    def unit(a, into, at, scale):
        m = a.shape[0]
        a = a.astype(BF16).astype(F32)
        sq = a * a
        hi = sq.astype(BF16)
        lo = (sq - hi.astype(F32)).astype(BF16)
        parts = [slice(j * group, (j + 1) * group) for j in range(steps)]
        mean = mm(
            jnp.concatenate(
                [jnp.concatenate([hi[:, p], lo[:, p]], axis=1) for p in parts], axis=0
            ),
            twice,
        ) * (1.0 / HEAD)
        for j, p in enumerate(parts):
            r = lax.rsqrt(mean[j * m : (j + 1) * m] + 1e-05) * scale
            into[at : at + m, p] = (a[:, p] * r).astype(BF16)

    def project(cells, at):
        unit(mm(cells, wqkv[:, width : 2 * width]), kbuf, at, 1.0)
        v = mm(cells, wqkv[:, 2 * width : 3 * width])
        vbuf[at : at + cells.shape[0], :] = v.astype(BF16)

    unit(mm(own[...], wqkv[:, 0:width]), qbuf, 0, 1.0 / 8.0)
    project(own[...], 0)

    loads[1].wait()
    s_lat, s_lon = shifts[0], shifts[1]
    total_keys = 2 * n + 2 * nook
    i = iota((1, total_keys), 1)
    in_own, in_vert, in_side = i < n, i < 2 * n, i < 2 * n + nook
    m = i - jnp.where(in_side, 2 * n, 2 * n + nook)
    row = jnp.where(in_vert, jnp.where(in_own, i, i - n) // cols, m // WIN)
    col = jnp.where(in_vert, i % cols, m % WIN)
    inside = in_own | (in_side & ~in_vert)
    key_row = jnp.where(inside, (row + s_lat) // WIN, jnp.where(row < s_lat, 0, 1))
    key_col = jnp.where(in_vert, (col + s_lon) // WIN, jnp.where(col < s_lon, 0, 2))
    gone = ~inside & (((row < s_lat) & (lat == 0)) | ((row >= s_lat) & (lat == n_lat - 1)))
    keyid = jnp.where(gone, -1, key_row * 4 + key_col)
    w = iota((n, 1), 0)
    same = (w // cols + s_lat) // WIN * 4 + (w % cols + s_lon) // WIN == keyid
    lane = iota((n, group), 1) // HEAD

    def attend(first, count, fresh):
        seen = same[:, first : first + count]
        for j in range(steps):
            lanes = slice(j * group, (j + 1) * group)
            qn = qbuf[:, lanes]
            stacked = jnp.concatenate(
                [jnp.where(lane == h, qn, jnp.zeros_like(qn)) for h in range(heads)], axis=0
            )
            scores = lax.dot_general(
                stacked, kbuf[first : first + count, lanes], (((1,), (1,)), ((), ())),
                preferred_element_type=F32,
            )
            e = []
            for h in range(heads):
                e.append(jnp.where(seen, jnp.exp(scores[h * n : (h + 1) * n]), 0.0))
                at = (j * heads + h) * n
                part = jnp.sum(e[h], axis=1, keepdims=True)
                denom[at : at + n, 0:1] = part if fresh else denom[at : at + n, 0:1] + part
            e = jnp.concatenate([v.astype(BF16) for v in e], axis=0)
            part = mm(e, vbuf[first : first + count, lanes])
            at = slice(j * heads * n, (j + 1) * heads * n)
            numer[at, :] = part if fresh else numer[at, :] + part

    attend(0, n, True)
    w = iota((n, 1), 0)
    v_at = w // cols
    vert_at = jnp.where(v_at < s_lat, REACH - s_lat + v_at, REACH + v_at - s_lat)
    vert_pick = onehot((n, 2 * edge), vert_at * cols + w % cols)

    @pl.when(has_up)
    def _():
        go_down.wait_recv()

    @pl.when(has_down)
    def _():
        go_up.wait_recv()

    project(mm(vert_pick, vertin[...]).astype(BF16), n)

    routes(n_lon, z, ids, info, place, 0)

    @pl.when(inner)
    def _():
        tell.wait_recv()

    far_z = jnp.where(inner, 3 - z, z)
    routes(n_lon, far_z, far_ids, far_info, place, 2 * slab)

    w = iota((nook, 1), 0)
    major, minor = w // WIN, w % WIN
    side_at = major * REACH + jnp.where(
        minor < s_lon, REACH - s_lon + minor, 2 * half + minor - s_lon
    )
    side0 = onehot((nook, 4 * half), side_at)
    side1 = onehot((nook, 4 * half), side_at + half)
    corn_at = jnp.where(major < s_lat, WIN - s_lat + major, WIN + major - s_lat)
    corn_pick = onehot((nook, 2 * nook), corn_at * WIN + minor)
    go_left.wait_recv()
    go_right.wait_recv()
    side[:, 0:lanes2] = mm(side0, sidein[...]).astype(BF16)
    side[:, lanes2:width] = mm(side1, sidein[...]).astype(BF16)
    corn_down = remote(side, cornin.at[pl.ds(0, nook)], cs.at[0], cr.at[0], down)
    corn_up = remote(side, cornin.at[pl.ds(nook, nook)], cs.at[1], cr.at[1], up)

    @pl.when(has_down)
    def _():
        corn_down.start()

    @pl.when(has_up)
    def _():
        corn_up.start()


    attend(n, n, False)

    @pl.when(has_up)
    def _():
        corn_down.wait_recv()

    @pl.when(has_down)
    def _():
        corn_up.wait_recv()

    corners = mm(corn_pick, cornin[...]).astype(BF16)
    project(jnp.concatenate([side[...], corners], axis=0), 2 * n)

    loads[4].wait()
    attend(2 * n, 2 * nook, False)
    total = tok[...].astype(F32)
    for j in range(steps):
        lanes = slice(j * group, (j + 1) * group)
        at = j * heads * n
        num, den = numer[at : at + n, :], denom[at : at + n, 0:1]
        for h in range(1, heads):
            rows_h = slice(at + h * n, at + (h + 1) * n)
            num = jnp.where(lane == h, numer[rows_h, :], num)
            den = jnp.where(lane == h, denom[rows_h, 0:1], den)
        total = total + mm((num / den).astype(BF16), wo[lanes, :])

    mixed = total.astype(BF16)
    acc[...] = mixed.astype(F32)
    normed2[...] = rms_rows(mixed).astype(BF16)

    @pl.when(inner)
    def _():
        lend.start()

    @pl.when(~inner)
    def _():
        far[...] = normed2[...]

    def pack(cells, first):
        end = cells[:, WIDE:width]
        for t in range(3):
            lanes = slice(t * TAIL, (t + 1) * TAIL)
            both = jnp.concatenate([cells[:, lanes], end], axis=0)
            at = t * 4 * slab + first
            send[first : first + 2 * slab, lanes] = mm(place[at : at + 2 * slab, :], both).astype(BF16)

    def rows(g, j):
        return pl.ds(pl.multiple_of(g * slab + j * UNIT, UNIT), UNIT)

    def forth(g):
        return flip(z, jnp.where(inner & (g >= 2), 3 - g, g))

    def home(g):
        return flip(z, jnp.where(inner, jnp.where(g == 3, 0, g), jnp.where(g == 2, 1, g)))

    def begin(g):
        return jnp.where((g == 0) | (inner & (g == 3)), 1, 0)

    out1, out2 = (send, got, s1, r1, forth), (results, back, s2, r2, home)

    to_x = [x, (x + 1) % 2]

    def launch(out, g):
        src, dst, ssem, rsem, to_plane = out
        base = to_plane(g) * 2
        mine = dst.at[rows(g, here)]

        @pl.when(begin(g) == 0)
        def _():
            remote(src.at[rows(g, here)], mine, ssem.at[g], rsem.at[g], (lat, base + x)).start()

        @pl.when(begin(g) == 1)
        def _():
            pltpu.make_async_copy(src.at[rows(g, here)], mine, rsem.at[g]).start()

        for k in range(1, plane):
            la, xx = at_lat[k // 2], to_x[k % 2]
            remote(
                src.at[rows(g, la * 2 + xx)], mine, ssem.at[g], rsem.at[g], (la, base + xx)
            ).start()

    def whole(g):
        return pl.ds(pl.multiple_of(g * slab, slab), slab)

    def land(out, g):
        src, dst, ssem, rsem, to_plane = out
        pltpu.make_async_copy(src.at[whole(g)], dst.at[whole(g)], rsem.at[g]).wait()

    def drain(out, g):
        src, dst, ssem, rsem, to_plane = out

        @pl.when(begin(g) == 0)
        def _():
            pltpu.make_async_copy(src.at[whole(g)], dst.at[whole(g)], ssem.at[g]).wait()

        @pl.when(begin(g) == 1)
        def _():
            few = pl.ds(pl.multiple_of(g * slab, slab), slab - UNIT)
            pltpu.make_async_copy(src.at[few], dst.at[few], ssem.at[g]).wait()

    pack(normed2, 0)
    launch(out1, 0)
    launch(out1, 1)
    loads[5].wait()
    gates(normed2, router, info, comb, 0)

    @pl.when(inner)
    def _():
        lend.wait_recv()

    pack(far, 2 * slab)
    launch(out1, 3)
    launch(out1, 2)

    gates(far, router, far_info, comb, 2 * slab)

    half_rows = plane * MOST
    count = 2 * half_rows
    r = iota((count, 1), 0)
    slot = r // half_rows * MOST + r % MOST
    base = r % half_rows // MOST * UNIT
    pick = onehot((count, slab), base + slot)
    tails = [
        onehot((count, slab), jnp.where(slot % 3 == t, base + MAIN + slot // 3, -1))
        for t in range(3)
    ]
    r = iota((1, count), 1)
    slot = r // half_rows * MOST + r % MOST
    base = r % half_rows // MOST * UNIT
    target = iota((slab, count), 0)
    put = hit(target == base + slot).astype(BF16)
    put_tails = [
        hit(target == jnp.where(slot % 3 == t, base + MAIN + slot // 3, -1)).astype(BF16)
        for t in range(3)
    ]
    for load in loads[6:]:
        load.wait()

    def experts(i, c):
        g = i + 1 - 2 * (i % 2)
        land(out1, g)
        at = pl.ds(pl.multiple_of(g * slab, slab), slab)
        wide = mm(pick, got[at, :]).astype(BF16)
        end = mm(tails[0], got[at, 0:TAIL])
        for t in range(1, 3):
            end = end + mm(tails[t], got[at, t * TAIL : (t + 1) * TAIL])
        cells = jnp.concatenate([wide, end.astype(BF16)], axis=1)
        parts = []
        for e in range(2):
            xe = cells[e * half_rows : (e + 1) * half_rows]
            gate = mm(xe, wg[:, e * FF : (e + 1) * FF])
            upper = mm(xe, wu[:, e * FF : (e + 1) * FF])
            hidden = (jax.nn.silu(gate) * upper).astype(BF16)
            parts.append(mm(hidden, wd[e * FF : (e + 1) * FF, :]).astype(BF16))
        part = jnp.concatenate(parts, axis=0)
        for t in range(3):
            lanes = slice(t * TAIL, (t + 1) * TAIL)
            results[at, lanes] = (
                mm(put, part[:, lanes]) + mm(put_tails[t], part[:, WIDE:width])
            ).astype(BF16)
        launch(out2, g)
        return c

    lax.fori_loop(0, 4, experts, 0)


    def gather(g, into):
        land(out2, g)
        at = slice(g * slab, (g + 1) * slab)
        for t in range(3):
            lanes = slice(t * TAIL, (t + 1) * TAIL)
            s = mm(comb[t * 4 * n : (t + 1) * 4 * n, at], back[at, lanes])
            into[:, lanes] += s[0:n] + s[n : 2 * n]
            into[:, WIDE:width] += s[2 * n : 3 * n] + s[3 * n : 4 * n]

    @pl.when(inner)
    def _():
        far_acc[...] = jnp.zeros_like(far_acc)
        gather(3, far_acc)
        gather(2, far_acc)
        share[...] = far_acc[...].astype(BF16)
        give.start()

    gather(1, acc)
    gather(0, acc)

    @pl.when(~inner)
    def _():
        gather(3, acc)
        gather(2, acc)
        out_ref[...] = acc[...].astype(BF16)

    @pl.when(inner)
    def _():
        give.wait_recv()
        out_ref[...] = (acc[...] + shared[...].astype(F32)).astype(BF16)
        tell.wait_send()
        lend.wait_send()
        give.wait_send()

    go_left.wait_send()
    go_right.wait_send()

    @pl.when(has_down)
    def _():
        go_down.wait_send()
        corn_down.wait_send()

    @pl.when(has_up)
    def _():
        go_up.wait_send()
        corn_up.wait_send()

    for g in range(4):
        drain(out1, g)
        drain(out2, g)


def routes(n_lon, z, ids, info, place, first):
    n = ids.shape[1]
    r0, r1 = ids[0:1, :], ids[1:2, :]
    ia, ib = iota((n, n), 0), iota((n, n), 1)

    def column(row):
        return jnp.sum(jnp.where(ia == ib, row.astype(F32), 0.0), axis=1, keepdims=True)

    c0, c1 = column(r0).astype(jnp.int32), column(r1).astype(jnp.int32)
    rank0c = jnp.sum(hit((c0 == r0) & (ib < ia)), axis=1, keepdims=True)
    rank1c = jnp.sum(hit(c1 == r0) + hit((c1 == r1) & (ib < ia)), axis=1, keepdims=True)
    rank0r = jnp.sum(hit((c0 == r0) & (ia < ib)), axis=0, keepdims=True)
    rank1r = jnp.sum(hit(c0 == r1) + hit((c1 == r1) & (ia < ib)), axis=0, keepdims=True)

    def places(e, rank):
        slot = e % 2 * MOST + rank.astype(jnp.int32)
        device = e // 2
        at_lat, at_lon = device // n_lon, device % n_lon
        base = (flip(at_lon // 2, z) * (place.shape[0] // 12 // UNIT) + at_lat * 2 + at_lon % 2) * UNIT
        return base + slot, base + MAIN + slot // 3, slot % 3

    m0, t0, q0 = places(c0, rank0c)
    m1, t1, q1 = places(c1, rank1c)
    col = iota(info.shape, 1)
    table = jnp.zeros(info.shape, F32)
    for i, v in enumerate((m0, t0, q0, m1, t1, q1, c0, c1)):
        table = jnp.where(col == i, v.astype(F32), table)
    info[...] = table
    m0, t0, q0 = places(r0, rank0r)
    m1, t1, q1 = places(r1, rank1r)
    total = place.shape[0] // 3
    count = total // 2
    row = iota((count, n), 0) + first
    main = (hit(row == m0) + hit(row == m1)).astype(BF16)
    for t in range(3):
        rows = slice(t * total + first, t * total + first + count)
        place[rows, 0:n] = main
        place[rows, n : 2 * n] = (
            hit((row == t0) & (q0 == t)) + hit((row == t1) & (q1 == t))
        ).astype(BF16)


def gates(cells, router, info, comb, begin):
    logits = lax.dot_general(
        cells[...], router[...], (((1,), (1,)), ((), ())), preferred_element_type=F32
    )
    n = logits.shape[0]
    eid = iota(logits.shape, 1).astype(F32)
    m0, t0, q0, m1, t1, q1, c0, c1 = (info[:, i : i + 1] for i in range(8))
    s0 = jax.nn.sigmoid(jnp.sum(jnp.where(eid == c0, logits, 0.0), axis=1, keepdims=True))
    s1 = jax.nn.sigmoid(jnp.sum(jnp.where(eid == c1, logits, 0.0), axis=1, keepdims=True))
    g0 = s0 / (s0 + s1)
    g1 = s1 / (s0 + s1)
    count = comb.shape[1] // 2
    at = (iota((n, count), 1) + begin).astype(F32)

    def keep(first, a):
        hi = a.astype(BF16)
        comb[first : first + n, begin : begin + count] = hi
        comb[first + n : first + 2 * n, begin : begin + count] = (a - hi.astype(F32)).astype(BF16)

    main = jnp.where(at == m0, g0, 0.0) + jnp.where(at == m1, g1, 0.0)
    for t in range(3):
        keep(t * 4 * n, main)
        keep(
            t * 4 * n + 2 * n,
            jnp.where((at == t0) & (q0 == t), g0, 0.0) + jnp.where((at == t1) & (q1 == t), g1, 0.0),
        )


def layer_block(n_lat, n_lon, shifts, tok, router, ids, w_qkv, w_out, w_gate, w_up, w_down):
    n, width = tok.shape
    total = n_lat * n_lon * UNIT
    keys = 2 * n + 2 * WIN * WIN
    hbm = pl.BlockSpec(memory_space=pl.ANY)
    dma = pltpu.SemaphoreType.DMA

    def vmem(*shape, dtype=BF16):
        return pltpu.VMEM(shape, dtype)

    return pl.pallas_call(
        functools.partial(layer_kernel, n_lat, n_lon),
        out_shape=pltpu.VMEM((n, width), BF16),
        in_specs=[hbm] * 9,
        out_specs=pl.BlockSpec(memory_space=pltpu.VMEM),
        scratch_shapes=[
            pltpu.SMEM((2,), jnp.int32),
            vmem(n, width),
            vmem(router.shape[1], width),
            vmem(TOP, n, dtype=jnp.int32),
            vmem(*w_qkv.shape),
            vmem(*w_out.shape),
            vmem(*w_gate.shape),
            vmem(*w_up.shape),
            vmem(*w_down.shape),
            vmem(n, width),
            vmem(4 * WIN * REACH, width // 2),
            vmem(4 * WIN * REACH, width // 2),
            vmem(2 * REACH * (n // WIN), width),
            vmem(WIN * WIN, width),
            vmem(2 * WIN * WIN, width),
            vmem(n, width),
            vmem(keys, width),
            vmem(keys, width),
            vmem(width // HEAD * n, width // 4, dtype=F32),
            vmem(width // HEAD * n, 128, dtype=F32),
            vmem(3 * total, 2 * n),
            vmem(12 * n, total),
            vmem(n, 128, dtype=F32),
            vmem(n, width),
            vmem(n, width, dtype=F32),
            vmem(total, WIDE),
            vmem(total, WIDE),
            vmem(total, WIDE),
            vmem(total, WIDE),
            vmem(TOP, n, dtype=jnp.int32),
            vmem(n, 128, dtype=F32),
            vmem(n, width),
            vmem(n, width, dtype=F32),
            vmem(n, width),
            vmem(n, width),
            dma((9,)),
            dma((2,)), dma((2,)), dma((2,)), dma((2,)), dma((2,)), dma((2,)),
            dma((3,)), dma((3,)),
            dma((4,)), dma((4,)), dma((4,)), dma((4,)),
        ],
        compiler_params=pltpu.CompilerParams(
            collective_id=1, has_side_effects=True, vmem_limit_bytes=56 * 2**20
        ),
    )(shifts, tok, router.T, ids.T, w_qkv, w_out, w_gate, w_up, w_down)


def body(tokens, shifts, w_qkv, w_out, router, expert_ids, w_gate, w_up, w_down):
    n_lat = lax.axis_size("lat")
    n_lon = lax.axis_size("lon")
    devices = n_lat * n_lon
    rows, cols, width = tokens.shape
    ids = expert_ids.reshape(-1, TOP)
    tok = tokens.reshape(-1, width)
    if (n_lat, n_lon) == (4, 8) and w_gate.shape[1] == 2 * FF:
        out = layer_block(
            n_lat, n_lon, shifts, tok, router, ids, w_qkv, w_out, w_gate, w_up, w_down
        )
        return out.reshape(rows, cols, width)
    mixed, normed2 = front_block(n_lat, n_lon, shifts, tok, w_qkv, w_out)
    return general(mixed, normed2, router, ids, w_gate, w_up, w_down, devices, rows, cols)


def general(mixed, normed2, router, ids, w_gate, w_up, w_down, devices, rows, cols):
    width = mixed.shape[1]
    logits = jnp.dot(normed2, router, preferred_element_type=jnp.float32)
    experts = router.shape[1]
    expert_iota = jnp.arange(experts, dtype=jnp.int32)
    picks = ids[:, :, None] == expert_iota[None, None, :]
    chosen = jnp.sum(jnp.where(picks, logits[:, None, :], 0.0), axis=-1)
    sig = jax.nn.sigmoid(chosen)
    gates = sig / jnp.sum(sig, axis=1, keepdims=True)
    flat = ids.reshape(-1)
    order = jnp.arange(flat.shape[0], dtype=jnp.int32)
    earlier = (flat[:, None] == flat[None, :]) & (order[None, :] < order[:, None])
    rank = jnp.sum(earlier.astype(jnp.int32), axis=1)
    share = w_gate.shape[1]
    piece = min(FF, share)
    repl = FF // piece
    group = share // piece
    most = MOST
    cap = group * most
    token_of = jnp.arange(flat.shape[0], dtype=jnp.int32) // TOP
    slot = flat % group * most + rank
    slot_index = jnp.stack(
        [(flat // group * repl + copy) * cap + slot for copy in range(repl)], axis=0
    )
    routed = normed2[token_of]
    send = (
        jnp.zeros((devices * cap, width), jnp.bfloat16)
        .at[slot_index.reshape(-1)]
        .set(jnp.tile(routed, (repl, 1)))
    )
    send = send.reshape(devices, group, most, width)
    received = lax.all_to_all(send, ("lat", "lon"), split_axis=0, concat_axis=0, tiled=True)
    results = []
    for local in range(group):
        block = received[:, local].reshape(-1, width)
        gate = jnp.dot(
            block,
            w_gate[:, local * piece : (local + 1) * piece],
            preferred_element_type=jnp.float32,
        )
        upper = jnp.dot(
            block, w_up[:, local * piece : (local + 1) * piece], preferred_element_type=jnp.float32
        )
        hidden = (jax.nn.silu(gate) * upper).astype(jnp.bfloat16)
        part = jnp.dot(
            hidden, w_down[local * piece : (local + 1) * piece], preferred_element_type=jnp.float32
        ).astype(jnp.bfloat16)
        results.append(part.reshape(received.shape[0], received.shape[2], width))
    back = lax.all_to_all(
        jnp.stack(results, axis=1), ("lat", "lon"), split_axis=0, concat_axis=0, tiled=True
    )
    back_flat = back.reshape(devices * cap, width)
    combined = jnp.zeros((flat.shape[0], width), jnp.float32)
    for copy in range(repl):
        combined = combined + back_flat[slot_index[copy]].astype(jnp.float32)
    combined = combined.reshape(-1, TOP, width)
    moe = jnp.sum(gates[:, :, None] * combined, axis=1)
    layer_out = (mixed.astype(jnp.float32) + moe).astype(jnp.bfloat16)
    return layer_out.reshape(rows, cols, width)


def solution(mesh):
    placed = (
        P("lat", "lon", None),
        P(),
        P(),
        P(),
        P(),
        P("lat", "lon", None, None),
        P(None, ("lat", "lon")),
        P(None, ("lat", "lon")),
        P(("lat", "lon"), None),
    )
    return jax.shard_map(
        body, mesh=mesh, in_specs=placed, out_specs=P("lat", "lon", None), check_vma=False
    )
```

```python
import functools

import jax
import jax.numpy as jnp
import numpy as np
from jax import lax
from jax.experimental import pallas as pl
from jax.experimental.pallas import tpu as pltpu
from jax.sharding import PartitionSpec as P

HEAD = 64
FF = 1024
TOP = 2
WIN = 8
MOST = 6
UNIT = 16
MAIN = 12
WIDE = 768
TAIL = 256
F32 = jnp.float32
BF16 = jnp.bfloat16


def rms_rows(x):
    xf = x.astype(jnp.float32)
    return xf * lax.rsqrt(jnp.mean(xf * xf, axis=-1, keepdims=True) + 1e-05)


def mm(a, b):
    return jnp.dot(a, b, preferred_element_type=F32)


def hit(cond):
    return jnp.where(cond, 1.0, 0.0)


def head_norm(x, ones):
    xf = x.astype(F32)
    sq = xf * xf
    hi = sq.astype(BF16)
    lo = (sq - hi.astype(F32)).astype(BF16)
    mean = (mm(hi, ones) + mm(lo, ones)) * (1.0 / HEAD)
    return xf * lax.rsqrt(mean + 1e-05)


REACH = WIN - 1


def front_kernel(
    n_lat, n_lon, shifts_ref, tok_ref, wqkv_hbm, wo_hbm, mixed_ref, send_ref,
    tall, tosend, side, wqkv, wo, qbuf, kbuf, vbuf, w_sem, vs, vr, hs, hr
):
    lat, lon = lax.axis_index("lat"), lax.axis_index("lon")
    loads = [
        pltpu.make_async_copy(wqkv_hbm, wqkv, w_sem.at[0]),
        pltpu.make_async_copy(wo_hbm, wo, w_sem.at[1]),
    ]
    for load in loads:
        load.start()
    n, width = tok_ref.shape
    cols = n // WIN
    left = (lat, lax.rem(lon + n_lon - 1, n_lon))
    right = (lat, lax.rem(lon + 1, n_lon))
    up, down = (lat - 1, lon), (lat + 1, lon)
    has_up, has_down = lat > 0, lat < n_lat - 1
    mesh_id = pl.DeviceIdType.MESH
    barrier = pltpu.get_barrier_semaphore()
    around = (
        left, right, (lax.rem(lat + n_lat - 1, n_lat), lon), (lax.rem(lat + 1, n_lat), lon)
    )
    for other in around:
        pl.semaphore_signal(barrier, inc=1, device_id=other, device_id_type=mesh_id)

    tall[n : 2 * n, :] = rms_rows(tok_ref[...]).astype(BF16)
    tall[0:cols, :] = jnp.zeros((cols, width), BF16)
    tall[3 * n - cols : 3 * n, :] = jnp.zeros((cols, width), BF16)
    edge = REACH * cols

    @pl.when(lat == 0)
    def _():
        tall[cols:n, :] = jnp.zeros((edge, width), BF16)

    @pl.when(lat == n_lat - 1)
    def _():
        tall[2 * n : 2 * n + edge, :] = jnp.zeros((edge, width), BF16)

    pl.semaphore_wait(barrier, len(around))

    def remote(src, dst, ssem, rsem, to):
        return pltpu.make_async_remote_copy(
            src_ref=src, dst_ref=dst, send_sem=ssem, recv_sem=rsem,
            device_id=to, device_id_type=mesh_id,
        )

    above, below = tall.at[pl.ds(cols, edge)], tall.at[pl.ds(2 * n, edge)]
    go_down = remote(tall.at[pl.ds(n + cols, edge)], above, vs.at[0], vr.at[0], down)
    go_up = remote(tall.at[pl.ds(n, edge)], below, vs.at[1], vr.at[1], up)

    @pl.when(has_down)
    def _():
        go_down.start()

    @pl.when(has_up)
    def _():
        go_up.start()

    s_lat, s_lon = shifts_ref[0], shifts_ref[1]
    sides = 2 * WIN * REACH
    out_row = lax.broadcasted_iota(jnp.int32, (2 * sides, 1), 0)
    local = jnp.where(out_row >= sides, out_row - sides, out_row)
    at = local // REACH * cols + local % REACH + jnp.where(out_row >= sides, cols - REACH, 0)
    start = (WIN - s_lat) * cols
    pick = hit(lax.broadcasted_iota(jnp.int32, (2 * sides, 3 * n), 1) == at + start).astype(BF16)

    @pl.when(has_up)
    def _():
        go_down.wait_recv()

    @pl.when(has_down)
    def _():
        go_up.wait_recv()

    everything = tall[...]
    tosend[...] = mm(pick, everything).astype(BF16)
    go_left = remote(
        tosend.at[pl.ds(0, sides)], side.at[pl.ds(sides, sides)], hs.at[0], hr.at[0], left
    )
    go_right = remote(
        tosend.at[pl.ds(sides, sides)], side.at[pl.ds(0, sides)], hs.at[1], hr.at[1], right
    )
    go_left.start()
    go_right.start()
    there = lax.broadcasted_iota(jnp.int32, (2 * n, 3 * n), 0) + start
    shift = hit(lax.broadcasted_iota(jnp.int32, (2 * n, 3 * n), 1) == there).astype(BF16)
    keys = mm(shift, everything).astype(BF16)

    steps = 4
    group = width // steps
    heads = group // HEAD
    ra = lax.broadcasted_iota(jnp.int32, (group, group), 0) // HEAD
    rb = lax.broadcasted_iota(jnp.int32, (group, group), 1) // HEAD
    ones = hit(ra == rb).astype(BF16)
    own = tall[n : 2 * n, :]
    loads[0].wait()

    def project(cells, first, count):
        for j in range(steps):
            lanes = slice(j * group, (j + 1) * group)
            k = mm(cells, wqkv[:, width + j * group : width + (j + 1) * group]).astype(BF16)
            kbuf[first : first + count, lanes] = head_norm(k, ones).astype(BF16)
            v = mm(cells, wqkv[:, 2 * width + j * group : 2 * width + (j + 1) * group])
            vbuf[first : first + count, lanes] = v.astype(BF16)

    for j in range(steps):
        lanes = slice(j * group, (j + 1) * group)
        q = mm(own, wqkv[:, lanes]).astype(BF16)
        qbuf[:, lanes] = (head_norm(q, ones) * (1.0 / 8.0)).astype(BF16)
    project(keys, 0, 2 * n)

    total_keys = 2 * n + 2 * sides
    i = lax.broadcasted_iota(jnp.int32, (1, total_keys), 1)
    m = jnp.where(i < 2 * n + sides, i - 2 * n, i - 2 * n - sides)
    inner = i < 2 * n
    r_of = jnp.where(inner, i // cols, m // REACH)
    c_of = jnp.where(
        inner, i % cols, m % REACH + jnp.where(i < 2 * n + sides, -REACH, cols)
    )
    at_row = lat * WIN - s_lat + r_of
    valid = (at_row >= 0) & (at_row < WIN * n_lat)
    keyid = jnp.where(valid, (r_of // WIN) * 4 + (c_of + s_lon + WIN) // WIN, -1)
    qi = lax.broadcasted_iota(jnp.int32, (n, 1), 0)
    qid = (qi // cols + s_lat) // WIN * 4 + (qi % cols + s_lon + WIN) // WIN
    same = qid == keyid
    lane = lax.broadcasted_iota(jnp.int32, (n, group), 1) // HEAD

    go_left.wait_recv()
    go_right.wait_recv()
    project(side[...], 2 * n, 2 * sides)
    loads[1].wait()
    acc = tok_ref[...].astype(F32)
    for j in range(steps):
        lanes = slice(j * group, (j + 1) * group)
        qn = qbuf[:, lanes]
        stacked = jnp.concatenate(
            [jnp.where(lane == h, qn, jnp.zeros_like(qn)) for h in range(heads)], axis=0
        )
        scores = lax.dot_general(
            stacked, kbuf[:, lanes], (((1,), (1,)), ((), ())), preferred_element_type=F32
        )
        weights = []
        for h in range(heads):
            e = jnp.where(same, jnp.exp(scores[h * n : (h + 1) * n]), 0.0)
            total = jnp.sum(e, axis=1, keepdims=True)
            weights.append((e * (1.0 / total)).astype(BF16))
        mixedv = mm(jnp.concatenate(weights, axis=0), vbuf[:, lanes])
        att = jnp.zeros((n, group), F32)
        for h in range(heads):
            att = jnp.where(lane == h, mixedv[h * n : (h + 1) * n], att)
        acc = acc + mm(att.astype(BF16), wo[lanes, :])

    mixed = acc.astype(BF16)
    mixed_ref[...] = mixed
    normed2 = rms_rows(mixed).astype(BF16)
    send_ref[...] = normed2

    go_left.wait_send()
    go_right.wait_send()

    @pl.when(has_down)
    def _():
        go_down.wait_send()

    @pl.when(has_up)
    def _():
        go_up.wait_send()


def front_block(n_lat, n_lon, shifts, tok, w_qkv, w_out):
    n, width = tok.shape
    sides = 2 * 2 * WIN * REACH
    vm = pl.BlockSpec(memory_space=pltpu.VMEM)
    hbm = pl.BlockSpec(memory_space=pl.ANY)
    dma = pltpu.SemaphoreType.DMA
    keys = 2 * n + sides
    return pl.pallas_call(
        functools.partial(front_kernel, n_lat, n_lon),
        in_specs=[pl.BlockSpec(memory_space=pltpu.SMEM), vm, hbm, hbm],
        out_specs=[vm, vm],
        out_shape=[jax.ShapeDtypeStruct((n, width), BF16)] * 2,
        scratch_shapes=[
            pltpu.VMEM((3 * n, width), BF16),
            pltpu.VMEM((sides, width), BF16),
            pltpu.VMEM((sides, width), BF16),
            pltpu.VMEM(w_qkv.shape, BF16),
            pltpu.VMEM(w_out.shape, BF16),
            pltpu.VMEM((n, width), BF16),
            pltpu.VMEM((keys, width), BF16),
            pltpu.VMEM((keys, width), BF16),
            dma((2,)), dma((2,)), dma((2,)), dma((2,)), dma((2,)),
        ],
        compiler_params=pltpu.CompilerParams(
            collective_id=2, has_side_effects=True, vmem_limit_bytes=40 * 2**20
        ),
    )(shifts, tok, w_qkv, w_out)


def iota(shape, axis):
    return lax.broadcasted_iota(jnp.int32, shape, axis)


def onehot(shape, target):
    return hit(iota(shape, 1) == target).astype(BF16)


def flip(z, g):
    return 2 * ((z // 2 + g // 2) % 2) + (z + g) % 2


def layer_kernel(
    n_lat, n_lon, shifts_hbm, tok_hbm, router_hbm, ids_hbm, wqkv_hbm, wo_hbm, wg_hbm, wu_hbm,
    wd_hbm, out_ref, shifts, tok, router, ids, wqkv, wo, wg, wu, wd, own, sideout, sidein, vertin,
    side, cornin, qbuf, kbuf, vbuf, numer, denom, place, comb, info, normed2, acc, send, got, results, back,
    far_ids, far_info, far, far_acc, share, shared, w_sem, vs, vr, hs, hr, cs, cr, ms, mr, s1, r1, s2, r2
):
    lat, lon = lax.axis_index("lat"), lax.axis_index("lon")
    z, x = lon // 2, lon % 2
    plane = 2 * n_lat
    slab = plane * UNIT
    here = lat * 2 + x
    inner = (z + 1) // 2 % 2 == 1
    mirror = (lat, (3 - z) * 2 + x)
    loads = [
        pltpu.make_async_copy(src, dst, w_sem.at[i])
        for i, (src, dst) in enumerate((
            (tok_hbm, tok), (shifts_hbm, shifts), (ids_hbm, ids), (wqkv_hbm, wqkv),
            (wo_hbm, wo), (router_hbm, router), (wg_hbm, wg), (wu_hbm, wu), (wd_hbm, wd),
        ))
    ]
    for load in loads[:6]:
        load.start()
    n, width = tok.shape
    cols = n // WIN
    mesh_id = pl.DeviceIdType.MESH
    left = (lat, lax.rem(lon + n_lon - 1, n_lon))
    right = (lat, lax.rem(lon + 1, n_lon))
    up, down = (lat - 1, lon), (lat + 1, lon)
    has_up, has_down = lat > 0, lat < n_lat - 1

    barrier = pltpu.get_barrier_semaphore()
    devices = n_lat * n_lon

    at_lat = [(lat + k) % n_lat for k in range(n_lat)]
    at_lon = [(lon + k) % n_lon for k in range(n_lon)]
    around = [(0, 1), (0, n_lon - 1), (1, 0), (n_lat - 1, 0)]
    others = [(a, b) for a in range(n_lat) for b in range(n_lon)]
    for a, b in around + [o for o in others if o not in around and o != (0, 0)]:
        pl.semaphore_signal(
            barrier, inc=1, device_id=(at_lat[a], at_lon[b]), device_id_type=mesh_id
        )

    edge = REACH * cols
    nook = WIN * WIN

    @pl.when(lat == 0)
    def _():
        vertin[0:edge, :] = jnp.zeros((edge, width), BF16)
        cornin[0:nook, :] = jnp.zeros((nook, width), BF16)

    @pl.when(lat == n_lat - 1)
    def _():
        vertin[edge : 2 * edge, :] = jnp.zeros((edge, width), BF16)
        cornin[nook : 2 * nook, :] = jnp.zeros((nook, width), BF16)

    half = WIN * REACH
    lanes2 = width // 2
    r = iota((4 * half, 1), 0)
    within = r % half
    cell = within // REACH * cols + within % REACH + jnp.where(r >= 2 * half, cols - REACH, 0)
    second = r // half % 2 == 1
    pick0 = onehot((4 * half, n), jnp.where(second, -1, cell))
    pick1 = onehot((4 * half, n), jnp.where(second, cell, -1))
    loads[0].wait()
    own[...] = rms_rows(tok[...]).astype(BF16)
    sideout[...] = (
        mm(pick0, own[:, 0:lanes2]) + mm(pick1, own[:, lanes2:width])
    ).astype(BF16)
    pl.semaphore_wait(barrier, devices - 1)

    def remote(src, dst, ssem, rsem, to):
        return pltpu.make_async_remote_copy(
            src_ref=src, dst_ref=dst, send_sem=ssem, recv_sem=rsem,
            device_id=to, device_id_type=mesh_id,
        )

    first, last = pl.ds(0, 2 * half), pl.ds(2 * half, 2 * half)
    go_left = remote(sideout.at[first], sidein.at[last], hs.at[0], hr.at[0], left)
    go_right = remote(sideout.at[last], sidein.at[first], hs.at[1], hr.at[1], right)
    go_left.start()
    go_right.start()
    go_down = remote(
        own.at[pl.ds(n - edge, edge)], vertin.at[pl.ds(0, edge)], vs.at[0], vr.at[0], down
    )
    go_up = remote(own.at[pl.ds(0, edge)], vertin.at[pl.ds(edge, edge)], vs.at[1], vr.at[1], up)

    @pl.when(has_down)
    def _():
        go_down.start()

    @pl.when(has_up)
    def _():
        go_up.start()

    tell = remote(ids, far_ids, ms.at[0], mr.at[0], mirror)
    lend = remote(normed2, far, ms.at[1], mr.at[1], mirror)
    give = remote(share, shared, ms.at[2], mr.at[2], mirror)
    loads[2].wait()

    @pl.when(inner)
    def _():
        tell.start()

    @pl.when(~inner)
    def _():
        far_ids[...] = ids[...]

    steps = 4
    group = width // steps
    heads = group // HEAD
    ones = hit(iota((group, group), 0) // HEAD == iota((group, group), 1) // HEAD).astype(BF16)
    loads[3].wait()
    for load in loads[6:]:
        load.start()

    twice = jnp.concatenate([ones, ones], axis=0)

    def unit(a, into, at, scale):
        m = a.shape[0]
        a = a.astype(BF16).astype(F32)
        sq = a * a
        hi = sq.astype(BF16)
        lo = (sq - hi.astype(F32)).astype(BF16)
        parts = [slice(j * group, (j + 1) * group) for j in range(steps)]
        mean = mm(
            jnp.concatenate(
                [jnp.concatenate([hi[:, p], lo[:, p]], axis=1) for p in parts], axis=0
            ),
            twice,
        ) * (1.0 / HEAD)
        for j, p in enumerate(parts):
            r = lax.rsqrt(mean[j * m : (j + 1) * m] + 1e-05) * scale
            into[at : at + m, p] = (a[:, p] * r).astype(BF16)

    def project(cells, at):
        unit(mm(cells, wqkv[:, width : 2 * width]), kbuf, at, 1.0)
        v = mm(cells, wqkv[:, 2 * width : 3 * width])
        vbuf[at : at + cells.shape[0], :] = v.astype(BF16)

    unit(mm(own[...], wqkv[:, 0:width]), qbuf, 0, 1.0 / 8.0)
    project(own[...], 0)

    loads[1].wait()
    s_lat, s_lon = shifts[0], shifts[1]
    total_keys = 2 * n + 2 * nook
    i = iota((1, total_keys), 1)
    in_own, in_vert, in_side = i < n, i < 2 * n, i < 2 * n + nook
    m = i - jnp.where(in_side, 2 * n, 2 * n + nook)
    row = jnp.where(in_vert, jnp.where(in_own, i, i - n) // cols, m // WIN)
    col = jnp.where(in_vert, i % cols, m % WIN)
    inside = in_own | (in_side & ~in_vert)
    key_row = jnp.where(inside, (row + s_lat) // WIN, jnp.where(row < s_lat, 0, 1))
    key_col = jnp.where(in_vert, (col + s_lon) // WIN, jnp.where(col < s_lon, 0, 2))
    gone = ~inside & (((row < s_lat) & (lat == 0)) | ((row >= s_lat) & (lat == n_lat - 1)))
    keyid = jnp.where(gone, -1, key_row * 4 + key_col)
    w = iota((n, 1), 0)
    same = (w // cols + s_lat) // WIN * 4 + (w % cols + s_lon) // WIN == keyid
    lane = iota((n, group), 1) // HEAD

    def attend(first, count, fresh):
        seen = same[:, first : first + count]
        for j in range(steps):
            lanes = slice(j * group, (j + 1) * group)
            qn = qbuf[:, lanes]
            stacked = jnp.concatenate(
                [jnp.where(lane == h, qn, jnp.zeros_like(qn)) for h in range(heads)], axis=0
            )
            scores = lax.dot_general(
                stacked, kbuf[first : first + count, lanes], (((1,), (1,)), ((), ())),
                preferred_element_type=F32,
            )
            e = []
            for h in range(heads):
                e.append(jnp.where(seen, jnp.exp(scores[h * n : (h + 1) * n]), 0.0))
                at = (j * heads + h) * n
                part = jnp.sum(e[h], axis=1, keepdims=True)
                denom[at : at + n, 0:1] = part if fresh else denom[at : at + n, 0:1] + part
            e = jnp.concatenate([v.astype(BF16) for v in e], axis=0)
            part = mm(e, vbuf[first : first + count, lanes])
            at = slice(j * heads * n, (j + 1) * heads * n)
            numer[at, :] = part if fresh else numer[at, :] + part

    attend(0, n, True)
    w = iota((n, 1), 0)
    v_at = w // cols
    vert_at = jnp.where(v_at < s_lat, REACH - s_lat + v_at, REACH + v_at - s_lat)
    vert_pick = onehot((n, 2 * edge), vert_at * cols + w % cols)

    @pl.when(has_up)
    def _():
        go_down.wait_recv()

    @pl.when(has_down)
    def _():
        go_up.wait_recv()

    project(mm(vert_pick, vertin[...]).astype(BF16), n)

    routes(n_lon, z, ids, info, place, 0)

    @pl.when(inner)
    def _():
        tell.wait_recv()

    far_z = jnp.where(inner, 3 - z, z)
    routes(n_lon, far_z, far_ids, far_info, place, 2 * slab)

    w = iota((nook, 1), 0)
    major, minor = w // WIN, w % WIN
    side_at = major * REACH + jnp.where(
        minor < s_lon, REACH - s_lon + minor, 2 * half + minor - s_lon
    )
    side0 = onehot((nook, 4 * half), side_at)
    side1 = onehot((nook, 4 * half), side_at + half)
    corn_at = jnp.where(major < s_lat, WIN - s_lat + major, WIN + major - s_lat)
    corn_pick = onehot((nook, 2 * nook), corn_at * WIN + minor)
    go_left.wait_recv()
    go_right.wait_recv()
    side[:, 0:lanes2] = mm(side0, sidein[...]).astype(BF16)
    side[:, lanes2:width] = mm(side1, sidein[...]).astype(BF16)
    corn_down = remote(side, cornin.at[pl.ds(0, nook)], cs.at[0], cr.at[0], down)
    corn_up = remote(side, cornin.at[pl.ds(nook, nook)], cs.at[1], cr.at[1], up)

    @pl.when(has_down)
    def _():
        corn_down.start()

    @pl.when(has_up)
    def _():
        corn_up.start()


    attend(n, n, False)

    @pl.when(has_up)
    def _():
        corn_down.wait_recv()

    @pl.when(has_down)
    def _():
        corn_up.wait_recv()

    corners = mm(corn_pick, cornin[...]).astype(BF16)
    project(jnp.concatenate([side[...], corners], axis=0), 2 * n)

    loads[4].wait()
    attend(2 * n, 2 * nook, False)
    total = tok[...].astype(F32)
    for j in range(steps):
        lanes = slice(j * group, (j + 1) * group)
        at = j * heads * n
        num, den = numer[at : at + n, :], denom[at : at + n, 0:1]
        for h in range(1, heads):
            rows_h = slice(at + h * n, at + (h + 1) * n)
            num = jnp.where(lane == h, numer[rows_h, :], num)
            den = jnp.where(lane == h, denom[rows_h, 0:1], den)
        total = total + mm((num / den).astype(BF16), wo[lanes, :])

    mixed = total.astype(BF16)
    acc[...] = mixed.astype(F32)
    normed2[...] = rms_rows(mixed).astype(BF16)

    @pl.when(inner)
    def _():
        lend.start()

    @pl.when(~inner)
    def _():
        far[...] = normed2[...]

    def pack(cells, first):
        end = cells[:, WIDE:width]
        for t in range(3):
            lanes = slice(t * TAIL, (t + 1) * TAIL)
            both = jnp.concatenate([cells[:, lanes], end], axis=0)
            at = t * 4 * slab + first
            send[first : first + 2 * slab, lanes] = mm(place[at : at + 2 * slab, :], both).astype(BF16)

    def rows(g, j):
        return pl.ds(pl.multiple_of(g * slab + j * UNIT, UNIT), UNIT)

    def forth(g):
        return flip(z, jnp.where(inner & (g >= 2), 3 - g, g))

    def home(g):
        return flip(z, jnp.where(inner, jnp.where(g == 3, 0, g), jnp.where(g == 2, 1, g)))

    def begin(g):
        return jnp.where((g == 0) | (inner & (g == 3)), 1, 0)

    out1, out2 = (send, got, s1, r1, forth), (results, back, s2, r2, home)

    to_x = [x, (x + 1) % 2]

    def launch(out, g):
        src, dst, ssem, rsem, to_plane = out
        base = to_plane(g) * 2
        mine = dst.at[rows(g, here)]

        @pl.when(begin(g) == 0)
        def _():
            remote(src.at[rows(g, here)], mine, ssem.at[g], rsem.at[g], (lat, base + x)).start()

        @pl.when(begin(g) == 1)
        def _():
            pltpu.make_async_copy(src.at[rows(g, here)], mine, rsem.at[g]).start()

        for k in range(1, plane):
            la, xx = at_lat[k // 2], to_x[k % 2]
            remote(
                src.at[rows(g, la * 2 + xx)], mine, ssem.at[g], rsem.at[g], (la, base + xx)
            ).start()

    def whole(g):
        return pl.ds(pl.multiple_of(g * slab, slab), slab)

    def land(out, g):
        src, dst, ssem, rsem, to_plane = out
        pltpu.make_async_copy(src.at[whole(g)], dst.at[whole(g)], rsem.at[g]).wait()

    def drain(out, g):
        src, dst, ssem, rsem, to_plane = out

        @pl.when(begin(g) == 0)
        def _():
            pltpu.make_async_copy(src.at[whole(g)], dst.at[whole(g)], ssem.at[g]).wait()

        @pl.when(begin(g) == 1)
        def _():
            few = pl.ds(pl.multiple_of(g * slab, slab), slab - UNIT)
            pltpu.make_async_copy(src.at[few], dst.at[few], ssem.at[g]).wait()

    pack(normed2, 0)
    launch(out1, 0)
    launch(out1, 1)
    loads[5].wait()
    gates(normed2, router, info, comb, 0)

    @pl.when(inner)
    def _():
        lend.wait_recv()

    pack(far, 2 * slab)
    early = jnp.where(inner, 2, 3)
    launch(out1, early)
    launch(out1, 5 - early)


    half_rows = plane * MOST
    count = 2 * half_rows
    r = iota((count, 1), 0)
    slot = r // half_rows * MOST + r % MOST
    base = r % half_rows // MOST * UNIT
    pick = onehot((count, slab), base + slot)
    tails = [
        onehot((count, slab), jnp.where(slot % 3 == t, base + MAIN + slot // 3, -1))
        for t in range(3)
    ]
    r = iota((1, count), 1)
    slot = r // half_rows * MOST + r % MOST
    base = r % half_rows // MOST * UNIT
    target = iota((slab, count), 0)
    put = hit(target == base + slot).astype(BF16)
    put_tails = [
        hit(target == jnp.where(slot % 3 == t, base + MAIN + slot // 3, -1)).astype(BF16)
        for t in range(3)
    ]
    for load in loads[6:]:
        load.wait()

    def experts(i, c):
        g = i + 1 - 2 * (i % 2)
        land(out1, g)
        at = pl.ds(pl.multiple_of(g * slab, slab), slab)
        wide = mm(pick, got[at, :]).astype(BF16)
        end = mm(tails[0], got[at, 0:TAIL])
        for t in range(1, 3):
            end = end + mm(tails[t], got[at, t * TAIL : (t + 1) * TAIL])
        cells = jnp.concatenate([wide, end.astype(BF16)], axis=1)
        parts = []
        for e in range(2):
            xe = cells[e * half_rows : (e + 1) * half_rows]
            gate = mm(xe, wg[:, e * FF : (e + 1) * FF])
            upper = mm(xe, wu[:, e * FF : (e + 1) * FF])
            hidden = (jax.nn.silu(gate) * upper).astype(BF16)
            parts.append(mm(hidden, wd[e * FF : (e + 1) * FF, :]).astype(BF16))
        part = jnp.concatenate(parts, axis=0)
        for t in range(3):
            lanes = slice(t * TAIL, (t + 1) * TAIL)
            results[at, lanes] = (
                mm(put, part[:, lanes]) + mm(put_tails[t], part[:, WIDE:width])
            ).astype(BF16)
        launch(out2, g)
        return c

    lax.fori_loop(0, 4, experts, 0)
    gates(far, router, far_info, comb, 2 * slab)


    def gather(g, into):
        land(out2, g)
        at = slice(g * slab, (g + 1) * slab)
        for t in range(3):
            lanes = slice(t * TAIL, (t + 1) * TAIL)
            s = mm(comb[t * 4 * n : (t + 1) * 4 * n, at], back[at, lanes])
            into[:, lanes] += s[0:n] + s[n : 2 * n]
            into[:, WIDE:width] += s[2 * n : 3 * n] + s[3 * n : 4 * n]

    @pl.when(inner)
    def _():
        far_acc[...] = jnp.zeros_like(far_acc)
        gather(3, far_acc)
        gather(2, far_acc)
        share[...] = far_acc[...].astype(BF16)
        give.start()

    gather(1, acc)
    gather(0, acc)

    @pl.when(~inner)
    def _():
        gather(3, acc)
        gather(2, acc)
        out_ref[...] = acc[...].astype(BF16)

    @pl.when(inner)
    def _():
        give.wait_recv()
        out_ref[...] = (acc[...] + shared[...].astype(F32)).astype(BF16)
        tell.wait_send()
        lend.wait_send()
        give.wait_send()

    go_left.wait_send()
    go_right.wait_send()

    @pl.when(has_down)
    def _():
        go_down.wait_send()
        corn_down.wait_send()

    @pl.when(has_up)
    def _():
        go_up.wait_send()
        corn_up.wait_send()

    for g in range(4):
        drain(out1, g)
        drain(out2, g)


def routes(n_lon, z, ids, info, place, first):
    n = ids.shape[1]
    r0, r1 = ids[0:1, :], ids[1:2, :]
    ia, ib = iota((n, n), 0), iota((n, n), 1)

    def column(row):
        return jnp.sum(jnp.where(ia == ib, row.astype(F32), 0.0), axis=1, keepdims=True)

    c0, c1 = column(r0).astype(jnp.int32), column(r1).astype(jnp.int32)
    rank0c = jnp.sum(hit((c0 == r0) & (ib < ia)), axis=1, keepdims=True)
    rank1c = jnp.sum(hit(c1 == r0) + hit((c1 == r1) & (ib < ia)), axis=1, keepdims=True)
    rank0r = jnp.sum(hit((c0 == r0) & (ia < ib)), axis=0, keepdims=True)
    rank1r = jnp.sum(hit(c0 == r1) + hit((c1 == r1) & (ia < ib)), axis=0, keepdims=True)

    def places(e, rank):
        slot = e % 2 * MOST + rank.astype(jnp.int32)
        device = e // 2
        at_lat, at_lon = device // n_lon, device % n_lon
        base = (flip(at_lon // 2, z) * (place.shape[0] // 12 // UNIT) + at_lat * 2 + at_lon % 2) * UNIT
        return base + slot, base + MAIN + slot // 3, slot % 3

    m0, t0, q0 = places(c0, rank0c)
    m1, t1, q1 = places(c1, rank1c)
    col = iota(info.shape, 1)
    table = jnp.zeros(info.shape, F32)
    for i, v in enumerate((m0, t0, q0, m1, t1, q1, c0, c1)):
        table = jnp.where(col == i, v.astype(F32), table)
    info[...] = table
    m0, t0, q0 = places(r0, rank0r)
    m1, t1, q1 = places(r1, rank1r)
    total = place.shape[0] // 3
    count = total // 2
    row = iota((count, n), 0) + first
    main = (hit(row == m0) + hit(row == m1)).astype(BF16)
    for t in range(3):
        rows = slice(t * total + first, t * total + first + count)
        place[rows, 0:n] = main
        place[rows, n : 2 * n] = (
            hit((row == t0) & (q0 == t)) + hit((row == t1) & (q1 == t))
        ).astype(BF16)


def gates(cells, router, info, comb, begin):
    logits = lax.dot_general(
        cells[...], router[...], (((1,), (1,)), ((), ())), preferred_element_type=F32
    )
    n = logits.shape[0]
    eid = iota(logits.shape, 1).astype(F32)
    m0, t0, q0, m1, t1, q1, c0, c1 = (info[:, i : i + 1] for i in range(8))
    s0 = jax.nn.sigmoid(jnp.sum(jnp.where(eid == c0, logits, 0.0), axis=1, keepdims=True))
    s1 = jax.nn.sigmoid(jnp.sum(jnp.where(eid == c1, logits, 0.0), axis=1, keepdims=True))
    g0 = s0 / (s0 + s1)
    g1 = s1 / (s0 + s1)
    count = comb.shape[1] // 2
    at = (iota((n, count), 1) + begin).astype(F32)

    def keep(first, a):
        hi = a.astype(BF16)
        comb[first : first + n, begin : begin + count] = hi
        comb[first + n : first + 2 * n, begin : begin + count] = (a - hi.astype(F32)).astype(BF16)

    main = jnp.where(at == m0, g0, 0.0) + jnp.where(at == m1, g1, 0.0)
    for t in range(3):
        keep(t * 4 * n, main)
        keep(
            t * 4 * n + 2 * n,
            jnp.where((at == t0) & (q0 == t), g0, 0.0) + jnp.where((at == t1) & (q1 == t), g1, 0.0),
        )


def layer_block(n_lat, n_lon, shifts, tok, router, ids, w_qkv, w_out, w_gate, w_up, w_down):
    n, width = tok.shape
    total = n_lat * n_lon * UNIT
    keys = 2 * n + 2 * WIN * WIN
    hbm = pl.BlockSpec(memory_space=pl.ANY)
    dma = pltpu.SemaphoreType.DMA

    def vmem(*shape, dtype=BF16):
        return pltpu.VMEM(shape, dtype)

    return pl.pallas_call(
        functools.partial(layer_kernel, n_lat, n_lon),
        out_shape=pltpu.VMEM((n, width), BF16),
        in_specs=[hbm] * 9,
        out_specs=pl.BlockSpec(memory_space=pltpu.VMEM),
        scratch_shapes=[
            pltpu.SMEM((2,), jnp.int32),
            vmem(n, width),
            vmem(router.shape[1], width),
            vmem(TOP, n, dtype=jnp.int32),
            vmem(*w_qkv.shape),
            vmem(*w_out.shape),
            vmem(*w_gate.shape),
            vmem(*w_up.shape),
            vmem(*w_down.shape),
            vmem(n, width),
            vmem(4 * WIN * REACH, width // 2),
            vmem(4 * WIN * REACH, width // 2),
            vmem(2 * REACH * (n // WIN), width),
            vmem(WIN * WIN, width),
            vmem(2 * WIN * WIN, width),
            vmem(n, width),
            vmem(keys, width),
            vmem(keys, width),
            vmem(width // HEAD * n, width // 4, dtype=F32),
            vmem(width // HEAD * n, 128, dtype=F32),
            vmem(3 * total, 2 * n),
            vmem(12 * n, total),
            vmem(n, 128, dtype=F32),
            vmem(n, width),
            vmem(n, width, dtype=F32),
            vmem(total, WIDE),
            vmem(total, WIDE),
            vmem(total, WIDE),
            vmem(total, WIDE),
            vmem(TOP, n, dtype=jnp.int32),
            vmem(n, 128, dtype=F32),
            vmem(n, width),
            vmem(n, width, dtype=F32),
            vmem(n, width),
            vmem(n, width),
            dma((9,)),
            dma((2,)), dma((2,)), dma((2,)), dma((2,)), dma((2,)), dma((2,)),
            dma((3,)), dma((3,)),
            dma((4,)), dma((4,)), dma((4,)), dma((4,)),
        ],
        compiler_params=pltpu.CompilerParams(
            collective_id=1, has_side_effects=True, vmem_limit_bytes=56 * 2**20
        ),
    )(shifts, tok, router.T, ids.T, w_qkv, w_out, w_gate, w_up, w_down)


def body(tokens, shifts, w_qkv, w_out, router, expert_ids, w_gate, w_up, w_down):
    n_lat = lax.axis_size("lat")
    n_lon = lax.axis_size("lon")
    devices = n_lat * n_lon
    rows, cols, width = tokens.shape
    ids = expert_ids.reshape(-1, TOP)
    tok = tokens.reshape(-1, width)
    if (n_lat, n_lon) == (4, 8) and w_gate.shape[1] == 2 * FF:
        out = layer_block(
            n_lat, n_lon, shifts, tok, router, ids, w_qkv, w_out, w_gate, w_up, w_down
        )
        return out.reshape(rows, cols, width)
    mixed, normed2 = front_block(n_lat, n_lon, shifts, tok, w_qkv, w_out)
    return general(mixed, normed2, router, ids, w_gate, w_up, w_down, devices, rows, cols)


def general(mixed, normed2, router, ids, w_gate, w_up, w_down, devices, rows, cols):
    width = mixed.shape[1]
    logits = jnp.dot(normed2, router, preferred_element_type=jnp.float32)
    experts = router.shape[1]
    expert_iota = jnp.arange(experts, dtype=jnp.int32)
    picks = ids[:, :, None] == expert_iota[None, None, :]
    chosen = jnp.sum(jnp.where(picks, logits[:, None, :], 0.0), axis=-1)
    sig = jax.nn.sigmoid(chosen)
    gates = sig / jnp.sum(sig, axis=1, keepdims=True)
    flat = ids.reshape(-1)
    order = jnp.arange(flat.shape[0], dtype=jnp.int32)
    earlier = (flat[:, None] == flat[None, :]) & (order[None, :] < order[:, None])
    rank = jnp.sum(earlier.astype(jnp.int32), axis=1)
    share = w_gate.shape[1]
    piece = min(FF, share)
    repl = FF // piece
    group = share // piece
    most = MOST
    cap = group * most
    token_of = jnp.arange(flat.shape[0], dtype=jnp.int32) // TOP
    slot = flat % group * most + rank
    slot_index = jnp.stack(
        [(flat // group * repl + copy) * cap + slot for copy in range(repl)], axis=0
    )
    routed = normed2[token_of]
    send = (
        jnp.zeros((devices * cap, width), jnp.bfloat16)
        .at[slot_index.reshape(-1)]
        .set(jnp.tile(routed, (repl, 1)))
    )
    send = send.reshape(devices, group, most, width)
    received = lax.all_to_all(send, ("lat", "lon"), split_axis=0, concat_axis=0, tiled=True)
    results = []
    for local in range(group):
        block = received[:, local].reshape(-1, width)
        gate = jnp.dot(
            block,
            w_gate[:, local * piece : (local + 1) * piece],
            preferred_element_type=jnp.float32,
        )
        upper = jnp.dot(
            block, w_up[:, local * piece : (local + 1) * piece], preferred_element_type=jnp.float32
        )
        hidden = (jax.nn.silu(gate) * upper).astype(jnp.bfloat16)
        part = jnp.dot(
            hidden, w_down[local * piece : (local + 1) * piece], preferred_element_type=jnp.float32
        ).astype(jnp.bfloat16)
        results.append(part.reshape(received.shape[0], received.shape[2], width))
    back = lax.all_to_all(
        jnp.stack(results, axis=1), ("lat", "lon"), split_axis=0, concat_axis=0, tiled=True
    )
    back_flat = back.reshape(devices * cap, width)
    combined = jnp.zeros((flat.shape[0], width), jnp.float32)
    for copy in range(repl):
        combined = combined + back_flat[slot_index[copy]].astype(jnp.float32)
    combined = combined.reshape(-1, TOP, width)
    moe = jnp.sum(gates[:, :, None] * combined, axis=1)
    layer_out = (mixed.astype(jnp.float32) + moe).astype(jnp.bfloat16)
    return layer_out.reshape(rows, cols, width)


def solution(mesh):
    placed = (
        P("lat", "lon", None),
        P(),
        P(),
        P(),
        P(),
        P("lat", "lon", None, None),
        P(None, ("lat", "lon")),
        P(None, ("lat", "lon")),
        P(("lat", "lon"), None),
    )
    return jax.shard_map(
        body, mesh=mesh, in_specs=placed, out_specs=P("lat", "lon", None), check_vma=False
    )
```
